256 devices in a mesh: gz: 32 (over y, z), gy: 8 (over x, core).
Axes of the slice: x: 4, y: 4, z: 8, core: 2. Of those that a mesh axis runs over, the one named last changes fastest.
Arguments:
- concentration: float32 [512, 64, 128], P('gz', 'gy'), may hold values from 0 to 2
- phases: int32 [512, 64, 128], P('gz', 'gy'), may hold values from 0 to 2, as said below
- grains: int32 [512, 64, 128], P('gz', 'gy'), may hold values from 0 to 63, as said below
- grain_class: int32 [64], replicated, may hold values from 0 to 3
- diffusivity: float32 [3, 4], replicated, may hold values from 1 to 2000
Outputs:
- solution: float32 [512, 64, 128], P('gz', 'gy')
The draws below stay inside these ranges and needn't reach their ends.
Inputs may be any that keep to these rules, and one draw needn't show every extreme that they name: `phases`: constant on aligned blocks of 8 x 8 x 8 cells. `grains`: constant on aligned blocks of 4 x 4 x 4 cells.
All inputs are finite; a program needn't handle non-finite values.
Results may differ from the reference program's by a relative error of at most 0.0003.
Values sent between devices are 32-bit elements; how exact they have to be, the bound alone decides.
No kernel may reach another device: no remote copies, remote signals or barrier semaphores. Data moves between devices by JAX's collectives and lax.ppermute only.
A program may use at most 64 MiB of HBM per device.

```python
import math
import jax
import jax.numpy as jnp
from jax import lax

NX = 128
NPH = 3
NCLS = 4
NGRAIN = 64
CYCLES = 2
COARSE = 6
NZ = 512
NY = 64


def draw_concentration(key, part):
    own_key = jax.random.fold_in(key, 11)
    rough = jax.random.uniform(own_key, (NZ, NY, NX), jnp.float32, -1.0, 1.0)
    return 1.0 + 0.8 * rough


def draw_phases(key, part):
    own_key = jax.random.fold_in(key, 23)
    coarse = jax.random.randint(own_key, (NZ // 8, NY // 8, NX // 8), 0, NPH)
    return jnp.repeat(jnp.repeat(jnp.repeat(coarse, 8, 0), 8, 1), 8, 2).astype(jnp.int32)


def draw_grains(key, part):
    own_key = jax.random.fold_in(key, 37)
    coarse = jax.random.randint(own_key, (NZ // 4, NY // 4, NX // 4), 0, NGRAIN)
    return jnp.repeat(jnp.repeat(jnp.repeat(coarse, 4, 0), 4, 1), 4, 2).astype(jnp.int32)


def with_ends(drawn, key, smallest, largest):
    dims = drawn.shape
    index_at = [jax.random.randint(jax.random.fold_in(key, axis), (), 0, dims[axis]) for axis in range(len(dims))]
    drawn = drawn.at[tuple(index_at)].set(smallest)
    longest = dims.index(max(dims))
    index_at[longest] = (index_at[longest] + 1) % dims[longest]
    return drawn.at[tuple(index_at)].set(largest)


def setup_inputs(seed: int = 0) -> dict:
    key_list = jax.random.split(jax.random.key(seed), 6)
    return {
        "concentration": draw_concentration(jax.random.fold_in(key_list[5], 71), 0),
        "phases": draw_phases(jax.random.fold_in(key_list[5], 71), 0),
        "grains": draw_grains(jax.random.fold_in(key_list[5], 71), 0),
        "grain_class": with_ends(jax.random.randint(key_list[3], (NGRAIN,), 0, NCLS), jax.random.fold_in(key_list[3], 1), 0, NCLS - 1).astype(jnp.int32),
        "diffusivity": jnp.clip(jnp.exp(jax.random.uniform(key_list[4], (NPH, NCLS), jnp.float32, math.log(1.0), math.log(2000.0))), 1.0, 2000.0),
    }


RELAX_WEIGHT = 0.8


def harmonic(near_k, far_k):
    return 2.0 * near_k * far_k / (near_k + far_k)


def face_set(padded, margin, y_start, y_total):
    centre = padded[1:-1, 1:-1]
    row_index = lax.broadcasted_iota(jnp.int32, centre.shape, 1) + y_start - margin
    col_index = lax.broadcasted_iota(jnp.int32, centre.shape, 2)
    z_low = harmonic(centre, padded[:-2, 1:-1])
    z_high = harmonic(centre, padded[2:, 1:-1])
    y_low = jnp.where(row_index == 0, 0.0, harmonic(centre, padded[1:-1, :-2]))
    y_high = jnp.where(row_index == y_total - 1, 0.0, harmonic(centre, padded[1:-1, 2:]))
    x_low = jnp.where(col_index == 0, 0.0, harmonic(centre, jnp.roll(centre, 1, 2)))
    x_high = jnp.where(col_index == centre.shape[2] - 1, 0.0, harmonic(centre, jnp.roll(centre, -1, 2)))
    diagonal = 1.0 + z_low + z_high + y_low + y_high + x_low + x_high
    return (z_low, z_high, y_low, y_high, x_low, x_high, diagonal)


def apply_operator(padded, faces):
    z_low, z_high, y_low, y_high, x_low, x_high, diagonal = faces
    centre = padded[1:-1, 1:-1]
    coupled = (z_low * padded[:-2, 1:-1] + z_high * padded[2:, 1:-1]
               + y_low * padded[1:-1, :-2] + y_high * padded[1:-1, 2:]
               + x_low * jnp.roll(centre, 1, 2) + x_high * jnp.roll(centre, -1, 2))
    return centre, diagonal * centre - coupled


def relax_sweep(padded, source, faces):
    centre, image = apply_operator(padded, faces)
    return centre + RELAX_WEIGHT * (source - image) / faces[6]


def defect(padded, source, faces):
    return source - apply_operator(padded, faces)[1]


def restrict(values):
    extent = values.shape
    return values.reshape(extent[0] // 2, 2, extent[1] // 2, 2, extent[2] // 2, 2).mean(axis=(1, 3, 5))


def prolong(coarse):
    return jnp.repeat(jnp.repeat(jnp.repeat(coarse, 2, 0), 2, 1), 2, 2)


def pad_periodic(values):
    wrapped = jnp.concatenate([values[-1:], values, values[:1]], axis=0)
    return jnp.pad(wrapped, ((0, 0), (1, 1), (0, 0)), mode="edge")


def vcycle(level_index, field, source, faces_list):
    faces = faces_list[level_index]
    if level_index == len(faces_list) - 1:
        for _ in range(COARSE):
            field = relax_sweep(pad_periodic(field), source, faces)
        return field
    for _ in range(2):
        field = relax_sweep(pad_periodic(field), source, faces)
    residual = defect(pad_periodic(field), source, faces)
    coarse_source = restrict(residual)
    correction = vcycle(level_index + 1, jnp.zeros_like(coarse_source), coarse_source, faces_list)
    field = field + prolong(correction)
    for _ in range(2):
        field = relax_sweep(pad_periodic(field), source, faces)
    return field


def reference(concentration, phases, grains, grain_class, diffusivity):
    kappa = diffusivity[phases, grain_class[grains]]
    faces_list = []
    for level_index in range(5):
        if level_index > 0:
            kappa = 0.5 * restrict(kappa)
        faces_list.append(face_set(pad_periodic(kappa), 0, 0, kappa.shape[1]))
    field = jnp.zeros_like(concentration)
    for _ in range(CYCLES):
        field = vcycle(0, field, concentration, faces_list)
    return field
```

```python
import jax
import jax.numpy as jnp
from jax import lax
from jax.experimental import pallas as pl
from jax.experimental.pallas import tpu as pltpu
from jax.sharding import PartitionSpec as P

HALO = 12
WZ = 40
BLOCKS = 10
WY = 24
VMEM_BYTES = 48 * 1024 * 1024


def harmonic(near_k, far_k):
    return 2.0 * near_k * far_k / (near_k + far_k)


def dot(left, right):
    return jnp.dot(left, right, precision=lax.Precision.HIGHEST, preferred_element_type=jnp.float32)


def iota(rows, dim, lanes=128):
    return lax.broadcasted_iota(jnp.int32, (rows, lanes), dim)


def matrix(condition, value):
    return jnp.where(condition, jnp.float32(value), jnp.float32(0.0))


def lane_map(make):
    return make(iota(128, 0), iota(128, 1))


class Level:
    def __init__(self, planes, ny, nx, zl, pad, cyclic, y_start, y_total, chunk):
        self.planes, self.ny, self.nx, self.zl, self.pad = planes, ny, nx, zl, pad
        self.cyclic, self.y_start, self.y_total = cyclic, y_start, y_total
        self.rows = planes * ny
        self.chunk = min(chunk, self.rows)

    def chunks(self, start=0, count=None):
        count = self.rows if count is None else count
        at = start
        while at < start + count:
            size = min(self.chunk, start + count - at)
            yield at, size
            at += size

    def neighbours(self, ref, at, size):
        base = self.pad + at
        here = ref[base : base + size]
        below = ref[base - self.ny : base - self.ny + size]
        above = ref[base + self.ny : base + self.ny + size]
        if self.zl > 1:
            cell = iota(size, 1) % (self.zl * self.nx)
            below = pltpu.roll(jnp.where(cell >= (self.zl - 1) * self.nx, below, here), self.nx, 1)
            above = pltpu.roll(jnp.where(cell < self.nx, above, here), 128 - self.nx, 1)
        return (
            here,
            (
                below,
                above,
                ref[base - 1 : base - 1 + size],
                ref[base + 1 : base + 1 + size],
                pltpu.roll(here, 1, 1),
                pltpu.roll(here, 127, 1),
            ),
        )

    def wrap(self, ref):
        if self.cyclic:
            ref[0 : self.pad] = ref[self.rows : self.rows + self.pad]
            ref[self.pad + self.rows : 2 * self.pad + self.rows] = ref[self.pad : 2 * self.pad]

    def build(self, kappa, faces):
        for at, size in self.chunks():
            here, around = self.neighbours(kappa, at, size)
            y = iota(size, 0) % self.ny + self.y_start
            x = iota(size, 1) % self.nx
            keep = (None, None, y != 0, y != self.y_total - 1, x != 0, x != self.nx - 1)
            total = jnp.full((size, 128), 1.0, jnp.float32)
            for number in range(6):
                face = harmonic(here, around[number])
                if keep[number] is not None:
                    face = jnp.where(keep[number], face, 0.0)
                faces[number, at : at + size] = face
                total = total + face
            faces[6, at : at + size] = 0.8 / total
            faces[7, at : at + size] = total

    def coupled(self, field, source, faces, at, size):
        here, around = self.neighbours(field, at, size)
        total = source[at : at + size]
        for number in range(6):
            total = total + faces[number, at : at + size] * around[number]
        return here, total

    def start(self, field, source, faces):
        for at, size in self.chunks():
            field[self.pad + at : self.pad + at + size] = faces[6, at : at + size] * source[at : at + size]
        self.wrap(field)

    def relax(self, field, target, source, faces, start=0, count=None):
        for at, size in self.chunks(start, count):
            here, total = self.coupled(field, source, faces, at, size)
            target[self.pad + at : self.pad + at + size] = 0.2 * here + faces[6, at : at + size] * total
        self.wrap(target)

    def defect(self, field, source, faces, out, start=0, count=None):
        for at, size in self.chunks(start, count):
            here, total = self.coupled(field, source, faces, at, size)
            out[at - start : at - start + size] = total - faces[7, at : at + size] * here

    def pairs(self, ref):
        half = self.rows // 2
        return ref[pl.ds(0, half, stride=2), :] + ref[pl.ds(1, half, stride=2), :]


def kappa_body(class_ref, diff_ref, phases_ref, grains_ref, conc_ref, kappa_ref, up_ref, down_ref):
    num_phases, num_classes = diff_ref.shape
    for block in range(4):
        grain = grains_ref[4 * block]
        phase = phases_ref[4 * block]
        cls = jnp.zeros(grain.shape, jnp.int32)
        for number in range(class_ref.shape[0]):
            cls = jnp.where(grain == number, class_ref[number], cls)
        value = jnp.ones(grain.shape, jnp.float32)
        for p in range(num_phases):
            for c in range(num_classes):
                value = jnp.where((phase == p) & (cls == c), diff_ref[p, c], value)
        kappa_ref[block] = value
        if block > 0:
            up_ref[HALO + block - 1] = value
        if block < 3:
            down_ref[HALO + block] = value
    for z in range(HALO):
        up_ref[z] = conc_ref[16 - HALO + z]
        down_ref[z] = conc_ref[z]


def window(refs, plane):
    return jnp.concatenate([ref[plane] for ref in refs], axis=0)


def build_fine(sources, y_device, kappa, coefs, z_faces):
    kappa[0:8] = jnp.ones((8, 128), jnp.float32)
    kappa[8 + BLOCKS * WY : 16 + BLOCKS * WY] = jnp.ones((8, 128), jnp.float32)
    for block in range(BLOCKS):
        kappa[8 + block * WY : 8 + (block + 1) * WY] = window(sources, WZ + block)
    y = iota(WY, 0) + y_device * 8 - 8
    x = iota(WY, 1)
    for block in range(BLOCKS + 1):
        low, high = max(block - 1, 0), min(block, BLOCKS - 1)
        z_faces[block] = harmonic(
            kappa[8 + low * WY : 8 + (low + 1) * WY], kappa[8 + high * WY : 8 + (high + 1) * WY]
        )
    for block in range(BLOCKS):
        at = 8 + block * WY
        k = kappa[at : at + WY]
        y_low = jnp.where(y == 0, 0.0, harmonic(k, kappa[at - 1 : at - 1 + WY]))
        y_high = jnp.where(y == 63, 0.0, harmonic(k, kappa[at + 1 : at + 1 + WY]))
        x_low = jnp.where(x == 0, 0.0, harmonic(k, pltpu.roll(k, 1, 1)))
        x_high = jnp.where(x == 127, 0.0, harmonic(k, pltpu.roll(k, 127, 1)))
        sides = 1.0 + y_low + y_high + x_low + x_high
        diagonals = (sides + z_faces[block] + k, sides + k + k, sides + k + z_faces[block + 1])
        for number, value in enumerate((k, y_low, y_high, x_low, x_high)):
            coefs[block, number] = value
        for number, value in enumerate(diagonals):
            coefs[block, 5 + number] = 0.8 / value
            coefs[block, 8 + number] = value


def fine_plane(field, sources, coefs, z_faces, z, low=0, size=WY):
    block, p = divmod(z, 4)
    rows = slice(low, low + size)
    at = WY + z * WY + low
    here = field[at : at + size]
    k = coefs[block, 0, rows]
    below = z_faces[block, rows] if p == 0 else k
    above = z_faces[block + 1, rows] if p == 3 else k
    source = window(sources, z) if size == WY else sources[1][z]
    total = (
        source
        + below * field[at - WY : at - WY + size]
        + above * field[at + WY : at + WY + size]
        + coefs[block, 1, rows] * field[at - 1 : at - 1 + size]
        + coefs[block, 2, rows] * field[at + 1 : at + 1 + size]
        + coefs[block, 3, rows] * pltpu.roll(here, 1, 1)
        + coefs[block, 4, rows] * pltpu.roll(here, 127, 1)
    )
    kind = (0, 1, 1, 2)[p]
    return here, total, coefs[block, 5 + kind, rows], coefs[block, 8 + kind, rows]


def level_one(y_device):
    return Level(20, 16, 64, 1, 16, False, y_device * 4 - 4, 32, 160)


def build_one(level, kappa, spread, packed, kappa_one, faces):
    for block in range(BLOCKS):
        spread[block * 32 : block * 32 + WY] = kappa[8 + block * WY : 8 + (block + 1) * WY]
        spread[block * 32 + WY : block * 32 + 32] = jnp.ones((32 - WY, 128), jnp.float32)
    pick = lane_map(lambda r, c: matrix(r == 2 * (c % 64), 0.5))
    packed[...] = dot(spread[pl.ds(0, BLOCKS * 16, stride=2), :], pick)
    ones = jnp.ones((16, 128), jnp.float32)
    kappa_one[0:16] = ones
    kappa_one[336:352] = ones
    for block in range(BLOCKS):
        value = packed[block * 16 : block * 16 + 16]
        kappa_one[16 + block * 32 : 32 + block * 32] = value
        kappa_one[32 + block * 32 : 48 + block * 32] = value
    level.build(kappa_one, faces)


def to_chunk(rows):
    group = iota(8, 1) // 32
    out = rows[0:8]
    for z in range(1, 4):
        out = jnp.where(group == z, rows[8 * z : 8 * z + 8], out)
    return out


def down_body(first, *refs):
    index, low, own, high = refs[:4]
    sources = (low, own, high)
    refs = refs[4:]
    if not first:
        fields, refs = refs[:3], refs[3:]
    chunk, edge, kept, source_one, kept_one = refs[:5]
    kappa, coefs, z_faces, va, vb, rs, spread, packed, kappa_one, faces, oa, tmp = refs[5:]
    y_device = index[1]
    build_fine(sources, y_device, kappa, coefs, z_faces)
    level = level_one(y_device)
    build_one(level, kappa, spread, packed, kappa_one, faces)
    zero = jnp.zeros((WY, 128), jnp.float32)
    for ref in (va, vb):
        ref[0:WY] = zero
        ref[(WZ + 1) * WY : (WZ + 2) * WY] = zero
    if first:
        for z in range(WZ):
            kind = (0, 1, 1, 2)[z % 4]
            va[(z + 1) * WY : (z + 2) * WY] = coefs[z // 4, 5 + kind] * window(sources, z)
    else:
        for z in range(WZ):
            vb[(z + 1) * WY : (z + 2) * WY] = window(fields, z)
        for z in range(WZ):
            here, total, weight, _ = fine_plane(vb, sources, coefs, z_faces, z)
            va[(z + 1) * WY : (z + 2) * WY] = 0.2 * here + weight * total
    for z in range(2, WZ - 2):
        here, total, weight, _ = fine_plane(va, sources, coefs, z_faces, z)
        value = 0.2 * here + weight * total
        vb[(z + 1) * WY : (z + 2) * WY] = value
        if 10 <= z < 30:
            kept[(z - 10) * WY : (z - 9) * WY] = value
    for plane in range(20):
        if 2 <= plane < 18:
            total_defect = 0.0
            for z in (2 * plane, 2 * plane + 1):
                here, total, _, diagonal = fine_plane(vb, sources, coefs, z_faces, z)
                total_defect = total_defect + (total - diagonal * here)
            rs[plane * 32 : plane * 32 + WY] = total_defect
            rs[plane * 32 + WY : plane * 32 + 32] = jnp.zeros((32 - WY, 128), jnp.float32)
        else:
            rs[plane * 32 : plane * 32 + 32] = jnp.zeros((32, 128), jnp.float32)
    mean_x = lane_map(lambda r, c: matrix(r // 2 == c % 64, 0.125))
    source_one[...] = dot(rs[pl.ds(0, 320, stride=2), :] + rs[pl.ds(1, 320, stride=2), :], mean_x)
    for ref in (oa, kept_one):
        ref[0:16] = jnp.zeros((16, 128), jnp.float32)
        ref[336:352] = jnp.zeros((16, 128), jnp.float32)
    level.start(oa, source_one, faces)
    level.relax(oa, kept_one, source_one, faces)
    level.defect(kept_one, source_one, faces, tmp, 6 * 16, 8 * 16)
    for z in range(4):
        tmp[z * 16 : z * 16 + 16] = tmp[z * 32 : z * 32 + 16] + tmp[z * 32 + 16 : z * 32 + 32]
    halves = tmp[pl.ds(0, 32, stride=2), :] + tmp[pl.ds(1, 32, stride=2), :]
    mean_two = lane_map(lambda r, c: matrix((r < 64) & (r // 2 == c % 32), 0.125))
    chunk[0:2] = to_chunk(dot(halves, mean_two))[2:4]
    if first:
        pick_two = lane_map(lambda r, c: matrix((r < 64) & (r == 2 * (c % 32)), 0.5))
        chunk[2:4] = to_chunk(dot(packed[pl.ds(48, 32, stride=2), :], pick_two))[2:4]
    for plane in range(20):
        edge[plane * 4 : plane * 4 + 4] = kept_one[16 + plane * 16 + 4 : 16 + plane * 16 + 8]


def up_body(first, z_devices, *refs):
    index, low, own, high, gathered = refs[:5]
    refs = refs[5:]
    if first:
        labelled = gathered
    else:
        labelled, refs = refs[0], refs[1:]
    edge_low, edge_high, kept, source_one, kept_one, out = refs[:6]
    (kappa, coefs, z_faces, va, vb, spread, packed, kappa_one, faces, oa, ob) = refs[6:17]
    (k2, g2, a2, b2, f2, r2, k3, g3, a3, b3, f3, r3, k4, g4, a4, b4, f4, r4) = refs[17:]
    sources = (low, own, high)
    z_device, y_device = index[0], index[1]
    two = Level(z_devices, 16, 32, 4, 16, True, 0, 16, 128)
    three = Level(z_devices, 8, 16, 2, 8, True, 0, 8, 128)
    four = Level(z_devices, 4, 8, 1, 8, True, 0, 4, 128)

    chunks = z_devices * 8
    for part in range(2):
        k2[pl.ds(two.pad + part, chunks, stride=2), :] = labelled[pl.ds(2 + part, chunks, stride=4), :]
        if first:
            g2[pl.ds(part, chunks, stride=2), :] = gathered[pl.ds(part, chunks, stride=4), :]
    if not first:
        g2 = gathered
    two.wrap(k2)
    two.build(k2, f2)
    mean_three = lane_map(lambda r, c: matrix(c % 32 == (r // 64) * 16 + (r % 32) // 2, 0.125))
    mean_four = lane_map(lambda r, c: matrix((r < 32) & (c % 8 == (r % 16) // 2), 0.125))
    r2[...] = k2[two.pad : two.pad + two.rows]
    k3[three.pad : three.pad + three.rows] = 0.5 * dot(two.pairs(r2), mean_three)
    three.wrap(k3)
    three.build(k3, f3)
    r3[...] = k3[three.pad : three.pad + three.rows]
    k4[four.pad : four.pad + four.rows] = 0.5 * dot(three.pairs(r3), mean_four)
    four.wrap(k4)
    four.build(k4, f4)

    two.start(a2, g2, f2)
    two.relax(a2, b2, g2, f2)
    two.defect(b2, g2, f2, r2)
    g3[...] = dot(two.pairs(r2), mean_three)
    three.start(a3, g3, f3)
    three.relax(a3, b3, g3, f3)
    three.defect(b3, g3, f3, r3)
    g4[...] = dot(three.pairs(r3), mean_four)
    four.start(a4, g4, f4)
    for _ in range(2):
        four.relax(a4, b4, g4, f4)
        four.relax(b4, a4, g4, f4)
    four.relax(a4, b4, g4, f4)

    def correct(level, field, coarse, tmp, spread_lanes):
        value = dot(coarse, spread_lanes)
        half = level.rows // 2
        tmp[pl.ds(0, half, stride=2), :] = value
        tmp[pl.ds(1, half, stride=2), :] = value
        inner = slice(level.pad, level.pad + level.rows)
        field[inner] = field[inner] + tmp[...]
        level.wrap(field)

    from_four = lane_map(lambda r, c: matrix((r < 8) & (r == (c % 16) // 2), 1.0))
    from_three = lane_map(lambda r, c: matrix((r < 32) & (r == (c // 64) * 16 + (c % 32) // 2), 1.0))
    correct(three, b3, b4[four.pad : four.pad + four.rows], r3, from_four)
    three.relax(b3, a3, g3, f3)
    three.relax(a3, b3, g3, f3)
    correct(two, b2, b3[three.pad : three.pad + three.rows], r2, from_three)
    two.relax(b2, a2, g2, f2)
    two.relax(a2, b2, g2, f2)

    build_fine(sources, y_device, kappa, coefs, z_faces)
    level = level_one(y_device)
    build_one(level, kappa, spread, packed, kappa_one, faces)

    near = b2[pl.ds(pl.multiple_of(z_device * 16, 16), 48), :]
    rows = matrix(iota(16, 1, 16) == y_device * 2 - 2 + iota(16, 0, 16) // 2, 1.0)
    spread_y = jnp.concatenate([dot(rows, near[16 * part : 16 * part + 16]) for part in range(3)], axis=0)
    by_z = [
        dot(spread_y, lane_map(lambda r, c, z=z: matrix(r == z * 32 + (c % 64) // 2, 1.0))) for z in range(4)
    ]
    for plane in range(20):
        part, z = divmod(plane // 2 + 1, 4)
        at = 16 + plane * 16
        field = jnp.concatenate(
            [edge_low[plane * 4 : plane * 4 + 4], kept_one[at + 4 : at + 8],
             edge_high[plane * 4 : plane * 4 + 4], jnp.zeros((4, 128), jnp.float32)], axis=0
        )
        oa[at : at + 16] = field + by_z[z][16 * part : 16 * part + 16]
    level.relax(oa, ob, source_one, faces, 4 * 16, 12 * 16)
    level.relax(ob, oa, source_one, faces, 5 * 16, 10 * 16)
    from_one = lane_map(lambda r, c: matrix((r < 64) & (r == c // 2), 1.0))
    value = dot(oa[16 + 80 : 16 + 240], from_one)
    spread[pl.ds(0, 160, stride=2), :] = value
    spread[pl.ds(1, 160, stride=2), :] = value
    for z in range(10, 30):
        at = ((z - 10) // 2) * 32
        va[(z + 1) * WY : (z + 2) * WY] = kept[(z - 10) * WY : (z - 9) * WY] + spread[at : at + WY]
    for z in range(11, 29):
        here, total, weight, _ = fine_plane(va, sources, coefs, z_faces, z)
        vb[(z + 1) * WY : (z + 2) * WY] = 0.2 * here + weight * total
    for z in range(12, 28):
        here, total, weight, _ = fine_plane(vb, sources, coefs, z_faces, z, 8, 8)
        out[z - 12] = 0.2 * here + weight * total


def floats(*shape):
    return jax.ShapeDtypeStruct(shape, jnp.float32)


def call(body, outs, scratch, args, smem):
    vmem = pl.BlockSpec(memory_space=pltpu.VMEM)
    return pl.pallas_call(
        body,
        out_shape=outs,
        in_specs=[pl.BlockSpec(memory_space=pltpu.SMEM)] * smem + [vmem] * (len(args) - smem),
        out_specs=[vmem] * len(outs),
        scratch_shapes=[pltpu.VMEM(shape, jnp.float32) for shape in scratch],
        compiler_params=pltpu.CompilerParams(vmem_limit_bytes=VMEM_BYTES),
    )(*args)


FINE = [(16 + BLOCKS * WY, 128), (BLOCKS, 11, WY, 128), (BLOCKS + 1, WY, 128), ((WZ + 2) * WY, 128), ((WZ + 2) * WY, 128)]
ONE = [(320, 128), (160, 128), (352, 128), (8, 320, 128), (352, 128)]


def down(index, sources, fields):
    first = fields is None
    outs = [
        floats(4 if first else 2, 128), floats(80, 128), floats(20 * WY, 128), floats(320, 128), floats(352, 128)
    ]
    scratch = FINE + [(640, 128)] + ONE + [(128, 128)]
    args = [index, *sources] + ([] if first else list(fields))
    return call(lambda *refs: down_body(first, *refs), outs, scratch, args, 1)


def up(index, sources, gathered, labelled, edges, kept):
    first = labelled is None
    z_devices = lax.axis_size("gz")
    scratch = FINE + ONE + [(352, 128)]
    for ny, pad in ((16, 16), (8, 8), (4, 8)):
        rows = z_devices * ny
        padded = (rows + 2 * pad, 128)
        scratch += [padded, (rows, 128), padded, padded, (8, rows, 128), (rows, 128)]
    args = [index, *sources, gathered] + ([] if first else [labelled]) + [*edges, *kept]
    return call(lambda *refs: up_body(first, z_devices, *refs), [floats(16, 8, 128)], scratch, args, 1)[0]


def shifted(array, axis, step):
    count = lax.axis_size(axis)
    return lax.ppermute(array, axis, [(i, (i + step) % count) for i in range(count)])


def both_sides(array, axis):
    return shifted(array, axis, 1), shifted(array, axis, -1)


def to_all(chunk):
    devices = lax.axis_size("gz") * lax.axis_size("gy")
    copies = jnp.broadcast_to(chunk[None], (devices,) + chunk.shape)
    out = lax.all_to_all(copies, ("gz", "gy"), 0, 0)
    return out.reshape(devices * chunk.shape[0], 128)


def per_device(concentration, phases, grains, grain_class, diffusivity):
    index = jnp.stack([lax.axis_index("gz"), lax.axis_index("gy")]).astype(jnp.int32)
    kappa, up_part, down_part = call(
        kappa_body,
        [floats(4, 8, 128), floats(HALO + 3, 8, 128), floats(HALO + 3, 8, 128)],
        [],
        [grain_class, diffusivity, phases, grains, concentration],
        2,
    )
    before = shifted(up_part, "gz", 1)
    after = shifted(down_part, "gz", -1)
    own = jnp.concatenate(
        [before[:HALO], concentration, after[:HALO], before[HALO:], kappa, after[HALO:]], axis=0
    )
    low, high = both_sides(own, "gy")
    sources = (low, own, high)

    chunk, edge, *kept = down(index, sources, None)
    edges = both_sides(edge, "gy")
    labelled = to_all(chunk)
    field = up(index, sources, labelled, None, edges, kept)

    before = shifted(field[16 - HALO :], "gz", 1)
    after = shifted(field[:HALO], "gz", -1)
    field = jnp.concatenate([before, field, after], axis=0)
    low, high = both_sides(field, "gy")
    chunk, edge, *kept = down(index, sources, (low, field, high))
    edges = both_sides(edge, "gy")
    gathered = to_all(chunk)
    return up(index, sources, gathered, labelled, edges, kept)


def solution(mesh):
    placed = (P("gz", "gy", None), P("gz", "gy", None), P("gz", "gy", None), P(), P())
    return jax.shard_map(
        per_device, mesh=mesh, in_specs=placed, out_specs=P("gz", "gy", None), check_vma=False
    )
```

```python
import jax
import jax.numpy as jnp
from jax import lax
from jax.experimental import pallas as pl
from jax.experimental.pallas import tpu as pltpu
from jax.sharding import PartitionSpec as P

HALO = 12
WZ = 40
BLOCKS = 10
WY = 24
VMEM_BYTES = 48 * 1024 * 1024


def harmonic(near_k, far_k):
    return 2.0 * near_k * far_k / (near_k + far_k)


def dot(left, right):
    return jnp.dot(left, right, precision=lax.Precision.HIGHEST, preferred_element_type=jnp.float32)


def iota(rows, dim, lanes=128):
    return lax.broadcasted_iota(jnp.int32, (rows, lanes), dim)


def matrix(condition, value):
    return jnp.where(condition, jnp.float32(value), jnp.float32(0.0))


def lane_map(make):
    return make(iota(128, 0), iota(128, 1))


class Level:
    def __init__(self, planes, ny, nx, zl, pad, cyclic, y_start, y_total, chunk):
        self.planes, self.ny, self.nx, self.zl, self.pad = planes, ny, nx, zl, pad
        self.cyclic, self.y_start, self.y_total = cyclic, y_start, y_total
        self.rows = planes * ny
        self.chunk = min(chunk, self.rows)

    def chunks(self, start=0, count=None):
        count = self.rows if count is None else count
        at = start
        while at < start + count:
            size = min(self.chunk, start + count - at)
            yield at, size
            at += size

    def neighbours(self, ref, at, size):
        base = self.pad + at
        here = ref[base : base + size]
        below = ref[base - self.ny : base - self.ny + size]
        above = ref[base + self.ny : base + self.ny + size]
        if self.zl > 1:
            cell = iota(size, 1) % (self.zl * self.nx)
            below = pltpu.roll(jnp.where(cell >= (self.zl - 1) * self.nx, below, here), self.nx, 1)
            above = pltpu.roll(jnp.where(cell < self.nx, above, here), 128 - self.nx, 1)
        return (
            here,
            (
                below,
                above,
                ref[base - 1 : base - 1 + size],
                ref[base + 1 : base + 1 + size],
                pltpu.roll(here, 1, 1),
            ),
        )

    def wrap(self, ref):
        if self.cyclic:
            ref[0 : self.pad] = ref[self.rows : self.rows + self.pad]
            ref[self.pad + self.rows : 2 * self.pad + self.rows] = ref[self.pad : 2 * self.pad]

    def shape(self):
        return (self.rows + 2 * self.pad, 128)

    def build(self, kappa, faces):
        for number in (0, 2):
            faces[number, 0 : self.pad] = jnp.zeros((self.pad, 128), jnp.float32)
            faces[number, self.pad + self.rows :] = jnp.zeros((self.pad, 128), jnp.float32)
        for at, size in self.chunks():
            here, around = self.neighbours(kappa, at, size)
            y = iota(size, 0) % self.ny + self.y_start
            x = iota(size, 1) % self.nx
            rows = slice(self.pad + at, self.pad + at + size)
            faces[0, rows] = harmonic(here, around[0])
            faces[2, rows] = jnp.where((y != 0) & (y != self.y_total), harmonic(here, around[2]), 0.0)
            faces[3, rows] = jnp.where(x != 0, harmonic(here, around[4]), 0.0)
        self.wrap(faces.at[0])
        for at, size in self.chunks():
            rows = slice(self.pad + at, self.pad + at + size)
            z_low, around = self.neighbours(faces.at[0], at, size)
            z_high = around[1]
            y_high = faces[2, self.pad + at + 1 : self.pad + at + 1 + size]
            x_low = faces[3, rows]
            total = 1.0 + z_low + z_high + faces[2, rows] + y_high + x_low + pltpu.roll(x_low, 127, 1)
            faces[1, rows] = z_high
            faces[4, rows] = 0.8 / total
            faces[5, rows] = total

    def coupled(self, field, source, faces, at, size):
        here, around = self.neighbours(field, at, size)
        rows = slice(self.pad + at, self.pad + at + size)
        next_rows = slice(self.pad + at + 1, self.pad + at + 1 + size)
        x_low = faces[3, rows]
        total = (
            source[at : at + size]
            + faces[0, rows] * around[0]
            + faces[1, rows] * around[1]
            + faces[2, rows] * around[2]
            + faces[2, next_rows] * around[3]
            + x_low * around[4]
            + pltpu.roll(x_low * here, 127, 1)
        )
        return here, total

    def start(self, field, source, faces):
        for at, size in self.chunks():
            rows = slice(self.pad + at, self.pad + at + size)
            field[rows] = faces[4, rows] * source[at : at + size]
        self.wrap(field)

    def relax(self, field, target, source, faces, start=0, count=None):
        for at, size in self.chunks(start, count):
            here, total = self.coupled(field, source, faces, at, size)
            rows = slice(self.pad + at, self.pad + at + size)
            target[rows] = 0.2 * here + faces[4, rows] * total
        self.wrap(target)

    def defect(self, field, source, faces, out, start=0, count=None):
        for at, size in self.chunks(start, count):
            here, total = self.coupled(field, source, faces, at, size)
            diagonal = faces[5, self.pad + at : self.pad + at + size]
            out[at - start : at - start + size] = total - diagonal * here

    def pairs(self, ref):
        half = self.rows // 2
        return ref[pl.ds(0, half, stride=2), :] + ref[pl.ds(1, half, stride=2), :]


def kappa_body(class_hbm, diff_hbm, phases_hbm, grains_hbm, conc_hbm, kappa_ref, up_ref, down_ref, classes, diff, phases, grains, sems):
    num_phases, num_classes = diff.shape
    pairs = [(class_hbm, classes), (diff_hbm, diff)]
    for block in range(4):
        pairs += [(phases_hbm.at[4 * block], phases.at[block]), (grains_hbm.at[4 * block], grains.at[block])]
    pairs += [
        (conc_hbm.at[16 - HALO : 16], up_ref.at[0:HALO]),
        (conc_hbm.at[0:HALO], down_ref.at[0:HALO]),
    ]
    copies = [pltpu.make_async_copy(source, target, sems.at[i]) for i, (source, target) in enumerate(pairs)]
    for copy in copies:
        copy.start()
    for copy in copies[:-2]:
        copy.wait()
    grain = grains[...]
    phase = phases[...]
    cls = jnp.zeros(grain.shape, jnp.int32)
    for number in range(classes.shape[0]):
        cls = jnp.where(grain == number, classes[number], cls)
    value = jnp.ones(grain.shape, jnp.float32)
    for p in range(num_phases):
        for c in range(num_classes):
            value = jnp.where((phase == p) & (cls == c), diff[p, c], value)
    kappa_ref[...] = value
    up_ref[HALO:] = value[1:]
    down_ref[HALO:] = value[:3]
    for copy in copies[-2:]:
        copy.wait()


def window(refs, plane):
    return jnp.concatenate([ref[plane] for ref in refs], axis=0)


def build_fine(sources, y_device, kappa, coefs, z_faces):
    kappa[0:8] = jnp.ones((8, 128), jnp.float32)
    kappa[8 + BLOCKS * WY : 16 + BLOCKS * WY] = jnp.ones((8, 128), jnp.float32)
    for block in range(BLOCKS):
        kappa[8 + block * WY : 8 + (block + 1) * WY] = window(sources, WZ + block)
    y = iota(WY, 0) + y_device * 8 - 8
    x = iota(WY, 1)
    for block in range(BLOCKS + 1):
        low, high = max(block - 1, 0), min(block, BLOCKS - 1)
        z_faces[block] = harmonic(
            kappa[8 + low * WY : 8 + (low + 1) * WY], kappa[8 + high * WY : 8 + (high + 1) * WY]
        )
    for block in range(BLOCKS):
        at = 8 + block * WY
        k = kappa[at : at + WY]
        y_low = jnp.where(y == 0, 0.0, harmonic(k, kappa[at - 1 : at - 1 + WY]))
        y_high = jnp.where(y == 63, 0.0, harmonic(k, kappa[at + 1 : at + 1 + WY]))
        x_low = jnp.where(x == 0, 0.0, harmonic(k, pltpu.roll(k, 1, 1)))
        x_high = jnp.where(x == 127, 0.0, harmonic(k, pltpu.roll(k, 127, 1)))
        sides = 1.0 + y_low + y_high + x_low + x_high
        diagonals = (sides + z_faces[block] + k, sides + k + k, sides + k + z_faces[block + 1])
        for number, value in enumerate((k, y_low, y_high, x_low, x_high)):
            coefs[block, number] = value
        for number, value in enumerate(diagonals):
            coefs[block, 5 + number] = 0.8 / value
            coefs[block, 8 + number] = value


def fine_plane(field, sources, coefs, z_faces, z, low=0, size=WY):
    block, p = divmod(z, 4)
    rows = slice(low, low + size)
    at = WY + z * WY + low
    here = field[at : at + size]
    k = coefs[block, 0, rows]
    below = z_faces[block, rows] if p == 0 else k
    above = z_faces[block + 1, rows] if p == 3 else k
    source = window(sources, z) if size == WY else sources[1][z]
    total = (
        source
        + below * field[at - WY : at - WY + size]
        + above * field[at + WY : at + WY + size]
        + coefs[block, 1, rows] * field[at - 1 : at - 1 + size]
        + coefs[block, 2, rows] * field[at + 1 : at + 1 + size]
        + coefs[block, 3, rows] * pltpu.roll(here, 1, 1)
        + coefs[block, 4, rows] * pltpu.roll(here, 127, 1)
    )
    kind = (0, 1, 1, 2)[p]
    return here, total, coefs[block, 5 + kind, rows], coefs[block, 8 + kind, rows]


def level_one(y_device):
    return Level(20, 16, 64, 1, 16, False, y_device * 4 - 4, 32, 160)


def build_one(level, kappa, spread, packed, kappa_one, faces):
    for block in range(BLOCKS):
        spread[block * 32 : block * 32 + WY] = kappa[8 + block * WY : 8 + (block + 1) * WY]
        spread[block * 32 + WY : block * 32 + 32] = jnp.ones((32 - WY, 128), jnp.float32)
    pick = lane_map(lambda r, c: matrix(r == 2 * (c % 64), 0.5))
    packed[...] = dot(spread[pl.ds(0, BLOCKS * 16, stride=2), :], pick)
    ones = jnp.ones((16, 128), jnp.float32)
    kappa_one[0:16] = ones
    kappa_one[336:352] = ones
    for block in range(BLOCKS):
        value = packed[block * 16 : block * 16 + 16]
        kappa_one[16 + block * 32 : 32 + block * 32] = value
        kappa_one[32 + block * 32 : 48 + block * 32] = value
    level.build(kappa_one, faces)


def to_chunk(rows):
    group = iota(8, 1) // 32
    out = rows[0:8]
    for z in range(1, 4):
        out = jnp.where(group == z, rows[8 * z : 8 * z + 8], out)
    return out


def down_body(first, copies, *refs):
    index, low, own, high = refs[:4]
    sources = (low, own, high)
    refs = refs[4:]
    if not first:
        fields, coefs, z_faces, faces, refs = refs[:3], refs[3], refs[4], refs[5], refs[6:]
    chunk, edge, kept, source_one, kept_one = refs[:5]
    refs = refs[5:]
    if first:
        coefs, z_faces, faces, refs = refs[0], refs[1], refs[2], refs[3:]
    va, vb, rs, oa, tmp = refs[:5]
    y_device = index[1]
    level = level_one(y_device)
    if first:
        kappa, spread, packed, kappa_one = refs[5:]
        build_fine(sources, y_device, kappa, coefs, z_faces)
        build_one(level, kappa, spread, packed, kappa_one, faces)
    zero = jnp.zeros((WY, 128), jnp.float32)
    for ref in (va, vb):
        ref[0:WY] = zero
        ref[(WZ + 1) * WY : (WZ + 2) * WY] = zero
    if first:
        for z in range(WZ):
            kind = (0, 1, 1, 2)[z % 4]
            va[(z + 1) * WY : (z + 2) * WY] = coefs[z // 4, 5 + kind] * window(sources, z)
    else:
        for z in range(WZ):
            vb[(z + 1) * WY : (z + 2) * WY] = window(fields, z)
        for z in range(WZ):
            here, total, weight, _ = fine_plane(vb, sources, coefs, z_faces, z)
            va[(z + 1) * WY : (z + 2) * WY] = 0.2 * here + weight * total
    for z in range(2, WZ - 2):
        here, total, weight, _ = fine_plane(va, sources, coefs, z_faces, z)
        value = 0.2 * here + weight * total
        vb[(z + 1) * WY : (z + 2) * WY] = value
        if 10 <= z < 30:
            kept[(z - 10) * WY : (z - 9) * WY] = value
    for plane in range(20):
        if 2 <= plane < 18:
            total_defect = 0.0
            for z in (2 * plane, 2 * plane + 1):
                here, total, _, diagonal = fine_plane(vb, sources, coefs, z_faces, z)
                total_defect = total_defect + (total - diagonal * here)
            rs[plane * 32 : plane * 32 + WY] = total_defect
            rs[plane * 32 + WY : plane * 32 + 32] = jnp.zeros((32 - WY, 128), jnp.float32)
        else:
            rs[plane * 32 : plane * 32 + 32] = jnp.zeros((32, 128), jnp.float32)
    mean_x = lane_map(lambda r, c: matrix(r // 2 == c % 64, 0.125))
    source_one[...] = dot(rs[pl.ds(0, 320, stride=2), :] + rs[pl.ds(1, 320, stride=2), :], mean_x)
    for ref in (oa, kept_one):
        ref[0:16] = jnp.zeros((16, 128), jnp.float32)
        ref[336:352] = jnp.zeros((16, 128), jnp.float32)
    level.start(oa, source_one, faces)
    level.relax(oa, kept_one, source_one, faces)
    level.defect(kept_one, source_one, faces, tmp, 6 * 16, 8 * 16)
    for z in range(4):
        tmp[z * 16 : z * 16 + 16] = tmp[z * 32 : z * 32 + 16] + tmp[z * 32 + 16 : z * 32 + 32]
    halves = tmp[pl.ds(0, 32, stride=2), :] + tmp[pl.ds(1, 32, stride=2), :]
    mean_two = lane_map(lambda r, c: matrix((r < 64) & (r // 2 == c % 32), 0.125))
    values = [to_chunk(dot(halves, mean_two))[2:4]]
    if first:
        pick_two = lane_map(lambda r, c: matrix((r < 64) & (r == 2 * (c % 32)), 0.5))
        values.append(to_chunk(dot(packed[pl.ds(48, 32, stride=2), :], pick_two))[2:4])
    repeats = 4 // len(values)
    tile = jnp.concatenate(values * repeats, axis=0)
    for at in range(0, copies // repeats):
        chunk[at * 8 : at * 8 + 8] = tile
    for plane in range(20):
        edge[plane * 4 : plane * 4 + 4] = kept_one[16 + plane * 16 + 4 : 16 + plane * 16 + 8]


def coarse_levels(z_devices):
    return (
        Level(z_devices, 16, 32, 4, 16, True, 0, 16, 128),
        Level(z_devices, 8, 16, 2, 8, True, 0, 8, 128),
        Level(z_devices, 4, 8, 1, 8, True, 0, 4, 128),
    )


def coarse_body(first, z_devices, *refs):
    two, three, four = coarse_levels(z_devices)
    index, gathered = refs[:2]
    refs = refs[2:]
    if first:
        near, f2, f3, f4 = refs[:4]
        refs = refs[4:]
    else:
        f2, f3, f4, near = refs[:4]
        refs = refs[4:]
    a2, b2, r2, a3, b3, r3, g3, a4, b4, g4 = refs[:10]
    z_device = index[0]
    mean_three = lane_map(lambda r, c: matrix(c % 32 == (r // 64) * 16 + (r % 32) // 2, 0.125))
    mean_four = lane_map(lambda r, c: matrix((r < 32) & (c % 8 == (r % 16) // 2), 0.125))
    if first:
        g2, k2, k3, k4 = refs[10:]
        chunks = z_devices * 8
        for part in range(2):
            k2[pl.ds(two.pad + part, chunks, stride=2), :] = gathered[pl.ds(2 + part, chunks, stride=4), :]
            g2[pl.ds(part, chunks, stride=2), :] = gathered[pl.ds(part, chunks, stride=4), :]
        two.wrap(k2)
        two.build(k2, f2)
        r2[...] = k2[two.pad : two.pad + two.rows]
        k3[three.pad : three.pad + three.rows] = 0.5 * dot(two.pairs(r2), mean_three)
        three.wrap(k3)
        three.build(k3, f3)
        r3[...] = k3[three.pad : three.pad + three.rows]
        k4[four.pad : four.pad + four.rows] = 0.5 * dot(three.pairs(r3), mean_four)
        four.wrap(k4)
        four.build(k4, f4)
    else:
        g2 = gathered

    two.start(a2, g2, f2)
    two.relax(a2, b2, g2, f2)
    two.defect(b2, g2, f2, r2)
    g3[...] = dot(two.pairs(r2), mean_three)
    three.start(a3, g3, f3)
    three.relax(a3, b3, g3, f3)
    three.defect(b3, g3, f3, r3)
    g4[...] = dot(three.pairs(r3), mean_four)
    four.start(a4, g4, f4)
    for _ in range(2):
        four.relax(a4, b4, g4, f4)
        four.relax(b4, a4, g4, f4)
    four.relax(a4, b4, g4, f4)

    def correct(level, field, coarse, tmp, spread_lanes):
        value = dot(coarse, spread_lanes)
        half = level.rows // 2
        tmp[pl.ds(0, half, stride=2), :] = value
        tmp[pl.ds(1, half, stride=2), :] = value
        inner = slice(level.pad, level.pad + level.rows)
        field[inner] = field[inner] + tmp[...]
        level.wrap(field)

    from_four = lane_map(lambda r, c: matrix((r < 8) & (r == (c % 16) // 2), 1.0))
    from_three = lane_map(lambda r, c: matrix((r < 32) & (r == (c // 64) * 16 + (c % 32) // 2), 1.0))
    correct(three, b3, b4[four.pad : four.pad + four.rows], r3, from_four)
    three.relax(b3, a3, g3, f3)
    three.relax(a3, b3, g3, f3)
    correct(two, b2, b3[three.pad : three.pad + three.rows], r2, from_three)
    two.relax(b2, a2, g2, f2)
    two.relax(a2, b2, g2, f2)
    near[...] = b2[pl.ds(pl.multiple_of(z_device * 16, 16), 48), :]


def up_body(index, low, own, high, coefs, z_faces, faces, near, edge_low, edge_high, kept, source_one, kept_one, out, va, vb, spread, oa, ob):
    sources = (low, own, high)
    y_device = index[1]
    level = level_one(y_device)
    rows = matrix(iota(16, 1, 16) == y_device * 2 - 2 + iota(16, 0, 16) // 2, 1.0)
    spread_y = jnp.concatenate([dot(rows, near[16 * part : 16 * part + 16]) for part in range(3)], axis=0)
    by_z = [
        dot(spread_y, lane_map(lambda r, c, z=z: matrix(r == z * 32 + (c % 64) // 2, 1.0))) for z in range(4)
    ]
    for plane in range(20):
        part, z = divmod(plane // 2 + 1, 4)
        at = 16 + plane * 16
        field = jnp.concatenate(
            [edge_low[plane * 4 : plane * 4 + 4], kept_one[at + 4 : at + 8],
             edge_high[plane * 4 : plane * 4 + 4], jnp.zeros((4, 128), jnp.float32)], axis=0
        )
        oa[at : at + 16] = field + by_z[z][16 * part : 16 * part + 16]
    level.relax(oa, ob, source_one, faces, 4 * 16, 12 * 16)
    level.relax(ob, oa, source_one, faces, 5 * 16, 10 * 16)
    from_one = lane_map(lambda r, c: matrix((r < 64) & (r == c // 2), 1.0))
    value = dot(oa[16 + 80 : 16 + 240], from_one)
    spread[pl.ds(0, 160, stride=2), :] = value
    spread[pl.ds(1, 160, stride=2), :] = value
    for z in range(10, 30):
        at = ((z - 10) // 2) * 32
        va[(z + 1) * WY : (z + 2) * WY] = kept[(z - 10) * WY : (z - 9) * WY] + spread[at : at + WY]
    for z in range(11, 29):
        here, total, weight, _ = fine_plane(va, sources, coefs, z_faces, z)
        vb[(z + 1) * WY : (z + 2) * WY] = 0.2 * here + weight * total
    for z in range(12, 28):
        here, total, weight, _ = fine_plane(vb, sources, coefs, z_faces, z, 8, 8)
        out[z - 12] = 0.2 * here + weight * total


def floats(*shape):
    return jax.ShapeDtypeStruct(shape, jnp.float32)


def call(body, outs, scratch, args, smem=1, any_space=False):
    vmem = pl.BlockSpec(memory_space=pltpu.VMEM)
    rest = pl.BlockSpec(memory_space=pl.ANY) if any_space else vmem
    return pl.pallas_call(
        body,
        out_shape=outs,
        in_specs=[pl.BlockSpec(memory_space=pltpu.SMEM)] * smem + [rest] * (len(args) - smem),
        out_specs=[vmem] * len(outs),
        scratch_shapes=[pltpu.VMEM(s, jnp.float32) if isinstance(s, tuple) else s for s in scratch],
        compiler_params=pltpu.CompilerParams(vmem_limit_bytes=VMEM_BYTES),
    )(*args)


FIELD = ((WZ + 2) * WY, 128)
COEFS = [(BLOCKS, 11, WY, 128), (BLOCKS + 1, WY, 128), (6, 352, 128)]


def device_count():
    return lax.axis_size("gz") * lax.axis_size("gy")


def down(index, sources, fields, coefs):
    first = fields is None
    copies = device_count()
    outs = [
        floats(copies * (4 if first else 2), 128),
        floats(80, 128),
        floats(20 * WY, 128),
        floats(320, 128),
        floats(352, 128),
    ]
    scratch = [FIELD, FIELD, (640, 128), (352, 128), (128, 128)]
    if first:
        outs += [floats(*shape) for shape in COEFS]
        scratch += [(16 + BLOCKS * WY, 128), (320, 128), (160, 128), (352, 128)]
        args = [index, *sources]
    else:
        args = [index, *sources, *fields, *coefs]
    result = call(lambda *refs: down_body(first, copies, *refs), outs, scratch, args)
    return result[0], result[1], result[2:5], result[5:] if first else coefs


def coarse(index, gathered, faces):
    first = faces is None
    z_devices = lax.axis_size("gz")
    levels = coarse_levels(z_devices)
    outs, scratch = [floats(48, 128)], []
    if first:
        outs += [floats(6, *level.shape()) for level in levels]
    for number, level in enumerate(levels):
        scratch += [level.shape(), level.shape(), (level.rows, 128)]
        if number > 0:
            scratch += [(level.rows, 128)]
    scratch = scratch[:9] + [(levels[2].rows, 128)]
    if first:
        scratch += [(levels[0].rows, 128)] + [level.shape() for level in levels]
    args = [index, gathered] + ([] if first else list(faces))
    near, *new = call(lambda *refs: coarse_body(first, z_devices, *refs), outs, scratch, args)
    return near, new if first else faces


def up(index, sources, coefs, near, edges, kept):
    scratch = [FIELD, FIELD, (320, 128), (352, 128), (352, 128)]
    return call(up_body, [floats(16, 8, 128)], scratch, [index, *sources, *coefs, near, *edges, *kept])[0]


def shifted(array, axis, step):
    count = lax.axis_size(axis)
    return lax.ppermute(array, axis, [(i, (i + step) % count) for i in range(count)])


def both_sides(array, axis):
    return shifted(array, axis, 1), shifted(array, axis, -1)


def to_all(copies):
    devices = device_count()
    copies = copies.reshape(devices, copies.shape[0] // devices, 128)
    out = lax.all_to_all(copies, ("gz", "gy"), 0, 0)
    return out.reshape(out.shape[0] * out.shape[1], 128)


def cycle(index, sources, fields, coefs, coarse_faces):
    copies, edge, kept, coefs = down(index, sources, fields, coefs)
    gathered = to_all(copies)
    edge, _ = lax.optimization_barrier((edge, gathered))
    edges = both_sides(edge, "gy")
    near, coarse_faces = coarse(index, gathered, coarse_faces)
    return up(index, sources, coefs, near, edges, kept), coefs, coarse_faces


def per_device(concentration, phases, grains, grain_class, diffusivity):
    index = jnp.stack([lax.axis_index("gz"), lax.axis_index("gy")]).astype(jnp.int32)
    plane = (4,) + phases.shape[1:]
    kappa, up_part, down_part = call(
        kappa_body,
        [floats(*plane), floats(HALO + 3, 8, 128), floats(HALO + 3, 8, 128)],
        [
            pltpu.SMEM(grain_class.shape, jnp.int32),
            pltpu.SMEM(diffusivity.shape, jnp.float32),
            pltpu.VMEM(plane, jnp.int32),
            pltpu.VMEM(plane, jnp.int32),
            pltpu.SemaphoreType.DMA((12,)),
        ],
        [grain_class, diffusivity, phases, grains, concentration],
        0,
        True,
    )
    before = shifted(up_part, "gz", 1)
    after = shifted(down_part, "gz", -1)
    own = jnp.concatenate(
        [before[:HALO], concentration, after[:HALO], before[HALO:], kappa, after[HALO:]], axis=0
    )
    low, high = both_sides(own, "gy")
    sources = (low, own, high)
    field, coefs, coarse_faces = cycle(index, sources, None, None, None)

    before = shifted(field[16 - HALO :], "gz", 1)
    after = shifted(field[:HALO], "gz", -1)
    field = jnp.concatenate([before, field, after], axis=0)
    low, high = both_sides(field, "gy")
    return cycle(index, sources, (low, field, high), coefs, coarse_faces)[0]


def solution(mesh):
    placed = (P("gz", "gy", None), P("gz", "gy", None), P("gz", "gy", None), P(), P())
    return jax.shard_map(
        per_device, mesh=mesh, in_specs=placed, out_specs=P("gz", "gy", None), check_vma=False
    )
```

```python
import jax
import jax.numpy as jnp
from jax import lax
from jax.experimental import pallas as pl
from jax.experimental.pallas import tpu as pltpu
from jax.sharding import PartitionSpec as P

HALO = 12
WZ = 40
BLOCKS = 10
WY = 24
NEAR = 9
SPAN = 20
VMEM_BYTES = 48 * 1024 * 1024


def harmonic(near_k, far_k):
    return 2.0 * near_k * far_k / (near_k + far_k)


def dot(left, right):
    return jnp.dot(left, right, precision=lax.Precision.HIGHEST, preferred_element_type=jnp.float32)


def iota(rows, dim, lanes=128):
    return lax.broadcasted_iota(jnp.int32, (rows, lanes), dim)


def matrix(condition, value):
    return jnp.where(condition, jnp.float32(value), jnp.float32(0.0))


def lane_map(make):
    return make(iota(128, 0), iota(128, 1))


class Level:
    def __init__(self, planes, ny, nx, zl, pad, y_start, y_total, chunk):
        self.planes, self.ny, self.nx, self.zl, self.pad = planes, ny, nx, zl, pad
        self.y_start, self.y_total = y_start, y_total
        self.rows = planes * ny
        self.chunk = min(chunk, self.rows)

    def chunks(self, start=0, count=None):
        count = self.rows if count is None else count
        at = start
        while at < start + count:
            size = min(self.chunk, start + count - at)
            yield at, size
            at += size

    def neighbours(self, ref, at, size):
        base = self.pad + at
        here = ref[base : base + size]
        below = ref[base - self.ny : base - self.ny + size]
        above = ref[base + self.ny : base + self.ny + size]
        if self.zl > 1:
            cell = iota(size, 1) % (self.zl * self.nx)
            below = pltpu.roll(jnp.where(cell >= (self.zl - 1) * self.nx, below, here), self.nx, 1)
            above = pltpu.roll(jnp.where(cell < self.nx, above, here), 128 - self.nx, 1)
        return (
            here,
            (
                below,
                above,
                ref[base - 1 : base - 1 + size],
                ref[base + 1 : base + 1 + size],
                pltpu.roll(here, 1, 1),
            ),
        )

    def close(self, ref, value):
        edge = jnp.full((self.pad, 128), value, jnp.float32)
        ref[0 : self.pad] = edge
        ref[self.pad + self.rows : 2 * self.pad + self.rows] = edge

    def shape(self):
        return (self.rows + 2 * self.pad, 128)

    def build(self, kappa, faces):
        for number in (0, 2):
            self.close(faces.at[number], 0.0)
        for at, size in self.chunks():
            here, around = self.neighbours(kappa, at, size)
            y = iota(size, 0) % self.ny + self.y_start
            x = iota(size, 1) % self.nx
            rows = slice(self.pad + at, self.pad + at + size)
            faces[0, rows] = harmonic(here, around[0])
            faces[2, rows] = jnp.where((y != 0) & (y != self.y_total), harmonic(here, around[2]), 0.0)
            faces[3, rows] = jnp.where(x != 0, harmonic(here, around[4]), 0.0)
        for at, size in self.chunks():
            rows = slice(self.pad + at, self.pad + at + size)
            z_low, around = self.neighbours(faces.at[0], at, size)
            z_high = around[1]
            y_high = faces[2, self.pad + at + 1 : self.pad + at + 1 + size]
            x_low = faces[3, rows]
            total = 1.0 + z_low + z_high + faces[2, rows] + y_high + x_low + pltpu.roll(x_low, 127, 1)
            faces[1, rows] = z_high
            faces[4, rows] = 0.8 / total
            faces[5, rows] = total

    def coupled(self, field, source, faces, at, size):
        here, around = self.neighbours(field, at, size)
        rows = slice(self.pad + at, self.pad + at + size)
        next_rows = slice(self.pad + at + 1, self.pad + at + 1 + size)
        x_low = faces[3, rows]
        total = (
            source[at : at + size]
            + faces[0, rows] * around[0]
            + faces[1, rows] * around[1]
            + faces[2, rows] * around[2]
            + faces[2, next_rows] * around[3]
            + x_low * around[4]
            + pltpu.roll(x_low * here, 127, 1)
        )
        return here, total

    def start(self, field, source, faces):
        for at, size in self.chunks():
            rows = slice(self.pad + at, self.pad + at + size)
            field[rows] = faces[4, rows] * source[at : at + size]

    def relax(self, field, target, source, faces, start=0, count=None):
        for at, size in self.chunks(start, count):
            here, total = self.coupled(field, source, faces, at, size)
            rows = slice(self.pad + at, self.pad + at + size)
            target[rows] = 0.2 * here + faces[4, rows] * total

    def defect(self, field, source, faces, out, start=0, count=None):
        for at, size in self.chunks(start, count):
            here, total = self.coupled(field, source, faces, at, size)
            diagonal = faces[5, self.pad + at : self.pad + at + size]
            out[at - start : at - start + size] = total - diagonal * here

    def pairs(self, ref):
        half = self.rows // 2
        return ref[pl.ds(0, half, stride=2), :] + ref[pl.ds(1, half, stride=2), :]


def parities(index):
    return index[0] % 2 == 0, index[1] % 2 == 0


def kappa_body(index, class_hbm, diff_hbm, phases_hbm, grains_hbm, conc_hbm, kappa_ref, mate_ref, other_ref, classes, diff, phases, grains, sems):
    even, _ = parities(index)
    num_phases, num_classes = diff.shape
    pairs = [(class_hbm, classes), (diff_hbm, diff)]
    for block in range(4):
        pairs += [(phases_hbm.at[4 * block], phases.at[block]), (grains_hbm.at[4 * block], grains.at[block])]
    top = 16 - HALO
    pairs += [
        (conc_hbm.at[pl.ds(jnp.where(even, top, 0), HALO)], mate_ref.at[0:HALO]),
        (conc_hbm.at[pl.ds(jnp.where(even, 0, top), HALO)], other_ref.at[0:HALO]),
    ]
    copies = [pltpu.make_async_copy(source, target, sems.at[i]) for i, (source, target) in enumerate(pairs)]
    for copy in copies:
        copy.start()
    for copy in copies[:-2]:
        copy.wait()
    grain = grains[...]
    phase = phases[...]
    cls = jnp.zeros(grain.shape, jnp.int32)
    for number in range(classes.shape[0]):
        cls = jnp.where(grain == number, classes[number], cls)
    value = jnp.ones(grain.shape, jnp.float32)
    for p in range(num_phases):
        for c in range(num_classes):
            value = jnp.where((phase == p) & (cls == c), diff[p, c], value)
    kappa_ref[...] = value
    mate_ref[HALO:] = jnp.where(even, value[1:], value[:3])
    other_ref[HALO:] = jnp.where(even, value[:3], value[1:])
    for copy in copies[-2:]:
        copy.wait()


def window(refs, plane, even):
    mate, own, other = (ref[plane] for ref in refs)
    return jnp.concatenate([jnp.where(even, other, mate), own, jnp.where(even, mate, other)], axis=0)


def build_fine(sources, even, y_device, kappa, coefs, z_faces):
    kappa[0:8] = jnp.ones((8, 128), jnp.float32)
    kappa[8 + BLOCKS * WY : 16 + BLOCKS * WY] = jnp.ones((8, 128), jnp.float32)
    for block in range(BLOCKS):
        kappa[8 + block * WY : 8 + (block + 1) * WY] = window(sources, WZ + block, even)
    y = iota(WY, 0) + y_device * 8 - 8
    x = iota(WY, 1)
    for block in range(BLOCKS + 1):
        low, high = max(block - 1, 0), min(block, BLOCKS - 1)
        z_faces[block] = harmonic(
            kappa[8 + low * WY : 8 + (low + 1) * WY], kappa[8 + high * WY : 8 + (high + 1) * WY]
        )
    for block in range(BLOCKS):
        at = 8 + block * WY
        k = kappa[at : at + WY]
        y_low = jnp.where(y == 0, 0.0, harmonic(k, kappa[at - 1 : at - 1 + WY]))
        y_high = jnp.where(y == 63, 0.0, harmonic(k, kappa[at + 1 : at + 1 + WY]))
        x_low = jnp.where(x == 0, 0.0, harmonic(k, pltpu.roll(k, 1, 1)))
        x_high = jnp.where(x == 127, 0.0, harmonic(k, pltpu.roll(k, 127, 1)))
        sides = 1.0 + y_low + y_high + x_low + x_high
        diagonals = (sides + z_faces[block] + k, sides + k + k, sides + k + z_faces[block + 1])
        for number, value in enumerate((k, y_low, y_high, x_low, x_high)):
            coefs[block, number] = value
        for number, value in enumerate(diagonals):
            coefs[block, 5 + number] = 0.8 / value
            coefs[block, 8 + number] = value


def fine_plane(field, source, coefs, z_faces, z, low=0, size=WY):
    block, p = divmod(z, 4)
    rows = slice(low, low + size)
    at = WY + z * WY + low
    here = field[at : at + size]
    k = coefs[block, 0, rows]
    below = z_faces[block, rows] if p == 0 else k
    above = z_faces[block + 1, rows] if p == 3 else k
    total = (
        source[z * WY + low : z * WY + low + size]
        + below * field[at - WY : at - WY + size]
        + above * field[at + WY : at + WY + size]
        + coefs[block, 1, rows] * field[at - 1 : at - 1 + size]
        + coefs[block, 2, rows] * field[at + 1 : at + 1 + size]
        + coefs[block, 3, rows] * pltpu.roll(here, 1, 1)
        + coefs[block, 4, rows] * pltpu.roll(here, 127, 1)
    )
    kind = (0, 1, 1, 2)[p]
    return here, total, coefs[block, 5 + kind, rows], coefs[block, 8 + kind, rows]


def level_one(y_device):
    return Level(20, 16, 64, 1, 16, y_device * 4 - 4, 32, 160)


def build_one(level, kappa, spread, packed, kappa_one, faces):
    for block in range(BLOCKS):
        spread[block * 32 : block * 32 + WY] = kappa[8 + block * WY : 8 + (block + 1) * WY]
        spread[block * 32 + WY : block * 32 + 32] = jnp.ones((32 - WY, 128), jnp.float32)
    pick = lane_map(lambda r, c: matrix(r == 2 * (c % 64), 0.5))
    packed[...] = dot(spread[pl.ds(0, BLOCKS * 16, stride=2), :], pick)
    level.close(kappa_one, 1.0)
    for block in range(BLOCKS):
        value = packed[block * 16 : block * 16 + 16]
        kappa_one[16 + block * 32 : 32 + block * 32] = value
        kappa_one[32 + block * 32 : 48 + block * 32] = value
    level.build(kappa_one, faces)


def to_chunk(rows):
    group = iota(8, 1) // 32
    out = rows[0:8]
    for z in range(1, 4):
        out = jnp.where(group == z, rows[8 * z : 8 * z + 8], out)
    return out


def down_body(first, copies, *refs):
    index, refs = refs[0], refs[1:]
    if first:
        sources, refs = refs[:3], refs[3:]
    else:
        fields, (source, coefs, z_faces, faces), refs = refs[:3], refs[3:7], refs[7:]
    chunk, edge, kept, source_one, kept_one = refs[:5]
    refs = refs[5:]
    if first:
        (source, coefs, z_faces, faces), refs = refs[:4], refs[4:]
    va, vb, rs, oa, tmp = refs[:5]
    _, even = parities(index)
    y_device = index[1]
    level = level_one(y_device)
    if first:
        kappa, spread, packed, kappa_one = refs[5:]
        build_fine(sources, even, y_device, kappa, coefs, z_faces)
        build_one(level, kappa, spread, packed, kappa_one, faces)
    zero = jnp.zeros((WY, 128), jnp.float32)
    for ref in (va, vb):
        ref[0:WY] = zero
        ref[(WZ + 1) * WY : (WZ + 2) * WY] = zero
    if first:
        for z in range(WZ):
            kind = (0, 1, 1, 2)[z % 4]
            value = window(sources, z, even)
            source[z * WY : (z + 1) * WY] = value
            va[(z + 1) * WY : (z + 2) * WY] = coefs[z // 4, 5 + kind] * value
    else:
        for z in range(WZ):
            vb[(z + 1) * WY : (z + 2) * WY] = window(fields, z, even)
        for z in range(WZ):
            here, total, weight, _ = fine_plane(vb, source, coefs, z_faces, z)
            va[(z + 1) * WY : (z + 2) * WY] = 0.2 * here + weight * total
    for z in range(2, WZ - 2):
        here, total, weight, _ = fine_plane(va, source, coefs, z_faces, z)
        value = 0.2 * here + weight * total
        vb[(z + 1) * WY : (z + 2) * WY] = value
        if 10 <= z < 30:
            kept[(z - 10) * WY : (z - 9) * WY] = value
    for plane in range(20):
        if 2 <= plane < 18:
            total_defect = 0.0
            for z in (2 * plane, 2 * plane + 1):
                here, total, _, diagonal = fine_plane(vb, source, coefs, z_faces, z)
                total_defect = total_defect + (total - diagonal * here)
            rs[plane * 32 : plane * 32 + WY] = total_defect
            rs[plane * 32 + WY : plane * 32 + 32] = jnp.zeros((32 - WY, 128), jnp.float32)
        else:
            rs[plane * 32 : plane * 32 + 32] = jnp.zeros((32, 128), jnp.float32)
    mean_x = lane_map(lambda r, c: matrix(r // 2 == c % 64, 0.125))
    source_one[...] = dot(rs[pl.ds(0, 320, stride=2), :] + rs[pl.ds(1, 320, stride=2), :], mean_x)
    for ref in (oa, kept_one):
        level.close(ref, 0.0)
    level.start(oa, source_one, faces)
    level.relax(oa, kept_one, source_one, faces)
    level.defect(kept_one, source_one, faces, tmp, 6 * 16, 8 * 16)
    for z in range(4):
        tmp[z * 16 : z * 16 + 16] = tmp[z * 32 : z * 32 + 16] + tmp[z * 32 + 16 : z * 32 + 32]
    halves = tmp[pl.ds(0, 32, stride=2), :] + tmp[pl.ds(1, 32, stride=2), :]
    mean_two = lane_map(lambda r, c: matrix((r < 64) & (r // 2 == c % 32), 0.125))
    values = [to_chunk(dot(halves, mean_two))[2:4]]
    if first:
        pick_two = lane_map(lambda r, c: matrix((r < 64) & (r == 2 * (c % 32)), 0.5))
        values.append(to_chunk(dot(packed[pl.ds(48, 32, stride=2), :], pick_two))[2:4])
    repeats = 4 // len(values)
    tile = jnp.concatenate(values * repeats, axis=0)
    for at in range(0, copies // repeats):
        chunk[at * 8 : at * 8 + 8] = tile
    for plane in range(20):
        edge[plane * 4 : plane * 4 + 4] = kept_one[16 + plane * 16 + 4 : 16 + plane * 16 + 8]


def coarse_levels():
    return (
        Level(SPAN, 16, 32, 4, 16, 0, 16, 160),
        Level(SPAN, 8, 16, 2, 8, 0, 8, 160),
        Level(SPAN, 4, 8, 1, 8, 0, 4, 128),
    )


def coarse_body(first, z_devices, *refs):
    two, three, four = coarse_levels()
    index, same, mate = refs[:3]
    refs = refs[3:]
    if first:
        near, f2, f3, f4 = refs[:4]
    else:
        f2, f3, f4, near = refs[:4]
    a2, b2, g2, r2, a3, b3, g3, r3, a4, b4, g4, cut_same, cut_mate = refs[4:17]
    z_device = index[0]
    even = index[1] % 2 == 0
    per = 4 if first else 2
    rows = 4 * per
    for number in range(SPAN):
        at = lax.rem(z_device + (number - NEAR + 4 * z_devices), z_devices) * rows
        at = pl.multiple_of(at, 8)
        cut_same[number * rows : (number + 1) * rows] = same[pl.ds(at, rows), :]
        cut_mate[number * rows : (number + 1) * rows] = mate[pl.ds(at, rows), :]

    def interleave(target, start, part):
        for y in range(2):
            take = pl.ds(part + y, 4 * SPAN, stride=per)
            one, two_ = cut_same[take, :], cut_mate[take, :]
            target[pl.ds(start + y, 4 * SPAN, stride=4), :] = jnp.where(even, one, two_)
            target[pl.ds(start + 2 + y, 4 * SPAN, stride=4), :] = jnp.where(even, two_, one)

    interleave(g2, 0, 0)
    mean_three = lane_map(lambda r, c: matrix(c % 32 == (r // 64) * 16 + (r % 32) // 2, 0.125))
    mean_four = lane_map(lambda r, c: matrix((r < 32) & (c % 8 == (r % 16) // 2), 0.125))
    if first:
        k2, k3, k4 = refs[17:]
        interleave(k2, two.pad, 2)
        two.close(k2, 1.0)
        two.build(k2, f2)
        r2[...] = k2[two.pad : two.pad + two.rows]
        k3[three.pad : three.pad + three.rows] = 0.5 * dot(two.pairs(r2), mean_three)
        three.close(k3, 1.0)
        three.build(k3, f3)
        r3[...] = k3[three.pad : three.pad + three.rows]
        k4[four.pad : four.pad + four.rows] = 0.5 * dot(three.pairs(r3), mean_four)
        four.close(k4, 1.0)
        four.build(k4, f4)
    for level, fields in ((two, (a2, b2)), (three, (a3, b3)), (four, (a4, b4))):
        for field in fields:
            level.close(field, 0.0)

    two.start(a2, g2, f2)
    two.relax(a2, b2, g2, f2)
    two.defect(b2, g2, f2, r2)
    g3[...] = dot(two.pairs(r2), mean_three)
    three.start(a3, g3, f3)
    three.relax(a3, b3, g3, f3)
    three.defect(b3, g3, f3, r3)
    g4[...] = dot(three.pairs(r3), mean_four)
    four.start(a4, g4, f4)
    for _ in range(2):
        four.relax(a4, b4, g4, f4)
        four.relax(b4, a4, g4, f4)
    four.relax(a4, b4, g4, f4)

    def correct(level, field, start, count, coarse, tmp, spread_lanes):
        value = dot(coarse, spread_lanes)
        tmp[pl.ds(0, count // 2, stride=2), :] = value
        tmp[pl.ds(1, count // 2, stride=2), :] = value
        inner = slice(level.pad + start, level.pad + start + count)
        field[inner] = field[inner] + tmp[0:count]

    from_four = lane_map(lambda r, c: matrix((r < 8) & (r == (c % 16) // 2), 1.0))
    from_three = lane_map(lambda r, c: matrix((r < 32) & (r == (c // 64) * 16 + (c % 32) // 2), 1.0))
    low = NEAR - 3
    correct(three, b3, 8 * low, 48, b4[four.pad + 4 * low : four.pad + 4 * low + 24], r3, from_four)
    three.relax(b3, a3, g3, f3, 8 * low, 48)
    low = NEAR - 1
    three.relax(a3, b3, g3, f3, 8 * low, 24)
    correct(two, b2, 16 * low, 48, b3[three.pad + 8 * low : three.pad + 8 * low + 24], r2, from_three)
    two.relax(b2, a2, g2, f2, 16 * low, 48)
    two.relax(a2, b2, g2, f2, 16 * low, 48)
    near[...] = b2[two.pad + 16 * low : two.pad + 16 * low + 48]


def up_body(last, *refs):
    index, source, coefs, z_faces, faces, near, edge_mate, edge_other, kept, source_one, kept_one, out = refs[:12]
    refs = refs[12:]
    if not last:
        (mate, other), refs = refs[:2], refs[2:]
    va, vb, spread, oa, ob = refs
    even_z, even = parities(index)
    y_device = index[1]
    level = level_one(y_device)
    rows = matrix(iota(16, 1, 16) == y_device * 2 - 2 + iota(16, 0, 16) // 2, 1.0)
    spread_y = jnp.concatenate([dot(rows, near[16 * part : 16 * part + 16]) for part in range(3)], axis=0)
    by_z = [
        dot(spread_y, lane_map(lambda r, c, z=z: matrix(r == z * 32 + (c % 64) // 2, 1.0))) for z in range(4)
    ]
    for plane in range(20):
        part, z = divmod(plane // 2 + 1, 4)
        at = 16 + plane * 16
        one, two = edge_mate[plane * 4 : plane * 4 + 4], edge_other[plane * 4 : plane * 4 + 4]
        field = jnp.concatenate(
            [jnp.where(even, two, one), kept_one[at + 4 : at + 8], jnp.where(even, one, two),
             jnp.zeros((4, 128), jnp.float32)], axis=0
        )
        oa[at : at + 16] = field + by_z[z][16 * part : 16 * part + 16]
    level.relax(oa, ob, source_one, faces, 4 * 16, 12 * 16)
    level.relax(ob, oa, source_one, faces, 5 * 16, 10 * 16)
    from_one = lane_map(lambda r, c: matrix((r < 64) & (r == c // 2), 1.0))
    value = dot(oa[16 + 80 : 16 + 240], from_one)
    spread[pl.ds(0, 160, stride=2), :] = value
    spread[pl.ds(1, 160, stride=2), :] = value
    for z in range(10, 30):
        at = ((z - 10) // 2) * 32
        va[(z + 1) * WY : (z + 2) * WY] = kept[(z - 10) * WY : (z - 9) * WY] + spread[at : at + WY]
    for z in range(11, 29):
        here, total, weight, _ = fine_plane(va, source, coefs, z_faces, z)
        vb[(z + 1) * WY : (z + 2) * WY] = 0.2 * here + weight * total
    for z in range(12, 28):
        here, total, weight, _ = fine_plane(vb, source, coefs, z_faces, z, 8, 8)
        out[z - 12] = 0.2 * here + weight * total
    if not last:
        top = 16 - HALO
        mate[...] = out[pl.ds(jnp.where(even_z, top, 0), HALO)]
        other[...] = out[pl.ds(jnp.where(even_z, 0, top), HALO)]


def floats(*shape):
    return jax.ShapeDtypeStruct(shape, jnp.float32)


def call(body, outs, scratch, args, inputs=pltpu.VMEM):
    vmem = pl.BlockSpec(memory_space=pltpu.VMEM)
    return pl.pallas_call(
        body,
        out_shape=outs,
        in_specs=[pl.BlockSpec(memory_space=pltpu.SMEM)] + [pl.BlockSpec(memory_space=inputs)] * (len(args) - 1),
        out_specs=[vmem] * len(outs),
        scratch_shapes=[pltpu.VMEM(s, jnp.float32) if isinstance(s, tuple) else s for s in scratch],
        compiler_params=pltpu.CompilerParams(vmem_limit_bytes=VMEM_BYTES),
    )(*args)


FIELD = ((WZ + 2) * WY, 128)
SHARED = [(WZ * WY, 128), (BLOCKS, 11, WY, 128), (BLOCKS + 1, WY, 128), (6, 352, 128)]
Z_AXIS = ("gz",)
Y_AXIS = ("gx", "core")


def down(index, arrays, shared):
    first = shared is None
    copies = lax.axis_size("gz") * lax.axis_size("gx")
    outs = [
        floats(copies * (4 if first else 2), 128),
        floats(80, 128),
        floats(20 * WY, 128),
        floats(320, 128),
        floats(352, 128),
    ]
    scratch = [FIELD, FIELD, (640, 128), (352, 128), (128, 128)]
    if first:
        outs += [floats(*shape) for shape in SHARED]
        scratch += [(16 + BLOCKS * WY, 128), (320, 128), (160, 128), (352, 128)]
        args = [index, *arrays]
    else:
        args = [index, *arrays, *shared]
    result = call(lambda *refs: down_body(first, copies, *refs), outs, scratch, args)
    return result[0], result[1], result[2:5], result[5:] if first else shared


def coarse(index, gathered, faces):
    first = faces is None
    z_devices = lax.axis_size("gz")
    levels = coarse_levels()
    outs, scratch = [floats(48, 128)], []
    if first:
        outs += [floats(6, *level.shape()) for level in levels]
    for level in levels:
        scratch += [level.shape(), level.shape(), (level.rows, 128), (level.rows, 128)]
    cut = (SPAN * (16 if first else 8), 128)
    scratch = scratch[:11] + [cut, cut]
    if first:
        scratch += [level.shape() for level in levels]
    args = [index, *gathered] + ([] if first else list(faces))
    near, *new = call(lambda *refs: coarse_body(first, z_devices, *refs), outs, scratch, args)
    return near, new if first else faces


def up(index, shared, near, edges, kept, last):
    outs = [floats(16, 8, 128)] + ([] if last else [floats(HALO, 8, 128)] * 2)
    scratch = [FIELD, FIELD, (320, 128), (352, 128), (352, 128)]
    return call(
        lambda *refs: up_body(last, *refs), outs, scratch, [index, *shared, near, *edges, *kept]
    )


def mate_of(i):
    return i + 1 if i % 2 == 0 else i - 1


def other_of(i):
    return i - 1 if i % 2 == 0 else i + 1


def swap(array, axis, partner):
    count = 1
    for name in axis:
        count *= lax.axis_size(name)
    return lax.ppermute(array, axis, [(i, partner(i) % count) for i in range(count)])


def swaps(mate, other, axis):
    far = swap(other, axis, other_of)
    return swap(mate, axis, mate_of), far


def to_all(copies):
    peers = lax.axis_size("gz") * lax.axis_size("gx")
    copies = copies.reshape(peers, copies.shape[0] // peers, 128)
    out = lax.all_to_all(copies, ("gz", "gx"), 0, 0)
    out = out.reshape(out.shape[0] * out.shape[1], 128)
    return out, swap(out, Y_AXIS, mate_of)


def stack(index, parts, own):
    even = index[0] % 2 == 0
    mate, other = parts
    before, after = jnp.where(even, other, mate), jnp.where(even, mate, other)
    pieces = [before[:HALO], own[0], after[:HALO]]
    if len(own) > 1:
        pieces += [before[HALO:], own[1], after[HALO:]]
    return jnp.concatenate(pieces, axis=0)


def cycle(index, arrays, shared, coarse_faces, last):
    copies, edge, kept, shared = down(index, arrays, shared)
    edges = swaps(edge, edge, Y_AXIS)
    gathered = to_all(copies)
    near, coarse_faces = coarse(index, gathered, coarse_faces)
    return up(index, shared, near, edges, kept, last), shared, coarse_faces


def per_device(concentration, phases, grains, grain_class, diffusivity):
    y_device = lax.axis_index("gx") * lax.axis_size("core") + lax.axis_index("core")
    index = jnp.stack([lax.axis_index("gz"), y_device]).astype(jnp.int32)
    plane = (4,) + phases.shape[1:]
    part = floats(HALO + 3, 8, 128)
    kappa, *parts = call(
        kappa_body,
        [floats(*plane), part, part],
        [
            pltpu.SMEM(grain_class.shape, jnp.int32),
            pltpu.SMEM(diffusivity.shape, jnp.float32),
            pltpu.VMEM(plane, jnp.int32),
            pltpu.VMEM(plane, jnp.int32),
            pltpu.SemaphoreType.DMA((12,)),
        ],
        [index] + [
            pltpu.with_memory_space_constraint(array, pltpu.HBM)
            for array in (grain_class, diffusivity, phases, grains, concentration)
        ],
        pltpu.HBM,
    )
    own = stack(index, swaps(*parts, Z_AXIS), (concentration, kappa))
    mate, other = swaps(own, own, Y_AXIS)
    (field, *parts), shared, faces = cycle(index, (mate, own, other), None, None, False)

    own = stack(index, swaps(*parts, Z_AXIS), (field,))
    mate, other = swaps(own, own, Y_AXIS)
    return cycle(index, (mate, own, other), shared, faces, True)[0][0]


def solution(mesh):
    z_devices, y_devices = mesh.shape["gz"], mesh.shape["gy"]
    cores = jax.sharding.Mesh(mesh.devices.reshape(z_devices, y_devices // 2, 2), ("gz", "gx", "core"))
    split = P("gz", ("gx", "core"), None)
    return jax.shard_map(
        per_device, mesh=cores, in_specs=(split, split, split, P(), P()), out_specs=split, check_vma=False
    )
```

```python
import jax
import jax.numpy as jnp
from jax import lax
from jax.experimental import pallas as pl
from jax.experimental.pallas import tpu as pltpu
from jax.sharding import PartitionSpec as P

HALO = 12
WZ = 40
BLOCKS = 10
WY = 24
NEAR = 9
SPAN = 20
VMEM_BYTES = 48 * 1024 * 1024


def harmonic(near_k, far_k):
    return 2.0 * near_k * far_k / (near_k + far_k)


def dot(left, right):
    right = right.astype(jnp.bfloat16)
    total = None
    for _ in range(3):
        part = left.astype(jnp.bfloat16)
        left = left - part.astype(jnp.float32)
        product = jnp.dot(part, right, preferred_element_type=jnp.float32)
        total = product if total is None else total + product
    return total


def iota(rows, dim, lanes=128):
    return lax.broadcasted_iota(jnp.int32, (rows, lanes), dim)


def matrix(condition, value):
    return jnp.where(condition, jnp.float32(value), jnp.float32(0.0))


def lane_map(make):
    return make(iota(128, 0), iota(128, 1))


class Level:
    def __init__(self, planes, ny, nx, zl, pad, y_start, y_total, chunk):
        self.planes, self.ny, self.nx, self.zl, self.pad = planes, ny, nx, zl, pad
        self.y_start, self.y_total = y_start, y_total
        self.rows = planes * ny
        self.chunk = min(chunk, self.rows)

    def chunks(self, start=0, count=None):
        count = self.rows if count is None else count
        at = start
        while at < start + count:
            size = min(self.chunk, start + count - at)
            yield at, size
            at += size

    def neighbours(self, ref, at, size):
        base = self.pad + at
        here = ref[base : base + size]
        below = ref[base - self.ny : base - self.ny + size]
        above = ref[base + self.ny : base + self.ny + size]
        if self.zl > 1:
            cell = iota(size, 1) & (self.zl * self.nx - 1)
            below = pltpu.roll(jnp.where(cell >= (self.zl - 1) * self.nx, below, here), self.nx, 1)
            above = pltpu.roll(jnp.where(cell < self.nx, above, here), 128 - self.nx, 1)
        return (
            here,
            (
                below,
                above,
                ref[base - 1 : base - 1 + size],
                ref[base + 1 : base + 1 + size],
                pltpu.roll(here, 1, 1),
            ),
        )

    def close(self, ref, value):
        edge = jnp.full((self.pad, 128), value, jnp.float32)
        ref[0 : self.pad] = edge
        ref[self.pad + self.rows : 2 * self.pad + self.rows] = edge

    def shape(self):
        return (self.rows + 2 * self.pad, 128)

    def build(self, kappa, faces):
        for number in (0, 2):
            self.close(faces.at[number], 0.0)
        for at, size in self.chunks():
            here, around = self.neighbours(kappa, at, size)
            y = (iota(size, 0) & (self.ny - 1)) + self.y_start
            x = iota(size, 1) & (self.nx - 1)
            rows = slice(self.pad + at, self.pad + at + size)
            faces[0, rows] = harmonic(here, around[0])
            faces[2, rows] = jnp.where((y != 0) & (y != self.y_total), harmonic(here, around[2]), 0.0)
            faces[3, rows] = jnp.where(x != 0, harmonic(here, around[4]), 0.0)
        for at, size in self.chunks():
            rows = slice(self.pad + at, self.pad + at + size)
            z_low, around = self.neighbours(faces.at[0], at, size)
            z_high = around[1]
            y_high = faces[2, self.pad + at + 1 : self.pad + at + 1 + size]
            x_low = faces[3, rows]
            total = 1.0 + z_low + z_high + faces[2, rows] + y_high + x_low + pltpu.roll(x_low, 127, 1)
            faces[1, rows] = z_high
            faces[4, rows] = 0.8 / total
            faces[5, rows] = total

    def coupled(self, field, source, faces, at, size):
        here, around = self.neighbours(field, at, size)
        rows = slice(self.pad + at, self.pad + at + size)
        next_rows = slice(self.pad + at + 1, self.pad + at + 1 + size)
        x_low = faces[3, rows]
        total = (
            source[at : at + size]
            + faces[0, rows] * around[0]
            + faces[1, rows] * around[1]
            + faces[2, rows] * around[2]
            + faces[2, next_rows] * around[3]
            + x_low * around[4]
            + pltpu.roll(x_low * here, 127, 1)
        )
        return here, total

    def start(self, field, source, faces):
        for at, size in self.chunks():
            rows = slice(self.pad + at, self.pad + at + size)
            field[rows] = faces[4, rows] * source[at : at + size]

    def relax(self, field, target, source, faces, start=0, count=None):
        for at, size in self.chunks(start, count):
            here, total = self.coupled(field, source, faces, at, size)
            rows = slice(self.pad + at, self.pad + at + size)
            target[rows] = 0.2 * here + faces[4, rows] * total

    def defect(self, field, source, faces, out, start=0, count=None):
        for at, size in self.chunks(start, count):
            here, total = self.coupled(field, source, faces, at, size)
            diagonal = faces[5, self.pad + at : self.pad + at + size]
            out[at - start : at - start + size] = total - diagonal * here

    def pairs(self, ref):
        half = self.rows // 2
        return ref[pl.ds(0, half, stride=2), :] + ref[pl.ds(1, half, stride=2), :]


def parities(index):
    return index[0] % 2 == 0, index[1] % 2 == 0


def kappa_body(index, class_hbm, diff_hbm, phases_hbm, grains_hbm, conc_hbm, kappa_ref, own_ref, mate_ref, other_ref, classes, diff, phases, grains, sems):
    even, _ = parities(index)
    num_phases, num_classes = diff.shape
    pairs = [(class_hbm, classes), (diff_hbm, diff)]
    for block in range(4):
        pairs += [(phases_hbm.at[4 * block], phases.at[block]), (grains_hbm.at[4 * block], grains.at[block])]
    top = 16 - HALO
    pairs += [
        (conc_hbm.at[pl.ds(jnp.where(even, top, 0), HALO)], mate_ref.at[0:HALO]),
        (conc_hbm.at[pl.ds(jnp.where(even, 0, top), HALO)], other_ref.at[0:HALO]),
        (conc_hbm, own_ref),
    ]
    copies = [pltpu.make_async_copy(source, target, sems.at[i]) for i, (source, target) in enumerate(pairs)]
    for copy in copies:
        copy.start()
    for copy in copies[:-3]:
        copy.wait()
    grain = grains[...]
    phase = phases[...]
    cls = jnp.zeros(grain.shape, jnp.int32)
    for number in range(classes.shape[0]):
        cls = jnp.where(grain == number, classes[number], cls)
    value = jnp.ones(grain.shape, jnp.float32)
    for p in range(num_phases):
        for c in range(num_classes):
            value = jnp.where((phase == p) & (cls == c), diff[p, c], value)
    kappa_ref[...] = value
    mate_ref[HALO:] = jnp.where(even, value[1:], value[:3])
    other_ref[HALO:] = jnp.where(even, value[:3], value[1:])
    for copy in copies[-3:]:
        copy.wait()


def window(refs, plane, even):
    mate, own, other = (ref[plane] for ref in refs)
    return jnp.concatenate([jnp.where(even, other, mate), own, jnp.where(even, mate, other)], axis=0)


def build_fine(sources, even, y_device, kappa, coefs, z_faces):
    kappa[0:8] = jnp.ones((8, 128), jnp.float32)
    kappa[8 + BLOCKS * WY : 16 + BLOCKS * WY] = jnp.ones((8, 128), jnp.float32)
    for block in range(BLOCKS):
        kappa[8 + block * WY : 8 + (block + 1) * WY] = window(sources, WZ + block, even)
    y = iota(WY, 0) + y_device * 8 - 8
    x = iota(WY, 1)
    for block in range(BLOCKS + 1):
        low, high = max(block - 1, 0), min(block, BLOCKS - 1)
        z_faces[block] = harmonic(
            kappa[8 + low * WY : 8 + (low + 1) * WY], kappa[8 + high * WY : 8 + (high + 1) * WY]
        )
    for block in range(BLOCKS):
        at = 8 + block * WY
        k = kappa[at : at + WY]
        y_low = jnp.where(y == 0, 0.0, harmonic(k, kappa[at - 1 : at - 1 + WY]))
        y_high = jnp.where(y == 63, 0.0, harmonic(k, kappa[at + 1 : at + 1 + WY]))
        x_low = jnp.where(x == 0, 0.0, harmonic(k, pltpu.roll(k, 1, 1)))
        x_high = jnp.where(x == 127, 0.0, harmonic(k, pltpu.roll(k, 127, 1)))
        sides = 1.0 + y_low + y_high + x_low + x_high
        diagonals = (sides + z_faces[block] + k, sides + k + k, sides + k + z_faces[block + 1])
        for number, value in enumerate((k, y_low, y_high, x_low, x_high)):
            coefs[block, number] = value
        for number, value in enumerate(diagonals):
            coefs[block, 5 + number] = 0.8 / value
            coefs[block, 8 + number] = value


def fine_plane(field, source, coefs, z_faces, z, low=0, size=WY):
    block, p = divmod(z, 4)
    rows = slice(low, low + size)
    at = WY + z * WY + low
    here = field[at : at + size]
    k = coefs[block, 0, rows]
    below = z_faces[block, rows] if p == 0 else k
    above = z_faces[block + 1, rows] if p == 3 else k
    total = (
        source[z * WY + low : z * WY + low + size]
        + below * field[at - WY : at - WY + size]
        + above * field[at + WY : at + WY + size]
        + coefs[block, 1, rows] * field[at - 1 : at - 1 + size]
        + coefs[block, 2, rows] * field[at + 1 : at + 1 + size]
        + coefs[block, 3, rows] * pltpu.roll(here, 1, 1)
        + coefs[block, 4, rows] * pltpu.roll(here, 127, 1)
    )
    kind = (0, 1, 1, 2)[p]
    return here, total, coefs[block, 5 + kind, rows], coefs[block, 8 + kind, rows]


def level_one(y_device):
    return Level(20, 16, 64, 1, 16, y_device * 4 - 4, 32, 160)


def build_one(level, kappa, spread, packed, kappa_one, faces):
    for block in range(BLOCKS):
        spread[block * 32 : block * 32 + WY] = kappa[8 + block * WY : 8 + (block + 1) * WY]
        spread[block * 32 + WY : block * 32 + 32] = jnp.ones((32 - WY, 128), jnp.float32)
    pick = lane_map(lambda r, c: matrix(r == 2 * (c & 63), 0.5))
    packed[...] = dot(spread[pl.ds(0, BLOCKS * 16, stride=2), :], pick)
    level.close(kappa_one, 1.0)
    for block in range(BLOCKS):
        value = packed[block * 16 : block * 16 + 16]
        kappa_one[16 + block * 32 : 32 + block * 32] = value
        kappa_one[32 + block * 32 : 48 + block * 32] = value
    level.build(kappa_one, faces)


def to_chunk(rows):
    group = iota(8, 1) >> 5
    out = rows[0:8]
    for z in range(1, 4):
        out = jnp.where(group == z, rows[8 * z : 8 * z + 8], out)
    return out


def down_body(first, copies, *refs):
    index, refs = refs[0], refs[1:]
    if first:
        sources, refs = refs[:3], refs[3:]
    else:
        fields, (source, coefs, z_faces, faces), refs = refs[:3], refs[3:7], refs[7:]
    chunk, edge, kept, source_one, kept_one = refs[:5]
    refs = refs[5:]
    if first:
        (source, coefs, z_faces, faces), refs = refs[:4], refs[4:]
    va, vb, rs, oa, tmp = refs[:5]
    _, even = parities(index)
    y_device = index[1]
    level = level_one(y_device)
    if first:
        kappa, spread, packed, kappa_one = refs[5:]
        build_fine(sources, even, y_device, kappa, coefs, z_faces)
        build_one(level, kappa, spread, packed, kappa_one, faces)
    zero = jnp.zeros((WY, 128), jnp.float32)
    for ref in (va, vb):
        ref[0:WY] = zero
        ref[(WZ + 1) * WY : (WZ + 2) * WY] = zero
    if first:
        for z in range(WZ):
            kind = (0, 1, 1, 2)[z % 4]
            value = window(sources, z, even)
            source[z * WY : (z + 1) * WY] = value
            va[(z + 1) * WY : (z + 2) * WY] = coefs[z // 4, 5 + kind] * value
    else:
        for z in range(WZ):
            vb[(z + 1) * WY : (z + 2) * WY] = window(fields, z, even)
        for z in range(WZ):
            here, total, weight, _ = fine_plane(vb, source, coefs, z_faces, z)
            va[(z + 1) * WY : (z + 2) * WY] = 0.2 * here + weight * total
    for z in range(2, WZ - 2):
        here, total, weight, _ = fine_plane(va, source, coefs, z_faces, z)
        value = 0.2 * here + weight * total
        vb[(z + 1) * WY : (z + 2) * WY] = value
        if 10 <= z < 30:
            kept[(z - 10) * WY : (z - 9) * WY] = value
    for plane in range(20):
        if 2 <= plane < 18:
            total_defect = 0.0
            for z in (2 * plane, 2 * plane + 1):
                here, total, _, diagonal = fine_plane(vb, source, coefs, z_faces, z)
                total_defect = total_defect + (total - diagonal * here)
            rs[plane * 32 : plane * 32 + WY] = total_defect
            rs[plane * 32 + WY : plane * 32 + 32] = jnp.zeros((32 - WY, 128), jnp.float32)
        else:
            rs[plane * 32 : plane * 32 + 32] = jnp.zeros((32, 128), jnp.float32)
    mean_x = lane_map(lambda r, c: matrix(r >> 1 == (c & 63), 0.125))
    source_one[...] = dot(rs[pl.ds(0, 320, stride=2), :] + rs[pl.ds(1, 320, stride=2), :], mean_x)
    for ref in (oa, kept_one):
        level.close(ref, 0.0)
    level.start(oa, source_one, faces)
    level.relax(oa, kept_one, source_one, faces)
    level.defect(kept_one, source_one, faces, tmp, 6 * 16, 8 * 16)
    for z in range(4):
        tmp[z * 16 : z * 16 + 16] = tmp[z * 32 : z * 32 + 16] + tmp[z * 32 + 16 : z * 32 + 32]
    halves = tmp[pl.ds(0, 32, stride=2), :] + tmp[pl.ds(1, 32, stride=2), :]
    mean_two = lane_map(lambda r, c: matrix((r < 64) & (r >> 1 == (c & 31)), 0.125))
    values = [to_chunk(dot(halves, mean_two))[2:4]]
    if first:
        pick_two = lane_map(lambda r, c: matrix((r < 64) & (r == 2 * (c & 31)), 0.5))
        values.append(to_chunk(dot(packed[pl.ds(48, 32, stride=2), :], pick_two))[2:4])
    repeats = 4 // len(values)
    tile = jnp.concatenate(values * repeats, axis=0)
    for at in range(0, copies // repeats):
        chunk[at * 8 : at * 8 + 8] = tile
    for plane in range(20):
        edge[plane * 4 : plane * 4 + 4] = kept_one[16 + plane * 16 + 4 : 16 + plane * 16 + 8]


def coarse_levels():
    return (
        Level(SPAN, 16, 32, 4, 16, 0, 16, 160),
        Level(SPAN, 8, 16, 2, 8, 0, 8, 160),
        Level(SPAN, 4, 8, 1, 8, 0, 4, 128),
    )


def coarse_body(first, z_devices, *refs):
    two, three, four = coarse_levels()
    index, same, mate = refs[:3]
    refs = refs[3:]
    if first:
        near, f2, f3, f4 = refs[:4]
    else:
        f2, f3, f4, near = refs[:4]
    a2, b2, g2, r2, a3, b3, g3, r3, a4, b4, g4, cut_same, cut_mate = refs[4:17]
    z_device = index[0]
    even = index[1] % 2 == 0
    per = 4 if first else 2
    rows = 4 * per
    for number in range(SPAN):
        at = lax.rem(z_device + (number - NEAR + 4 * z_devices), z_devices) * rows
        at = pl.multiple_of(at, 8)
        cut_same[number * rows : (number + 1) * rows] = same[pl.ds(at, rows), :]
        cut_mate[number * rows : (number + 1) * rows] = mate[pl.ds(at, rows), :]

    def interleave(target, start, part):
        for y in range(2):
            take = pl.ds(part + y, 4 * SPAN, stride=per)
            one, two_ = cut_same[take, :], cut_mate[take, :]
            target[pl.ds(start + y, 4 * SPAN, stride=4), :] = jnp.where(even, one, two_)
            target[pl.ds(start + 2 + y, 4 * SPAN, stride=4), :] = jnp.where(even, two_, one)

    interleave(g2, 0, 0)
    mean_three = lane_map(lambda r, c: matrix((c & 31) == (r >> 6) * 16 + ((r & 31) >> 1), 0.125))
    mean_four = lane_map(lambda r, c: matrix((r < 32) & ((c & 7) == (r & 15) >> 1), 0.125))
    if first:
        k2, k3, k4 = refs[17:]
        interleave(k2, two.pad, 2)
        two.close(k2, 1.0)
        two.build(k2, f2)
        r2[...] = k2[two.pad : two.pad + two.rows]
        k3[three.pad : three.pad + three.rows] = 0.5 * dot(two.pairs(r2), mean_three)
        three.close(k3, 1.0)
        three.build(k3, f3)
        r3[...] = k3[three.pad : three.pad + three.rows]
        k4[four.pad : four.pad + four.rows] = 0.5 * dot(three.pairs(r3), mean_four)
        four.close(k4, 1.0)
        four.build(k4, f4)
    for level, fields in ((two, (a2, b2)), (three, (a3, b3)), (four, (a4, b4))):
        for field in fields:
            level.close(field, 0.0)

    two.start(a2, g2, f2)
    two.relax(a2, b2, g2, f2)
    two.defect(b2, g2, f2, r2)
    g3[...] = dot(two.pairs(r2), mean_three)
    three.start(a3, g3, f3)
    three.relax(a3, b3, g3, f3)
    three.defect(b3, g3, f3, r3)
    g4[...] = dot(three.pairs(r3), mean_four)
    four.start(a4, g4, f4)
    for _ in range(2):
        four.relax(a4, b4, g4, f4)
        four.relax(b4, a4, g4, f4)
    four.relax(a4, b4, g4, f4)

    def correct(level, field, start, count, coarse, tmp, spread_lanes):
        value = dot(coarse, spread_lanes)
        tmp[pl.ds(0, count // 2, stride=2), :] = value
        tmp[pl.ds(1, count // 2, stride=2), :] = value
        inner = slice(level.pad + start, level.pad + start + count)
        field[inner] = field[inner] + tmp[0:count]

    from_four = lane_map(lambda r, c: matrix((r < 8) & (r == (c & 15) >> 1), 1.0))
    from_three = lane_map(lambda r, c: matrix((r < 32) & (r == (c >> 6) * 16 + ((c & 31) >> 1)), 1.0))
    low = NEAR - 3
    correct(three, b3, 8 * low, 48, b4[four.pad + 4 * low : four.pad + 4 * low + 24], r3, from_four)
    three.relax(b3, a3, g3, f3, 8 * low, 48)
    low = NEAR - 1
    three.relax(a3, b3, g3, f3, 8 * low, 24)
    correct(two, b2, 16 * low, 48, b3[three.pad + 8 * low : three.pad + 8 * low + 24], r2, from_three)
    two.relax(b2, a2, g2, f2, 16 * low, 48)
    two.relax(a2, b2, g2, f2, 16 * low, 48)
    near[...] = b2[two.pad + 16 * low : two.pad + 16 * low + 48]


def up_body(last, *refs):
    index, source, coefs, z_faces, faces, near, edge_mate, edge_other, kept, source_one, kept_one, out = refs[:12]
    refs = refs[12:]
    if not last:
        (mate, other), refs = refs[:2], refs[2:]
    va, vb, spread, oa, ob = refs
    even_z, even = parities(index)
    y_device = index[1]
    level = level_one(y_device)
    rows = matrix(iota(16, 1, 16) == y_device * 2 - 2 + (iota(16, 0, 16) >> 1), 1.0)
    spread_y = jnp.concatenate([dot(rows, near[16 * part : 16 * part + 16]) for part in range(3)], axis=0)
    by_z = [
        dot(spread_y, lane_map(lambda r, c, z=z: matrix(r == z * 32 + ((c & 63) >> 1), 1.0))) for z in range(4)
    ]
    for plane in range(20):
        part, z = divmod(plane // 2 + 1, 4)
        at = 16 + plane * 16
        one, two = edge_mate[plane * 4 : plane * 4 + 4], edge_other[plane * 4 : plane * 4 + 4]
        field = jnp.concatenate(
            [jnp.where(even, two, one), kept_one[at + 4 : at + 8], jnp.where(even, one, two),
             jnp.zeros((4, 128), jnp.float32)], axis=0
        )
        oa[at : at + 16] = field + by_z[z][16 * part : 16 * part + 16]
    level.relax(oa, ob, source_one, faces, 4 * 16, 12 * 16)
    level.relax(ob, oa, source_one, faces, 5 * 16, 10 * 16)
    from_one = lane_map(lambda r, c: matrix((r < 64) & (r == c >> 1), 1.0))
    value = dot(oa[16 + 80 : 16 + 240], from_one)
    spread[pl.ds(0, 160, stride=2), :] = value
    spread[pl.ds(1, 160, stride=2), :] = value
    for z in range(10, 30):
        at = ((z - 10) // 2) * 32
        va[(z + 1) * WY : (z + 2) * WY] = kept[(z - 10) * WY : (z - 9) * WY] + spread[at : at + WY]
    for z in range(11, 29):
        here, total, weight, _ = fine_plane(va, source, coefs, z_faces, z)
        vb[(z + 1) * WY : (z + 2) * WY] = 0.2 * here + weight * total
    for z in range(12, 28):
        here, total, weight, _ = fine_plane(vb, source, coefs, z_faces, z, 8, 8)
        out[z - 12] = 0.2 * here + weight * total
    if not last:
        top = 16 - HALO
        mate[...] = out[pl.ds(jnp.where(even_z, top, 0), HALO)]
        other[...] = out[pl.ds(jnp.where(even_z, 0, top), HALO)]


def floats(*shape):
    return jax.ShapeDtypeStruct(shape, jnp.float32)


def call(body, outs, scratch, args, inputs=pltpu.VMEM):
    vmem = pl.BlockSpec(memory_space=pltpu.VMEM)
    return pl.pallas_call(
        body,
        out_shape=outs,
        in_specs=[pl.BlockSpec(memory_space=pltpu.SMEM)] + [pl.BlockSpec(memory_space=inputs)] * (len(args) - 1),
        out_specs=[vmem] * len(outs),
        scratch_shapes=[pltpu.VMEM(s, jnp.float32) if isinstance(s, tuple) else s for s in scratch],
        compiler_params=pltpu.CompilerParams(vmem_limit_bytes=VMEM_BYTES),
    )(*args)


FIELD = ((WZ + 2) * WY, 128)
SHARED = [(WZ * WY, 128), (BLOCKS, 11, WY, 128), (BLOCKS + 1, WY, 128), (6, 352, 128)]
Z_AXIS = ("gz",)
Y_AXIS = ("gx", "core")


def down(index, arrays, shared):
    first = shared is None
    copies = lax.axis_size("gz") * lax.axis_size("gx")
    outs = [
        floats(copies * (4 if first else 2), 128),
        floats(80, 128),
        floats(20 * WY, 128),
        floats(320, 128),
        floats(352, 128),
    ]
    scratch = [FIELD, FIELD, (640, 128), (352, 128), (128, 128)]
    if first:
        outs += [floats(*shape) for shape in SHARED]
        scratch += [(16 + BLOCKS * WY, 128), (320, 128), (160, 128), (352, 128)]
        args = [index, *arrays]
    else:
        args = [index, *arrays, *shared]
    result = call(lambda *refs: down_body(first, copies, *refs), outs, scratch, args)
    return result[0], result[1], result[2:5], result[5:] if first else shared


def coarse(index, gathered, faces):
    first = faces is None
    z_devices = lax.axis_size("gz")
    levels = coarse_levels()
    outs, scratch = [floats(48, 128)], []
    if first:
        outs += [floats(6, *level.shape()) for level in levels]
    for level in levels:
        scratch += [level.shape(), level.shape(), (level.rows, 128), (level.rows, 128)]
    cut = (SPAN * (16 if first else 8), 128)
    scratch = scratch[:11] + [cut, cut]
    if first:
        scratch += [level.shape() for level in levels]
    args = [index, *gathered] + ([] if first else list(faces))
    near, *new = call(lambda *refs: coarse_body(first, z_devices, *refs), outs, scratch, args)
    return near, new if first else faces


def up(index, shared, near, edges, kept, last):
    outs = [floats(16, 8, 128)] + ([] if last else [floats(HALO, 8, 128)] * 2)
    scratch = [FIELD, FIELD, (320, 128), (352, 128), (352, 128)]
    return call(
        lambda *refs: up_body(last, *refs), outs, scratch, [index, *shared, near, *edges, *kept]
    )


def mate_of(i):
    return i + 1 if i % 2 == 0 else i - 1


def other_of(i):
    return i - 1 if i % 2 == 0 else i + 1


def swap(array, axis, partner):
    count = 1
    for name in axis:
        count *= lax.axis_size(name)
    return lax.ppermute(array, axis, [(i, partner(i) % count) for i in range(count)])


def swaps(mate, other, axis):
    far = swap(other, axis, other_of)
    return swap(mate, axis, mate_of), far


def to_all(copies):
    peers = lax.axis_size("gz") * lax.axis_size("gx")
    copies = copies.reshape(peers, copies.shape[0] // peers, 128)
    out = lax.all_to_all(copies, ("gz", "gx"), 0, 0)
    out = out.reshape(out.shape[0] * out.shape[1], 128)
    return out, swap(out, Y_AXIS, mate_of)


def stack(index, parts, own):
    even = index[0] % 2 == 0
    mate, other = parts
    before, after = jnp.where(even, other, mate), jnp.where(even, mate, other)
    pieces = [before[:HALO], own[0], after[:HALO]]
    if len(own) > 1:
        pieces += [before[HALO:], own[1], after[HALO:]]
    return jnp.concatenate(pieces, axis=0)


def cycle(index, arrays, shared, coarse_faces, last):
    copies, edge, kept, shared = down(index, arrays, shared)
    edges = swaps(edge, edge, Y_AXIS)
    gathered = to_all(copies)
    near, coarse_faces = coarse(index, gathered, coarse_faces)
    return up(index, shared, near, edges, kept, last), shared, coarse_faces


def per_device(concentration, phases, grains, grain_class, diffusivity):
    y_device = lax.axis_index("gx") * lax.axis_size("core") + lax.axis_index("core")
    index = jnp.stack([lax.axis_index("gz"), y_device]).astype(jnp.int32)
    plane = (4,) + phases.shape[1:]
    part = floats(HALO + 3, 8, 128)
    kappa, block, *parts = call(
        kappa_body,
        [floats(*plane), floats(*phases.shape), part, part],
        [
            pltpu.SMEM(grain_class.shape, jnp.int32),
            pltpu.SMEM(diffusivity.shape, jnp.float32),
            pltpu.VMEM(plane, jnp.int32),
            pltpu.VMEM(plane, jnp.int32),
            pltpu.SemaphoreType.DMA((13,)),
        ],
        [index] + [
            pltpu.with_memory_space_constraint(array, pltpu.HBM)
            for array in (grain_class, diffusivity, phases, grains, concentration)
        ],
        pltpu.HBM,
    )
    own = stack(index, swaps(*parts, Z_AXIS), (block, kappa))
    mate, other = swaps(own, own, Y_AXIS)
    (field, *parts), shared, faces = cycle(index, (mate, own, other), None, None, False)

    own = stack(index, swaps(*parts, Z_AXIS), (field,))
    mate, other = swaps(own, own, Y_AXIS)
    return cycle(index, (mate, own, other), shared, faces, True)[0][0]


def solution(mesh):
    z_devices, y_devices = mesh.shape["gz"], mesh.shape["gy"]
    cores = jax.sharding.Mesh(mesh.devices.reshape(z_devices, y_devices // 2, 2), ("gz", "gx", "core"))
    split = P("gz", ("gx", "core"), None)
    return jax.shard_map(
        per_device, mesh=cores, in_specs=(split, split, split, P(), P()), out_specs=split, check_vma=False
    )
```

```python
import jax
import jax.numpy as jnp
from jax import lax
from jax.experimental import pallas as pl
from jax.experimental.pallas import tpu as pltpu
from jax.sharding import PartitionSpec as P

HALO = 12
WZ = 40
BLOCKS = 10
WY = 24
NEAR = 9
SPAN = 20
VMEM_BYTES = 48 * 1024 * 1024


def harmonic(near_k, far_k):
    return 2.0 * near_k * far_k / (near_k + far_k)


def dot(left, right):
    return jnp.dot(left, right, precision=lax.Precision.HIGHEST, preferred_element_type=jnp.float32)


def iota(rows, dim, lanes=128):
    return lax.broadcasted_iota(jnp.int32, (rows, lanes), dim)


def matrix(condition, value):
    return jnp.where(condition, jnp.float32(value), jnp.float32(0.0))


def lane_map(make):
    return make(iota(128, 0), iota(128, 1))


class Level:
    def __init__(self, planes, ny, zl, step, span, pad, y_start, y_total, chunk):
        self.planes, self.ny, self.zl, self.step, self.span, self.pad = planes, ny, zl, step, span, pad
        self.y_start, self.y_total = y_start, y_total
        self.rows = planes * ny
        self.chunk = min(chunk, self.rows)

    def chunks(self, start=0, count=None):
        count = self.rows if count is None else count
        at = start
        while at < start + count:
            size = min(self.chunk, start + count - at)
            yield at, size
            at += size

    def neighbours(self, ref, at, size):
        base = self.pad + at
        here = ref[base : base + size]
        below = ref[base - self.ny : base - self.ny + size]
        above = ref[base + self.ny : base + self.ny + size]
        if self.zl > 1:
            width = 128 // self.zl
            lane = iota(size, 1)
            below = pltpu.roll(jnp.where(lane >= 128 - width, below, here), width, 1)
            above = pltpu.roll(jnp.where(lane < width, above, here), 128 - width, 1)
        return (
            here,
            (
                below,
                above,
                ref[base - 1 : base - 1 + size],
                ref[base + 1 : base + 1 + size],
                pltpu.roll(here, self.step, 1),
            ),
        )

    def close(self, ref, value):
        edge = jnp.full((self.pad, 128), value, jnp.float32)
        ref[0 : self.pad] = edge
        ref[self.pad + self.rows : 2 * self.pad + self.rows] = edge

    def shape(self):
        return (self.rows + 2 * self.pad, 128)

    def build(self, kappa, faces):
        for number in (0, 2):
            self.close(faces.at[number], 0.0)
        for at, size in self.chunks():
            here, around = self.neighbours(kappa, at, size)
            y = (iota(size, 0) & (self.ny - 1)) + self.y_start
            x = iota(size, 1) & (self.span - 1)
            rows = slice(self.pad + at, self.pad + at + size)
            faces[0, rows] = harmonic(here, around[0])
            faces[2, rows] = jnp.where((y != 0) & (y != self.y_total), harmonic(here, around[2]), 0.0)
            faces[3, rows] = jnp.where(x >= self.step, harmonic(here, around[4]), 0.0)
        for at, size in self.chunks():
            rows = slice(self.pad + at, self.pad + at + size)
            z_low, around = self.neighbours(faces.at[0], at, size)
            z_high = around[1]
            y_high = faces[2, self.pad + at + 1 : self.pad + at + 1 + size]
            x_low = faces[3, rows]
            total = 1.0 + z_low + z_high + faces[2, rows] + y_high + x_low + pltpu.roll(x_low, 128 - self.step, 1)
            faces[1, rows] = z_high
            faces[4, rows] = 0.8 / total
            faces[5, rows] = total

    def coupled(self, field, source, faces, at, size):
        here, around = self.neighbours(field, at, size)
        rows = slice(self.pad + at, self.pad + at + size)
        next_rows = slice(self.pad + at + 1, self.pad + at + 1 + size)
        x_low = faces[3, rows]
        total = (
            source[at : at + size]
            + faces[0, rows] * around[0]
            + faces[1, rows] * around[1]
            + faces[2, rows] * around[2]
            + faces[2, next_rows] * around[3]
            + x_low * around[4]
            + pltpu.roll(x_low * here, 128 - self.step, 1)
        )
        return here, total

    def start(self, field, source, faces):
        for at, size in self.chunks():
            rows = slice(self.pad + at, self.pad + at + size)
            field[rows] = faces[4, rows] * source[at : at + size]

    def relax(self, field, target, source, faces, start=0, count=None):
        for at, size in self.chunks(start, count):
            here, total = self.coupled(field, source, faces, at, size)
            rows = slice(self.pad + at, self.pad + at + size)
            target[rows] = 0.2 * here + faces[4, rows] * total

    def defect(self, field, source, faces, out, start=0, count=None):
        for at, size in self.chunks(start, count):
            here, total = self.coupled(field, source, faces, at, size)
            diagonal = faces[5, self.pad + at : self.pad + at + size]
            out[at - start : at - start + size] = total - diagonal * here

    def pairs(self, ref):
        half = self.rows // 2
        return ref[pl.ds(0, half, stride=2), :] + ref[pl.ds(1, half, stride=2), :]


def coarsen(value, step, zl=1):
    lane = iota(value.shape[0], 1)
    value = value + jnp.where((lane & step) == 0, pltpu.roll(value, 128 - step, 1), pltpu.roll(value, step, 1))
    if zl == 4:
        value = value + jnp.where((lane & 32) == 0, pltpu.roll(value, 96, 1), pltpu.roll(value, 32, 1))
    if zl == 2:
        value = value + pltpu.roll(value, 64, 1)
    return 0.125 * value


def parities(index):
    return index[0] % 2 == 0, index[1] % 2 == 0


def kappa_body(index, class_hbm, diff_hbm, phases_hbm, grains_hbm, conc_hbm, kappa_ref, own_ref, mate_ref, other_ref, classes, diff, phases, grains, sems):
    even, _ = parities(index)
    num_phases, num_classes = diff.shape
    pairs = [(class_hbm, classes), (diff_hbm, diff)]
    for block in range(4):
        pairs += [(phases_hbm.at[4 * block], phases.at[block]), (grains_hbm.at[4 * block], grains.at[block])]
    top = 16 - HALO
    pairs += [
        (conc_hbm.at[pl.ds(jnp.where(even, top, 0), HALO)], mate_ref.at[0:HALO]),
        (conc_hbm.at[pl.ds(jnp.where(even, 0, top), HALO)], other_ref.at[0:HALO]),
        (conc_hbm, own_ref),
    ]
    copies = [pltpu.make_async_copy(source, target, sems.at[i]) for i, (source, target) in enumerate(pairs)]
    for copy in copies:
        copy.start()
    for copy in copies[:-3]:
        copy.wait()
    grain = grains[...]
    phase = phases[...]
    cls = jnp.zeros(grain.shape, jnp.int32)
    for number in range(classes.shape[0]):
        cls = jnp.where(grain == number, classes[number], cls)
    value = jnp.ones(grain.shape, jnp.float32)
    for p in range(num_phases):
        for c in range(num_classes):
            value = jnp.where((phase == p) & (cls == c), diff[p, c], value)
    kappa_ref[...] = value
    mate_ref[HALO:] = jnp.where(even, value[1:], value[:3])
    other_ref[HALO:] = jnp.where(even, value[:3], value[1:])
    for copy in copies[-3:]:
        copy.wait()


def window(refs, plane, even):
    mate, own, other = (ref[plane] for ref in refs)
    return jnp.concatenate([jnp.where(even, other, mate), own, jnp.where(even, mate, other)], axis=0)


def build_fine(sources, even, y_device, kappa, coefs, z_faces):
    kappa[0:8] = jnp.ones((8, 128), jnp.float32)
    kappa[8 + BLOCKS * WY : 16 + BLOCKS * WY] = jnp.ones((8, 128), jnp.float32)
    for block in range(BLOCKS):
        kappa[8 + block * WY : 8 + (block + 1) * WY] = window(sources, WZ + block, even)
    y = iota(WY, 0) + y_device * 8 - 8
    x = iota(WY, 1)
    for block in range(BLOCKS + 1):
        low, high = max(block - 1, 0), min(block, BLOCKS - 1)
        z_faces[block] = harmonic(
            kappa[8 + low * WY : 8 + (low + 1) * WY], kappa[8 + high * WY : 8 + (high + 1) * WY]
        )
    for block in range(BLOCKS):
        at = 8 + block * WY
        k = kappa[at : at + WY]
        y_low = jnp.where(y == 0, 0.0, harmonic(k, kappa[at - 1 : at - 1 + WY]))
        y_high = jnp.where(y == 63, 0.0, harmonic(k, kappa[at + 1 : at + 1 + WY]))
        x_low = jnp.where(x == 0, 0.0, harmonic(k, pltpu.roll(k, 1, 1)))
        x_high = jnp.where(x == 127, 0.0, harmonic(k, pltpu.roll(k, 127, 1)))
        sides = 1.0 + y_low + y_high + x_low + x_high
        diagonals = (sides + z_faces[block] + k, sides + k + k, sides + k + z_faces[block + 1])
        for number, value in enumerate((k, y_low, y_high, x_low, x_high)):
            coefs[block, number] = value
        for number, value in enumerate(diagonals):
            coefs[block, 5 + number] = 0.8 / value
            coefs[block, 8 + number] = value


def fine_plane(field, source, coefs, z_faces, z, low=0, size=WY):
    block, p = divmod(z, 4)
    rows = slice(low, low + size)
    at = WY + z * WY + low
    here = field[at : at + size]
    k = coefs[block, 0, rows]
    below = z_faces[block, rows] if p == 0 else k
    above = z_faces[block + 1, rows] if p == 3 else k
    total = (
        source[z * WY + low : z * WY + low + size]
        + below * field[at - WY : at - WY + size]
        + above * field[at + WY : at + WY + size]
        + coefs[block, 1, rows] * field[at - 1 : at - 1 + size]
        + coefs[block, 2, rows] * field[at + 1 : at + 1 + size]
        + coefs[block, 3, rows] * pltpu.roll(here, 1, 1)
        + coefs[block, 4, rows] * pltpu.roll(here, 127, 1)
    )
    kind = (0, 1, 1, 2)[p]
    return here, total, coefs[block, 5 + kind, rows], coefs[block, 8 + kind, rows]


def level_one(y_device):
    return Level(20, 16, 1, 2, 128, 16, y_device * 4 - 4, 32, 160)


def build_one(level, kappa, spread, packed, kappa_one, faces):
    for block in range(BLOCKS):
        spread[block * 32 : block * 32 + WY] = kappa[8 + block * WY : 8 + (block + 1) * WY]
        spread[block * 32 + WY : block * 32 + 32] = jnp.ones((32 - WY, 128), jnp.float32)
    packed[...] = 0.5 * spread[pl.ds(0, BLOCKS * 16, stride=2), :]
    level.close(kappa_one, 1.0)
    for block in range(BLOCKS):
        value = packed[block * 16 : block * 16 + 16]
        kappa_one[16 + block * 32 : 32 + block * 32] = value
        kappa_one[32 + block * 32 : 48 + block * 32] = value
    level.build(kappa_one, faces)


def to_chunk(rows):
    group = iota(8, 1) >> 5
    out = rows[0:8]
    for z in range(1, 4):
        out = jnp.where(group == z, rows[8 * z : 8 * z + 8], out)
    return out


def down_body(first, copies, *refs):
    index, refs = refs[0], refs[1:]
    if first:
        sources, refs = refs[:3], refs[3:]
    else:
        fields, (source, coefs, z_faces, faces), refs = refs[:3], refs[3:7], refs[7:]
    chunk, edge, kept, source_one, kept_one = refs[:5]
    refs = refs[5:]
    if first:
        (source, coefs, z_faces, faces), refs = refs[:4], refs[4:]
    va, vb, rs, oa, tmp = refs[:5]
    _, even = parities(index)
    y_device = index[1]
    level = level_one(y_device)
    if first:
        kappa, spread, packed, kappa_one = refs[5:]
        build_fine(sources, even, y_device, kappa, coefs, z_faces)
        build_one(level, kappa, spread, packed, kappa_one, faces)
    zero = jnp.zeros((WY, 128), jnp.float32)
    for ref in (va, vb):
        ref[0:WY] = zero
        ref[(WZ + 1) * WY : (WZ + 2) * WY] = zero
    if first:
        for z in range(WZ):
            kind = (0, 1, 1, 2)[z % 4]
            value = window(sources, z, even)
            source[z * WY : (z + 1) * WY] = value
            va[(z + 1) * WY : (z + 2) * WY] = coefs[z // 4, 5 + kind] * value
    else:
        for z in range(WZ):
            vb[(z + 1) * WY : (z + 2) * WY] = window(fields, z, even)
        for z in range(WZ):
            here, total, weight, _ = fine_plane(vb, source, coefs, z_faces, z)
            va[(z + 1) * WY : (z + 2) * WY] = 0.2 * here + weight * total
    for z in range(2, WZ - 2):
        here, total, weight, _ = fine_plane(va, source, coefs, z_faces, z)
        value = 0.2 * here + weight * total
        vb[(z + 1) * WY : (z + 2) * WY] = value
        if 10 <= z < 30:
            kept[(z - 10) * WY : (z - 9) * WY] = value
    for plane in range(20):
        if 2 <= plane < 18:
            total_defect = 0.0
            for z in (2 * plane, 2 * plane + 1):
                here, total, _, diagonal = fine_plane(vb, source, coefs, z_faces, z)
                total_defect = total_defect + (total - diagonal * here)
            rs[plane * 32 : plane * 32 + WY] = total_defect
            rs[plane * 32 + WY : plane * 32 + 32] = jnp.zeros((32 - WY, 128), jnp.float32)
        else:
            rs[plane * 32 : plane * 32 + 32] = jnp.zeros((32, 128), jnp.float32)
    source_one[...] = coarsen(rs[pl.ds(0, 320, stride=2), :] + rs[pl.ds(1, 320, stride=2), :], 1)
    for ref in (oa, kept_one):
        level.close(ref, 0.0)
    level.start(oa, source_one, faces)
    level.relax(oa, kept_one, source_one, faces)
    level.defect(kept_one, source_one, faces, tmp, 6 * 16, 8 * 16)
    for z in range(4):
        tmp[z * 16 : z * 16 + 16] = tmp[z * 32 : z * 32 + 16] + tmp[z * 32 + 16 : z * 32 + 32]
    halves = tmp[pl.ds(0, 32, stride=2), :] + tmp[pl.ds(1, 32, stride=2), :]
    mean_two = lane_map(lambda r, c: matrix(((r & 1) == 0) & (r >> 2 == (c & 31)), 0.125))
    values = [to_chunk(dot(halves, mean_two))[2:4]]
    if first:
        pick_two = lane_map(lambda r, c: matrix(r == 4 * (c & 31), 0.5))
        values.append(to_chunk(dot(packed[pl.ds(48, 32, stride=2), :], pick_two))[2:4])
    repeats = 4 // len(values)
    tile = jnp.concatenate(values * repeats, axis=0)
    for at in range(0, copies // repeats):
        chunk[at * 8 : at * 8 + 8] = tile
    for plane in range(20):
        edge[plane * 4 : plane * 4 + 4] = kept_one[16 + plane * 16 + 4 : 16 + plane * 16 + 8]


def coarse_levels():
    return (
        Level(SPAN, 16, 4, 1, 32, 16, 0, 16, 160),
        Level(SPAN, 8, 2, 2, 32, 8, 0, 8, 160),
        Level(SPAN, 4, 1, 4, 32, 8, 0, 4, 128),
    )


def coarse_body(first, z_devices, *refs):
    two, three, four = coarse_levels()
    index, same, mate = refs[:3]
    refs = refs[3:]
    if first:
        near, f2, f3, f4 = refs[:4]
    else:
        f2, f3, f4, near = refs[:4]
    a2, b2, g2, r2, a3, b3, g3, r3, a4, b4, g4, cut_same, cut_mate = refs[4:17]
    z_device = index[0]
    even = index[1] % 2 == 0
    per = 4 if first else 2
    rows = 4 * per
    for number in range(SPAN):
        at = lax.rem(z_device + (number - NEAR + 4 * z_devices), z_devices) * rows
        at = pl.multiple_of(at, 8)
        cut_same[number * rows : (number + 1) * rows] = same[pl.ds(at, rows), :]
        cut_mate[number * rows : (number + 1) * rows] = mate[pl.ds(at, rows), :]

    def interleave(target, start, part):
        for y in range(2):
            take = pl.ds(part + y, 4 * SPAN, stride=per)
            one, two_ = cut_same[take, :], cut_mate[take, :]
            target[pl.ds(start + y, 4 * SPAN, stride=4), :] = jnp.where(even, one, two_)
            target[pl.ds(start + 2 + y, 4 * SPAN, stride=4), :] = jnp.where(even, two_, one)

    interleave(g2, 0, 0)
    if first:
        k2, k3, k4 = refs[17:]
        interleave(k2, two.pad, 2)
        two.close(k2, 1.0)
        two.build(k2, f2)
        r2[...] = k2[two.pad : two.pad + two.rows]
        k3[three.pad : three.pad + three.rows] = 0.5 * coarsen(two.pairs(r2), 1, 4)
        three.close(k3, 1.0)
        three.build(k3, f3)
        r3[...] = k3[three.pad : three.pad + three.rows]
        k4[four.pad : four.pad + four.rows] = 0.5 * coarsen(three.pairs(r3), 2, 2)
        four.close(k4, 1.0)
        four.build(k4, f4)
    for level, fields in ((two, (a2, b2)), (three, (a3, b3)), (four, (a4, b4))):
        for field in fields:
            level.close(field, 0.0)

    two.start(a2, g2, f2)
    two.relax(a2, b2, g2, f2)
    two.defect(b2, g2, f2, r2)
    g3[...] = coarsen(two.pairs(r2), 1, 4)
    three.start(a3, g3, f3)
    three.relax(a3, b3, g3, f3)
    three.defect(b3, g3, f3, r3)
    g4[...] = coarsen(three.pairs(r3), 2, 2)
    four.start(a4, g4, f4)
    for _ in range(2):
        four.relax(a4, b4, g4, f4)
        four.relax(b4, a4, g4, f4)
    four.relax(a4, b4, g4, f4)

    def correct(level, field, start, count, value, tmp):
        tmp[pl.ds(0, count // 2, stride=2), :] = value
        tmp[pl.ds(1, count // 2, stride=2), :] = value
        inner = slice(level.pad + start, level.pad + start + count)
        field[inner] = field[inner] + tmp[0:count]

    low = NEAR - 3
    correct(three, b3, 8 * low, 48, b4[four.pad + 4 * low : four.pad + 4 * low + 24], r3)
    three.relax(b3, a3, g3, f3, 8 * low, 48)
    low = NEAR - 1
    three.relax(a3, b3, g3, f3, 8 * low, 24)
    correct(two, b2, 16 * low, 48, b3[three.pad + 8 * low : three.pad + 8 * low + 24], r2)
    two.relax(b2, a2, g2, f2, 16 * low, 48)
    two.relax(a2, b2, g2, f2, 16 * low, 48)
    near[...] = b2[two.pad + 16 * low : two.pad + 16 * low + 48]


def up_body(last, *refs):
    index, source, coefs, z_faces, faces, near, edge_mate, edge_other, kept, source_one, kept_one, out = refs[:12]
    refs = refs[12:]
    if not last:
        (mate, other), refs = refs[:2], refs[2:]
    va, vb, spread, oa, ob = refs
    even_z, even = parities(index)
    y_device = index[1]
    level = level_one(y_device)
    rows = matrix(iota(16, 1, 16) == y_device * 2 - 2 + (iota(16, 0, 16) >> 1), 1.0)
    spread_y = jnp.concatenate([dot(rows, near[16 * part : 16 * part + 16]) for part in range(3)], axis=0)
    by_z = [
        dot(spread_y, lane_map(lambda r, c, z=z: matrix(r == z * 32 + (c >> 2), 1.0))) for z in range(4)
    ]
    for plane in range(20):
        part, z = divmod(plane // 2 + 1, 4)
        at = 16 + plane * 16
        one, two = edge_mate[plane * 4 : plane * 4 + 4], edge_other[plane * 4 : plane * 4 + 4]
        field = jnp.concatenate(
            [jnp.where(even, two, one), kept_one[at + 4 : at + 8], jnp.where(even, one, two),
             jnp.zeros((4, 128), jnp.float32)], axis=0
        )
        oa[at : at + 16] = field + by_z[z][16 * part : 16 * part + 16]
    level.relax(oa, ob, source_one, faces, 4 * 16, 12 * 16)
    level.relax(ob, oa, source_one, faces, 5 * 16, 10 * 16)
    value = oa[16 + 80 : 16 + 240]
    spread[pl.ds(0, 160, stride=2), :] = value
    spread[pl.ds(1, 160, stride=2), :] = value
    for z in range(10, 30):
        at = ((z - 10) // 2) * 32
        va[(z + 1) * WY : (z + 2) * WY] = kept[(z - 10) * WY : (z - 9) * WY] + spread[at : at + WY]
    for z in range(11, 29):
        here, total, weight, _ = fine_plane(va, source, coefs, z_faces, z)
        vb[(z + 1) * WY : (z + 2) * WY] = 0.2 * here + weight * total
    for z in range(12, 28):
        here, total, weight, _ = fine_plane(vb, source, coefs, z_faces, z, 8, 8)
        out[z - 12] = 0.2 * here + weight * total
    if not last:
        top = 16 - HALO
        mate[...] = out[pl.ds(jnp.where(even_z, top, 0), HALO)]
        other[...] = out[pl.ds(jnp.where(even_z, 0, top), HALO)]


def floats(*shape):
    return jax.ShapeDtypeStruct(shape, jnp.float32)


def call(body, outs, scratch, args, inputs=pltpu.VMEM):
    vmem = pl.BlockSpec(memory_space=pltpu.VMEM)
    return pl.pallas_call(
        body,
        out_shape=outs,
        in_specs=[pl.BlockSpec(memory_space=pltpu.SMEM)] + [pl.BlockSpec(memory_space=inputs)] * (len(args) - 1),
        out_specs=[vmem] * len(outs),
        scratch_shapes=[pltpu.VMEM(s, jnp.float32) if isinstance(s, tuple) else s for s in scratch],
        compiler_params=pltpu.CompilerParams(vmem_limit_bytes=VMEM_BYTES),
    )(*args)


FIELD = ((WZ + 2) * WY, 128)
SHARED = [(WZ * WY, 128), (BLOCKS, 11, WY, 128), (BLOCKS + 1, WY, 128), (6, 352, 128)]
Z_AXIS = ("gz",)
Y_AXIS = ("gx", "core")


def down(index, arrays, shared):
    first = shared is None
    copies = lax.axis_size("gz") * lax.axis_size("gx")
    outs = [
        floats(copies * (4 if first else 2), 128),
        floats(80, 128),
        floats(20 * WY, 128),
        floats(320, 128),
        floats(352, 128),
    ]
    scratch = [FIELD, FIELD, (640, 128), (352, 128), (128, 128)]
    if first:
        outs += [floats(*shape) for shape in SHARED]
        scratch += [(16 + BLOCKS * WY, 128), (320, 128), (160, 128), (352, 128)]
        args = [index, *arrays]
    else:
        args = [index, *arrays, *shared]
    result = call(lambda *refs: down_body(first, copies, *refs), outs, scratch, args)
    return result[0], result[1], result[2:5], result[5:] if first else shared


def coarse(index, gathered, faces):
    first = faces is None
    z_devices = lax.axis_size("gz")
    levels = coarse_levels()
    outs, scratch = [floats(48, 128)], []
    if first:
        outs += [floats(6, *level.shape()) for level in levels]
    for level in levels:
        scratch += [level.shape(), level.shape(), (level.rows, 128), (level.rows, 128)]
    cut = (SPAN * (16 if first else 8), 128)
    scratch = scratch[:11] + [cut, cut]
    if first:
        scratch += [level.shape() for level in levels]
    args = [index, *gathered] + ([] if first else list(faces))
    near, *new = call(lambda *refs: coarse_body(first, z_devices, *refs), outs, scratch, args)
    return near, new if first else faces


def up(index, shared, near, edges, kept, last):
    outs = [floats(16, 8, 128)] + ([] if last else [floats(HALO, 8, 128)] * 2)
    scratch = [FIELD, FIELD, (320, 128), (352, 128), (352, 128)]
    return call(
        lambda *refs: up_body(last, *refs), outs, scratch, [index, *shared, near, *edges, *kept]
    )


def mate_of(i):
    return i + 1 if i % 2 == 0 else i - 1


def other_of(i):
    return i - 1 if i % 2 == 0 else i + 1


def swap(array, axis, partner):
    count = 1
    for name in axis:
        count *= lax.axis_size(name)
    return lax.ppermute(array, axis, [(i, partner(i) % count) for i in range(count)])


def swaps(mate, other, axis):
    far = swap(other, axis, other_of)
    return swap(mate, axis, mate_of), far


def to_all(copies):
    peers = lax.axis_size("gz") * lax.axis_size("gx")
    copies = copies.reshape(peers, copies.shape[0] // peers, 128)
    out = lax.all_to_all(copies, ("gz", "gx"), 0, 0)
    out = out.reshape(out.shape[0] * out.shape[1], 128)
    return out, swap(out, Y_AXIS, mate_of)


def stack(index, parts, own):
    even = index[0] % 2 == 0
    mate, other = parts
    before, after = jnp.where(even, other, mate), jnp.where(even, mate, other)
    pieces = [before[:HALO], own[0], after[:HALO]]
    if len(own) > 1:
        pieces += [before[HALO:], own[1], after[HALO:]]
    return jnp.concatenate(pieces, axis=0)


def cycle(index, arrays, shared, coarse_faces, last):
    copies, edge, kept, shared = down(index, arrays, shared)
    edges = swaps(edge, edge, Y_AXIS)
    gathered = to_all(copies)
    near, coarse_faces = coarse(index, gathered, coarse_faces)
    return up(index, shared, near, edges, kept, last), shared, coarse_faces


def per_device(concentration, phases, grains, grain_class, diffusivity):
    y_device = lax.axis_index("gx") * lax.axis_size("core") + lax.axis_index("core")
    index = jnp.stack([lax.axis_index("gz"), y_device]).astype(jnp.int32)
    plane = (4,) + phases.shape[1:]
    part = floats(HALO + 3, 8, 128)
    kappa, block, *parts = call(
        kappa_body,
        [floats(*plane), floats(*phases.shape), part, part],
        [
            pltpu.SMEM(grain_class.shape, jnp.int32),
            pltpu.SMEM(diffusivity.shape, jnp.float32),
            pltpu.VMEM(plane, jnp.int32),
            pltpu.VMEM(plane, jnp.int32),
            pltpu.SemaphoreType.DMA((13,)),
        ],
        [index] + [
            pltpu.with_memory_space_constraint(array, pltpu.HBM)
            for array in (grain_class, diffusivity, phases, grains, concentration)
        ],
        pltpu.HBM,
    )
    own = stack(index, swaps(*parts, Z_AXIS), (block, kappa))
    mate, other = swaps(own, own, Y_AXIS)
    (field, *parts), shared, faces = cycle(index, (mate, own, other), None, None, False)

    own = stack(index, swaps(*parts, Z_AXIS), (field,))
    mate, other = swaps(own, own, Y_AXIS)
    return cycle(index, (mate, own, other), shared, faces, True)[0][0]


def solution(mesh):
    z_devices, y_devices = mesh.shape["gz"], mesh.shape["gy"]
    cores = jax.sharding.Mesh(mesh.devices.reshape(z_devices, y_devices // 2, 2), ("gz", "gx", "core"))
    split = P("gz", ("gx", "core"), None)
    return jax.shard_map(
        per_device, mesh=cores, in_specs=(split, split, split, P(), P()), out_specs=split, check_vma=False
    )
```

```python
import jax
import jax.numpy as jnp
from jax import lax
from jax.experimental import pallas as pl
from jax.experimental.pallas import tpu as pltpu
from jax.sharding import PartitionSpec as P

HALO = 10
FIELD_HALO = 11
WZ = 40
BLOCKS = 10
WY = 24
NEAR = 9
SPAN = 20
VMEM_BYTES = 48 * 1024 * 1024


def harmonic(near_k, far_k):
    return 2.0 * near_k * far_k / (near_k + far_k)


def dot(left, right):
    return jnp.dot(left, right, precision=lax.Precision.HIGHEST, preferred_element_type=jnp.float32)


def iota(rows, dim, lanes=128):
    return lax.broadcasted_iota(jnp.int32, (rows, lanes), dim)


def matrix(condition, value):
    return jnp.where(condition, jnp.float32(value), jnp.float32(0.0))


def lane_map(make):
    return make(iota(128, 0), iota(128, 1))


class Level:
    def __init__(self, planes, ny, zl, step, span, pad, y_start, y_total, chunk):
        self.planes, self.ny, self.zl, self.step, self.span, self.pad = planes, ny, zl, step, span, pad
        self.y_start, self.y_total = y_start, y_total
        self.rows = planes * ny
        self.chunk = min(chunk, self.rows)

    def chunks(self, start=0, count=None):
        count = self.rows if count is None else count
        at = start
        while at < start + count:
            size = min(self.chunk, start + count - at)
            yield at, size
            at += size

    def neighbours(self, ref, at, size):
        base = self.pad + at
        here = ref[base : base + size]
        below = ref[base - self.ny : base - self.ny + size]
        above = ref[base + self.ny : base + self.ny + size]
        if self.zl > 1:
            width = 128 // self.zl
            lane = iota(size, 1)
            below = pltpu.roll(jnp.where(lane >= 128 - width, below, here), width, 1)
            above = pltpu.roll(jnp.where(lane < width, above, here), 128 - width, 1)
        return (
            here,
            (
                below,
                above,
                ref[base - 1 : base - 1 + size],
                ref[base + 1 : base + 1 + size],
                pltpu.roll(here, self.step, 1),
            ),
        )

    def close(self, ref, value):
        edge = jnp.full((self.pad, 128), value, jnp.float32)
        ref[0 : self.pad] = edge
        ref[self.pad + self.rows : 2 * self.pad + self.rows] = edge

    def shape(self):
        return (self.rows + 2 * self.pad, 128)

    def build(self, kappa, faces):
        for number in (0, 2):
            self.close(faces.at[number], 0.0)
        for at, size in self.chunks():
            here, around = self.neighbours(kappa, at, size)
            y = (iota(size, 0) & (self.ny - 1)) + self.y_start
            x = iota(size, 1) & (self.span - 1)
            rows = slice(self.pad + at, self.pad + at + size)
            faces[0, rows] = harmonic(here, around[0])
            faces[2, rows] = jnp.where((y != 0) & (y != self.y_total), harmonic(here, around[2]), 0.0)
            faces[3, rows] = jnp.where(x >= self.step, harmonic(here, around[4]), 0.0)
        for at, size in self.chunks():
            rows = slice(self.pad + at, self.pad + at + size)
            z_low, around = self.neighbours(faces.at[0], at, size)
            z_high = around[1]
            y_high = faces[2, self.pad + at + 1 : self.pad + at + 1 + size]
            x_low = faces[3, rows]
            total = 1.0 + z_low + z_high + faces[2, rows] + y_high + x_low + pltpu.roll(x_low, 128 - self.step, 1)
            faces[1, rows] = z_high
            faces[4, rows] = 0.8 / total
            faces[5, rows] = total

    def coupled(self, field, source, faces, at, size):
        here, around = self.neighbours(field, at, size)
        rows = slice(self.pad + at, self.pad + at + size)
        next_rows = slice(self.pad + at + 1, self.pad + at + 1 + size)
        x_low = faces[3, rows]
        total = (
            source[at : at + size]
            + faces[0, rows] * around[0]
            + faces[1, rows] * around[1]
            + faces[2, rows] * around[2]
            + faces[2, next_rows] * around[3]
            + x_low * around[4]
            + pltpu.roll(x_low * here, 128 - self.step, 1)
        )
        return here, total

    def start(self, field, source, faces):
        for at, size in self.chunks():
            rows = slice(self.pad + at, self.pad + at + size)
            field[rows] = faces[4, rows] * source[at : at + size]

    def relax(self, field, target, source, faces, start=0, count=None):
        for at, size in self.chunks(start, count):
            here, total = self.coupled(field, source, faces, at, size)
            rows = slice(self.pad + at, self.pad + at + size)
            target[rows] = 0.2 * here + faces[4, rows] * total

    def defect(self, field, source, faces, out, start=0, count=None):
        for at, size in self.chunks(start, count):
            here, total = self.coupled(field, source, faces, at, size)
            diagonal = faces[5, self.pad + at : self.pad + at + size]
            out[at - start : at - start + size] = total - diagonal * here

    def pairs(self, ref):
        half = self.rows // 2
        return ref[pl.ds(0, half, stride=2), :] + ref[pl.ds(1, half, stride=2), :]


def coarsen(value, step, zl=1):
    lane = iota(value.shape[0], 1)
    value = value + jnp.where((lane & step) == 0, pltpu.roll(value, 128 - step, 1), pltpu.roll(value, step, 1))
    if zl == 4:
        value = value + jnp.where((lane & 32) == 0, pltpu.roll(value, 96, 1), pltpu.roll(value, 32, 1))
    if zl == 2:
        value = value + pltpu.roll(value, 64, 1)
    return 0.125 * value


def parities(index):
    return index[0] % 2 == 0, index[1] % 2 == 0


def kappa_body(index, class_hbm, diff_hbm, phases_hbm, grains_hbm, conc_hbm, kappa_ref, own_ref, mate_ref, other_ref, classes, diff, phases, grains, sems):
    even, _ = parities(index)
    num_phases, num_classes = diff.shape
    pairs = [(class_hbm, classes), (diff_hbm, diff)]
    for block in range(4):
        pairs += [(phases_hbm.at[4 * block], phases.at[block]), (grains_hbm.at[4 * block], grains.at[block])]
    top = 16 - HALO
    pairs += [
        (conc_hbm.at[pl.ds(jnp.where(even, top, 0), HALO)], mate_ref.at[0:HALO]),
        (conc_hbm.at[pl.ds(jnp.where(even, 0, top), HALO)], other_ref.at[0:HALO]),
        (conc_hbm, own_ref),
    ]
    copies = [pltpu.make_async_copy(source, target, sems.at[i]) for i, (source, target) in enumerate(pairs)]
    for copy in copies:
        copy.start()
    for copy in copies[:-3]:
        copy.wait()
    grain = grains[...]
    phase = phases[...]
    cls = jnp.zeros(grain.shape, jnp.int32)
    for number in range(classes.shape[0]):
        cls = jnp.where(grain == number, classes[number], cls)
    value = jnp.ones(grain.shape, jnp.float32)
    for p in range(num_phases):
        for c in range(num_classes):
            value = jnp.where((phase == p) & (cls == c), diff[p, c], value)
    rows = jnp.concatenate([value[block, 4 * half : 4 * half + 1] for block in range(4) for half in range(2)], axis=0)
    kappa_ref[0] = rows
    mate_ref[HALO] = rows
    other_ref[HALO] = rows
    for copy in copies[-3:]:
        copy.wait()


def window(refs, plane, even):
    mate, own, other = (ref[plane] for ref in refs)
    return jnp.concatenate([jnp.where(even, other, mate), own, jnp.where(even, mate, other)], axis=0)


def build_fine(sources, even, y_device, kappa, coefs, z_faces):
    kappa[0:8] = jnp.ones((8, 128), jnp.float32)
    kappa[8 + BLOCKS * WY : 16 + BLOCKS * WY] = jnp.ones((8, 128), jnp.float32)
    for block in range(BLOCKS):
        plane, number = divmod(block + 1, 4)
        two = slice(2 * number, 2 * number + 2)
        mate, own, other = (ref[16 + 2 * HALO + plane, two] for ref in sources)
        rows = (jnp.where(even, other, mate), own, jnp.where(even, mate, other))
        kappa[8 + block * WY : 8 + (block + 1) * WY] = jnp.concatenate(
            [jnp.broadcast_to(pair[half : half + 1], (4, 128)) for pair in rows for half in range(2)], axis=0
        )
    y = iota(WY, 0) + y_device * 8 - 8
    x = iota(WY, 1)
    for block in range(BLOCKS + 1):
        low, high = max(block - 1, 0), min(block, BLOCKS - 1)
        z_faces[block] = harmonic(
            kappa[8 + low * WY : 8 + (low + 1) * WY], kappa[8 + high * WY : 8 + (high + 1) * WY]
        )
    for block in range(BLOCKS):
        at = 8 + block * WY
        k = kappa[at : at + WY]
        y_low = jnp.where(y == 0, 0.0, harmonic(k, kappa[at - 1 : at - 1 + WY]))
        y_high = jnp.where(y == 63, 0.0, harmonic(k, kappa[at + 1 : at + 1 + WY]))
        x_low = jnp.where(x == 0, 0.0, harmonic(k, pltpu.roll(k, 1, 1)))
        x_high = jnp.where(x == 127, 0.0, harmonic(k, pltpu.roll(k, 127, 1)))
        sides = 1.0 + y_low + y_high + x_low + x_high
        diagonals = (sides + z_faces[block] + k, sides + k + k, sides + k + z_faces[block + 1])
        for number, value in enumerate((k, y_low, y_high, x_low, x_high)):
            coefs[block, number] = value
        for number, value in enumerate(diagonals):
            coefs[block, 5 + number] = 0.8 / value
            coefs[block, 8 + number] = value


def fine_plane(field, source, coefs, z_faces, z, low=0, size=WY):
    block, p = divmod(z, 4)
    rows = slice(low, low + size)
    at = WY + z * WY + low
    here = field[at : at + size]
    k = coefs[block, 0, rows]
    below = z_faces[block, rows] if p == 0 else k
    above = z_faces[block + 1, rows] if p == 3 else k
    total = (
        source[z * WY + low : z * WY + low + size]
        + below * field[at - WY : at - WY + size]
        + above * field[at + WY : at + WY + size]
        + coefs[block, 1, rows] * field[at - 1 : at - 1 + size]
        + coefs[block, 2, rows] * field[at + 1 : at + 1 + size]
        + coefs[block, 3, rows] * pltpu.roll(here, 1, 1)
        + coefs[block, 4, rows] * pltpu.roll(here, 127, 1)
    )
    kind = (0, 1, 1, 2)[p]
    return here, total, coefs[block, 5 + kind, rows], coefs[block, 8 + kind, rows]


def level_one(y_device):
    return Level(20, 16, 1, 2, 128, 16, y_device * 4 - 4, 32, 160)


def build_one(level, kappa, spread, packed, kappa_one, faces):
    for block in range(BLOCKS):
        spread[block * 32 : block * 32 + WY] = kappa[8 + block * WY : 8 + (block + 1) * WY]
        spread[block * 32 + WY : block * 32 + 32] = jnp.ones((32 - WY, 128), jnp.float32)
    packed[...] = 0.5 * spread[pl.ds(0, BLOCKS * 16, stride=2), :]
    level.close(kappa_one, 1.0)
    for block in range(BLOCKS):
        value = packed[block * 16 : block * 16 + 16]
        kappa_one[16 + block * 32 : 32 + block * 32] = value
        kappa_one[32 + block * 32 : 48 + block * 32] = value
    level.build(kappa_one, faces)


def to_chunk(rows):
    group = iota(8, 1) >> 5
    out = rows[0:8]
    for z in range(1, 4):
        out = jnp.where(group == z, rows[8 * z : 8 * z + 8], out)
    return out


def down_body(first, copies, *refs):
    index, refs = refs[0], refs[1:]
    if first:
        sources, refs = refs[:3], refs[3:]
    else:
        fields, (source, coefs, z_faces, faces), refs = refs[:3], refs[3:7], refs[7:]
    chunk, edge, kept, source_one, kept_one = refs[:5]
    refs = refs[5:]
    if first:
        (source, coefs, z_faces, faces), refs = refs[:4], refs[4:]
    va, vb, rs, oa, tmp = refs[:5]
    _, even = parities(index)
    y_device = index[1]
    level = level_one(y_device)
    if first:
        kappa, spread, packed, kappa_one = refs[5:]
        build_fine(sources, even, y_device, kappa, coefs, z_faces)
        build_one(level, kappa, spread, packed, kappa_one, faces)
    zero = jnp.zeros((WY, 128), jnp.float32)
    for ref in (va, vb):
        ref[0:WY] = zero
        ref[(WZ + 1) * WY : (WZ + 2) * WY] = zero
    if first:
        for z in range(WZ):
            kind = (0, 1, 1, 2)[z % 4]
            inside = 0 <= z + HALO - 12 < 16 + 2 * HALO
            value = window(sources, z + HALO - 12, even) if inside else zero
            source[z * WY : (z + 1) * WY] = value
            va[(z + 1) * WY : (z + 2) * WY] = coefs[z // 4, 5 + kind] * value
    else:
        for z in range(1, WZ - 1):
            vb[(z + 1) * WY : (z + 2) * WY] = window(fields, z - 1, even)
        for z in range(2, WZ - 2):
            here, total, weight, _ = fine_plane(vb, source, coefs, z_faces, z)
            va[(z + 1) * WY : (z + 2) * WY] = 0.2 * here + weight * total
    for z in range(3, WZ - 3):
        here, total, weight, _ = fine_plane(va, source, coefs, z_faces, z)
        value = 0.2 * here + weight * total
        vb[(z + 1) * WY : (z + 2) * WY] = value
        if 10 <= z < 30:
            kept[(z - 10) * WY : (z - 9) * WY] = value
    for plane in range(20):
        if 2 <= plane < 18:
            total_defect = 0.0
            for z in (2 * plane, 2 * plane + 1):
                here, total, _, diagonal = fine_plane(vb, source, coefs, z_faces, z)
                total_defect = total_defect + (total - diagonal * here)
            rs[plane * 32 : plane * 32 + WY] = total_defect
            rs[plane * 32 + WY : plane * 32 + 32] = jnp.zeros((32 - WY, 128), jnp.float32)
        else:
            rs[plane * 32 : plane * 32 + 32] = jnp.zeros((32, 128), jnp.float32)
    source_one[...] = coarsen(rs[pl.ds(0, 320, stride=2), :] + rs[pl.ds(1, 320, stride=2), :], 1)
    for ref in (oa, kept_one):
        level.close(ref, 0.0)
    level.start(oa, source_one, faces)
    level.relax(oa, kept_one, source_one, faces)
    level.defect(kept_one, source_one, faces, tmp, 6 * 16, 8 * 16)
    for z in range(4):
        tmp[z * 16 : z * 16 + 16] = tmp[z * 32 : z * 32 + 16] + tmp[z * 32 + 16 : z * 32 + 32]
    halves = tmp[pl.ds(0, 32, stride=2), :] + tmp[pl.ds(1, 32, stride=2), :]
    mean_two = lane_map(lambda r, c: matrix(((r & 1) == 0) & (r >> 2 == (c & 31)), 0.125))
    values = [to_chunk(dot(halves, mean_two))[2:4]]
    if first:
        pick_two = lane_map(lambda r, c: matrix(r == 4 * (c & 31), 0.5))
        values.append(to_chunk(dot(packed[pl.ds(48, 32, stride=2), :], pick_two))[2:4])
    repeats = 4 // len(values)
    tile = jnp.concatenate(values * repeats, axis=0)
    for at in range(0, copies // repeats):
        chunk[at * 8 : at * 8 + 8] = tile
    for plane in range(20):
        edge[plane * 4 : plane * 4 + 4] = kept_one[16 + plane * 16 + 4 : 16 + plane * 16 + 8]


def coarse_levels():
    return (
        Level(SPAN, 16, 4, 1, 32, 16, 0, 16, 160),
        Level(SPAN, 8, 2, 2, 32, 8, 0, 8, 160),
        Level(SPAN, 4, 1, 4, 32, 8, 0, 4, 128),
    )


def coarse_body(first, z_devices, *refs):
    two, three, four = coarse_levels()
    index, same, mate = refs[:3]
    refs = refs[3:]
    if first:
        near, f2, f3, f4 = refs[:4]
    else:
        f2, f3, f4, near = refs[:4]
    a2, b2, g2, r2, a3, b3, g3, r3, a4, b4, g4, cut_same, cut_mate = refs[4:17]
    z_device = index[0]
    even = index[1] % 2 == 0
    per = 4 if first else 2
    rows = 4 * per
    for number in range(SPAN):
        at = lax.rem(z_device + (number - NEAR + 4 * z_devices), z_devices) * rows
        at = pl.multiple_of(at, 8)
        cut_same[number * rows : (number + 1) * rows] = same[pl.ds(at, rows), :]
        cut_mate[number * rows : (number + 1) * rows] = mate[pl.ds(at, rows), :]

    def interleave(target, start, part):
        for y in range(2):
            take = pl.ds(part + y, 4 * SPAN, stride=per)
            one, two_ = cut_same[take, :], cut_mate[take, :]
            target[pl.ds(start + y, 4 * SPAN, stride=4), :] = jnp.where(even, one, two_)
            target[pl.ds(start + 2 + y, 4 * SPAN, stride=4), :] = jnp.where(even, two_, one)

    interleave(g2, 0, 0)
    if first:
        k2, k3, k4 = refs[17:]
        interleave(k2, two.pad, 2)
        two.close(k2, 1.0)
        two.build(k2, f2)
        r2[...] = k2[two.pad : two.pad + two.rows]
        k3[three.pad : three.pad + three.rows] = 0.5 * coarsen(two.pairs(r2), 1, 4)
        three.close(k3, 1.0)
        three.build(k3, f3)
        r3[...] = k3[three.pad : three.pad + three.rows]
        k4[four.pad : four.pad + four.rows] = 0.5 * coarsen(three.pairs(r3), 2, 2)
        four.close(k4, 1.0)
        four.build(k4, f4)
    for level, fields in ((two, (a2, b2)), (three, (a3, b3)), (four, (a4, b4))):
        for field in fields:
            level.close(field, 0.0)

    two.start(a2, g2, f2)
    two.relax(a2, b2, g2, f2)
    two.defect(b2, g2, f2, r2)
    g3[...] = coarsen(two.pairs(r2), 1, 4)
    three.start(a3, g3, f3)
    three.relax(a3, b3, g3, f3)
    three.defect(b3, g3, f3, r3)
    g4[...] = coarsen(three.pairs(r3), 2, 2)
    four.start(a4, g4, f4)
    for _ in range(2):
        four.relax(a4, b4, g4, f4)
        four.relax(b4, a4, g4, f4)
    four.relax(a4, b4, g4, f4)

    def correct(level, field, start, count, value, tmp):
        tmp[pl.ds(0, count // 2, stride=2), :] = value
        tmp[pl.ds(1, count // 2, stride=2), :] = value
        inner = slice(level.pad + start, level.pad + start + count)
        field[inner] = field[inner] + tmp[0:count]

    low = NEAR - 3
    correct(three, b3, 8 * low, 48, b4[four.pad + 4 * low : four.pad + 4 * low + 24], r3)
    three.relax(b3, a3, g3, f3, 8 * low, 48)
    low = NEAR - 1
    three.relax(a3, b3, g3, f3, 8 * low, 24)
    correct(two, b2, 16 * low, 48, b3[three.pad + 8 * low : three.pad + 8 * low + 24], r2)
    two.relax(b2, a2, g2, f2, 16 * low, 48)
    two.relax(a2, b2, g2, f2, 16 * low, 48)
    near[...] = b2[two.pad + 16 * low : two.pad + 16 * low + 48]


def up_body(last, *refs):
    index, source, coefs, z_faces, faces, near, edge_mate, edge_other, kept, source_one, kept_one, out = refs[:12]
    refs = refs[12:]
    if last:
        out_hbm, (out, sems), refs = out, refs[-2:], refs[:-2]
        halves = (slice(0, 8), slice(8, 16))
        copies = [
            pltpu.make_async_copy(out.at[half], out_hbm.at[half], sems.at[i]) for i, half in enumerate(halves)
        ]
    else:
        (mate, other), refs = refs[:2], refs[2:]
    va, vb, spread, oa, ob = refs
    even_z, even = parities(index)
    y_device = index[1]
    level = level_one(y_device)
    rows = matrix(iota(16, 1, 16) == y_device * 2 - 2 + (iota(16, 0, 16) >> 1), 1.0)
    spread_y = jnp.concatenate([dot(rows, near[16 * part : 16 * part + 16]) for part in range(3)], axis=0)
    by_z = [
        dot(spread_y, lane_map(lambda r, c, z=z: matrix(r == z * 32 + (c >> 2), 1.0))) for z in range(4)
    ]
    for plane in range(20):
        part, z = divmod(plane // 2 + 1, 4)
        at = 16 + plane * 16
        one, two = edge_mate[plane * 4 : plane * 4 + 4], edge_other[plane * 4 : plane * 4 + 4]
        field = jnp.concatenate(
            [jnp.where(even, two, one), kept_one[at + 4 : at + 8], jnp.where(even, one, two),
             jnp.zeros((4, 128), jnp.float32)], axis=0
        )
        oa[at : at + 16] = field + by_z[z][16 * part : 16 * part + 16]
    level.relax(oa, ob, source_one, faces, 4 * 16, 12 * 16)
    level.relax(ob, oa, source_one, faces, 5 * 16, 10 * 16)
    value = oa[16 + 80 : 16 + 240]
    spread[pl.ds(0, 160, stride=2), :] = value
    spread[pl.ds(1, 160, stride=2), :] = value
    for z in range(10, 30):
        at = ((z - 10) // 2) * 32
        va[(z + 1) * WY : (z + 2) * WY] = kept[(z - 10) * WY : (z - 9) * WY] + spread[at : at + WY]
    for z in range(11, 29):
        here, total, weight, _ = fine_plane(va, source, coefs, z_faces, z)
        vb[(z + 1) * WY : (z + 2) * WY] = 0.2 * here + weight * total
    for z in range(12, 28):
        here, total, weight, _ = fine_plane(vb, source, coefs, z_faces, z, 8, 8)
        out[z - 12] = 0.2 * here + weight * total
        if last and z in (19, 27):
            copies[z // 27].start()
    if last:
        for copy in copies:
            copy.wait()
    else:
        top = 16 - FIELD_HALO
        mate[...] = out[pl.ds(jnp.where(even_z, top, 0), FIELD_HALO)]
        other[...] = out[pl.ds(jnp.where(even_z, 0, top), FIELD_HALO)]


def floats(*shape):
    return jax.ShapeDtypeStruct(shape, jnp.float32)


def call(body, outs, scratch, args, inputs=pltpu.VMEM, outputs=pltpu.VMEM):
    return pl.pallas_call(
        body,
        out_shape=outs,
        in_specs=[pl.BlockSpec(memory_space=pltpu.SMEM)] + [pl.BlockSpec(memory_space=inputs)] * (len(args) - 1),
        out_specs=[pl.BlockSpec(memory_space=outputs)] * len(outs),
        scratch_shapes=[pltpu.VMEM(s, jnp.float32) if isinstance(s, tuple) else s for s in scratch],
        compiler_params=pltpu.CompilerParams(vmem_limit_bytes=VMEM_BYTES),
    )(*args)


FIELD = ((WZ + 2) * WY, 128)
SHARED = [(WZ * WY, 128), (BLOCKS, 11, WY, 128), (BLOCKS + 1, WY, 128), (6, 352, 128)]
Z_AXIS = ("gz",)
Y_AXIS = ("gx", "core")


def down(index, arrays, shared):
    first = shared is None
    copies = lax.axis_size("gz") * lax.axis_size("gx")
    outs = [
        floats(copies * (4 if first else 2), 128),
        floats(80, 128),
        floats(20 * WY, 128),
        floats(320, 128),
        floats(352, 128),
    ]
    scratch = [FIELD, FIELD, (640, 128), (352, 128), (128, 128)]
    if first:
        outs += [floats(*shape) for shape in SHARED]
        scratch += [(16 + BLOCKS * WY, 128), (320, 128), (160, 128), (352, 128)]
        args = [index, *arrays]
    else:
        args = [index, *arrays, *shared]
    result = call(lambda *refs: down_body(first, copies, *refs), outs, scratch, args)
    return result[0], result[1], result[2:5], result[5:] if first else shared


def coarse(index, gathered, faces):
    first = faces is None
    z_devices = lax.axis_size("gz")
    levels = coarse_levels()
    outs, scratch = [floats(48, 128)], []
    if first:
        outs += [floats(6, *level.shape()) for level in levels]
    for level in levels:
        scratch += [level.shape(), level.shape(), (level.rows, 128), (level.rows, 128)]
    cut = (SPAN * (16 if first else 8), 128)
    scratch = scratch[:11] + [cut, cut]
    if first:
        scratch += [level.shape() for level in levels]
    args = [index, *gathered] + ([] if first else list(faces))
    near, *new = call(lambda *refs: coarse_body(first, z_devices, *refs), outs, scratch, args)
    return near, new if first else faces


def up(index, shared, near, edges, kept, last):
    outs = [floats(16, 8, 128)] + ([] if last else [floats(FIELD_HALO, 8, 128)] * 2)
    scratch = [FIELD, FIELD, (320, 128), (352, 128), (352, 128)]
    if last:
        scratch += [(16, 8, 128), pltpu.SemaphoreType.DMA((2,))]
    args = [index, *shared, near, *edges, *kept]
    return call(
        lambda *refs: up_body(last, *refs), outs, scratch, args, outputs=pltpu.HBM if last else pltpu.VMEM
    )


def mate_of(i):
    return i + 1 if i % 2 == 0 else i - 1


def other_of(i):
    return i - 1 if i % 2 == 0 else i + 1


def swap(array, axis, partner):
    count = 1
    for name in axis:
        count *= lax.axis_size(name)
    return lax.ppermute(array, axis, [(i, partner(i) % count) for i in range(count)])


def swaps(mate, other, axis):
    far = swap(other, axis, other_of)
    return swap(mate, axis, mate_of), far


def to_all(copies):
    peers = lax.axis_size("gz") * lax.axis_size("gx")
    copies = copies.reshape(peers, copies.shape[0] // peers, 128)
    out = lax.all_to_all(copies, ("gz", "gx"), 0, 0)
    out = out.reshape(out.shape[0] * out.shape[1], 128)
    return out, swap(out, Y_AXIS, mate_of)


def stack(index, parts, own, halo):
    even = index[0] % 2 == 0
    mate, other = parts
    before, after = jnp.where(even, other, mate), jnp.where(even, mate, other)
    pieces = [before[:halo], own[0], after[:halo]]
    if len(own) > 1:
        pieces += [before[halo:], own[1], after[halo:]]
    return jnp.concatenate(pieces, axis=0)


def cycle(index, arrays, shared, coarse_faces, last):
    copies, edge, kept, shared = down(index, arrays, shared)
    edges = swaps(edge, edge, Y_AXIS)
    gathered = to_all(copies)
    near, coarse_faces = coarse(index, gathered, coarse_faces)
    return up(index, shared, near, edges, kept, last), shared, coarse_faces


def per_device(concentration, phases, grains, grain_class, diffusivity):
    y_device = lax.axis_index("gx") * lax.axis_size("core") + lax.axis_index("core")
    index = jnp.stack([lax.axis_index("gz"), y_device]).astype(jnp.int32)
    plane = (4,) + phases.shape[1:]
    part = floats(HALO + 1, 8, 128)
    kappa, block, *parts = call(
        kappa_body,
        [floats(1, 8, 128), floats(*phases.shape), part, part],
        [
            pltpu.SMEM(grain_class.shape, jnp.int32),
            pltpu.SMEM(diffusivity.shape, jnp.float32),
            pltpu.VMEM(plane, jnp.int32),
            pltpu.VMEM(plane, jnp.int32),
            pltpu.SemaphoreType.DMA((13,)),
        ],
        [index] + [
            pltpu.with_memory_space_constraint(array, pltpu.HBM)
            for array in (grain_class, diffusivity, phases, grains, concentration)
        ],
        pltpu.HBM,
    )
    own = stack(index, swaps(*parts, Z_AXIS), (block, kappa), HALO)
    mate, other = swaps(own, own, Y_AXIS)
    (field, *parts), shared, faces = cycle(index, (mate, own, other), None, None, False)

    own = stack(index, swaps(*parts, Z_AXIS), (field,), FIELD_HALO)
    mate, other = swaps(own, own, Y_AXIS)
    return cycle(index, (mate, own, other), shared, faces, True)[0][0]


def solution(mesh):
    z_devices, y_devices = mesh.shape["gz"], mesh.shape["gy"]
    cores = jax.sharding.Mesh(mesh.devices.reshape(z_devices, y_devices // 2, 2), ("gz", "gx", "core"))
    split = P("gz", ("gx", "core"), None)
    return jax.shard_map(
        per_device, mesh=cores, in_specs=(split, split, split, P(), P()), out_specs=split, check_vma=False
    )
```

```python
import jax
import jax.numpy as jnp
from jax import lax
from jax.experimental import pallas as pl
from jax.experimental.pallas import tpu as pltpu
from jax.sharding import PartitionSpec as P

HALO = 10
FIELD_HALO = 11
WZ = 40
BLOCKS = 10
WY = 24
NEAR = 9
SPAN = 20
VMEM_BYTES = 48 * 1024 * 1024


def harmonic(near_k, far_k):
    return 2.0 * near_k * far_k / (near_k + far_k)


def dot(left, right):
    return jnp.dot(left, right, precision=lax.Precision.HIGHEST, preferred_element_type=jnp.float32)


def iota(rows, dim, lanes=128):
    return lax.broadcasted_iota(jnp.int32, (rows, lanes), dim)


def matrix(condition, value):
    return jnp.where(condition, jnp.float32(value), jnp.float32(0.0))


def lane_map(make):
    return make(iota(128, 0), iota(128, 1))


class Level:
    def __init__(self, planes, ny, zl, step, span, pad, y_start, y_total, chunk):
        self.planes, self.ny, self.zl, self.step, self.span, self.pad = planes, ny, zl, step, span, pad
        self.y_start, self.y_total = y_start, y_total
        self.rows = planes * ny
        self.chunk = min(chunk, self.rows)

    def chunks(self, start=0, count=None):
        count = self.rows if count is None else count
        at = start
        while at < start + count:
            size = min(self.chunk, start + count - at)
            yield at, size
            at += size

    def neighbours(self, ref, at, size):
        base = self.pad + at
        here = ref[base : base + size]
        below = ref[base - self.ny : base - self.ny + size]
        above = ref[base + self.ny : base + self.ny + size]
        if self.zl > 1:
            width = 128 // self.zl
            lane = iota(size, 1)
            below = pltpu.roll(jnp.where(lane >= 128 - width, below, here), width, 1)
            above = pltpu.roll(jnp.where(lane < width, above, here), 128 - width, 1)
        return (
            here,
            (
                below,
                above,
                ref[base - 1 : base - 1 + size],
                ref[base + 1 : base + 1 + size],
                pltpu.roll(here, self.step, 1),
            ),
        )

    def close(self, ref, value):
        edge = jnp.full((self.pad, 128), value, jnp.float32)
        ref[0 : self.pad] = edge
        ref[self.pad + self.rows : 2 * self.pad + self.rows] = edge

    def shape(self):
        return (self.rows + 2 * self.pad, 128)

    def build(self, kappa, faces):
        for number in (0, 2):
            self.close(faces.at[number], 0.0)
        for at, size in self.chunks():
            here, around = self.neighbours(kappa, at, size)
            y = (iota(size, 0) & (self.ny - 1)) + self.y_start
            x = iota(size, 1) & (self.span - 1)
            rows = slice(self.pad + at, self.pad + at + size)
            faces[0, rows] = harmonic(here, around[0])
            faces[2, rows] = jnp.where((y != 0) & (y != self.y_total), harmonic(here, around[2]), 0.0)
            faces[3, rows] = jnp.where(x >= self.step, harmonic(here, around[4]), 0.0)
        for at, size in self.chunks():
            rows = slice(self.pad + at, self.pad + at + size)
            z_low, around = self.neighbours(faces.at[0], at, size)
            z_high = around[1]
            y_high = faces[2, self.pad + at + 1 : self.pad + at + 1 + size]
            x_low = faces[3, rows]
            total = 1.0 + z_low + z_high + faces[2, rows] + y_high + x_low + pltpu.roll(x_low, 128 - self.step, 1)
            faces[1, rows] = z_high
            faces[4, rows] = 0.8 / total
            faces[5, rows] = total

    def coupled(self, field, source, faces, at, size):
        here, around = self.neighbours(field, at, size)
        rows = slice(self.pad + at, self.pad + at + size)
        next_rows = slice(self.pad + at + 1, self.pad + at + 1 + size)
        x_low = faces[3, rows]
        total = (
            source[at : at + size]
            + faces[0, rows] * around[0]
            + faces[1, rows] * around[1]
            + faces[2, rows] * around[2]
            + faces[2, next_rows] * around[3]
            + x_low * around[4]
            + pltpu.roll(x_low * here, 128 - self.step, 1)
        )
        return here, total

    def start(self, field, source, faces):
        for at, size in self.chunks():
            rows = slice(self.pad + at, self.pad + at + size)
            field[rows] = faces[4, rows] * source[at : at + size]

    def relax(self, field, target, source, faces, start=0, count=None):
        for at, size in self.chunks(start, count):
            here, total = self.coupled(field, source, faces, at, size)
            rows = slice(self.pad + at, self.pad + at + size)
            target[rows] = 0.2 * here + faces[4, rows] * total

    def defect(self, field, source, faces, out, start=0, count=None):
        for at, size in self.chunks(start, count):
            here, total = self.coupled(field, source, faces, at, size)
            diagonal = faces[5, self.pad + at : self.pad + at + size]
            out[at - start : at - start + size] = total - diagonal * here

    def pairs(self, ref):
        half = self.rows // 2
        return ref[pl.ds(0, half, stride=2), :] + ref[pl.ds(1, half, stride=2), :]


def coarsen(value, step, zl=1):
    lane = iota(value.shape[0], 1)
    value = value + jnp.where((lane & step) == 0, pltpu.roll(value, 128 - step, 1), pltpu.roll(value, step, 1))
    if zl == 4:
        value = value + jnp.where((lane & 32) == 0, pltpu.roll(value, 96, 1), pltpu.roll(value, 32, 1))
    if zl == 2:
        value = value + pltpu.roll(value, 64, 1)
    return 0.125 * value


def parities(index):
    return index[0] % 2 == 0, index[1] % 2 == 0


def kappa_body(index, class_hbm, diff_hbm, phases_hbm, grains_hbm, conc_hbm, kappa_ref, own_ref, mate_ref, other_ref, classes, diff, phases, grains, sems):
    even, _ = parities(index)
    num_phases, num_classes = diff.shape
    pairs = [(class_hbm, classes), (diff_hbm, diff)]
    for block in range(4):
        pairs += [(phases_hbm.at[4 * block], phases.at[block]), (grains_hbm.at[4 * block], grains.at[block])]
    top = 16 - HALO
    pairs += [
        (conc_hbm.at[pl.ds(jnp.where(even, top, 0), HALO)], mate_ref.at[0:HALO]),
        (conc_hbm.at[pl.ds(jnp.where(even, 0, top), HALO)], other_ref.at[0:HALO]),
        (conc_hbm, own_ref),
    ]
    copies = [pltpu.make_async_copy(source, target, sems.at[i]) for i, (source, target) in enumerate(pairs)]
    for copy in copies:
        copy.start()
    for copy in copies[:-3]:
        copy.wait()
    grain = grains[...]
    phase = phases[...]
    cls = jnp.zeros(grain.shape, jnp.int32)
    for number in range(classes.shape[0]):
        cls = jnp.where(grain == number, classes[number], cls)
    value = jnp.ones(grain.shape, jnp.float32)
    for p in range(num_phases):
        for c in range(num_classes):
            value = jnp.where((phase == p) & (cls == c), diff[p, c], value)
    rows = jnp.concatenate([value[block, 4 * half : 4 * half + 1] for block in range(4) for half in range(2)], axis=0)
    kappa_ref[0] = rows
    mate_ref[HALO] = rows
    other_ref[HALO] = rows
    for copy in copies[-3:]:
        copy.wait()


def window(refs, plane, even):
    mate, own, other = (ref[plane] for ref in refs)
    return jnp.concatenate([jnp.where(even, other, mate), own, jnp.where(even, mate, other)], axis=0)


def build_fine(sources, even, y_device, kappa, coefs, z_faces):
    kappa[0:8] = jnp.ones((8, 128), jnp.float32)
    kappa[8 + BLOCKS * WY : 16 + BLOCKS * WY] = jnp.ones((8, 128), jnp.float32)
    for block in range(BLOCKS):
        plane, number = divmod(block + 1, 4)
        two = slice(2 * number, 2 * number + 2)
        mate, own, other = (ref[16 + 2 * HALO + plane, two] for ref in sources)
        rows = (jnp.where(even, other, mate), own, jnp.where(even, mate, other))
        kappa[8 + block * WY : 8 + (block + 1) * WY] = jnp.concatenate(
            [jnp.broadcast_to(pair[half : half + 1], (4, 128)) for pair in rows for half in range(2)], axis=0
        )
    y = iota(WY, 0) + y_device * 8 - 8
    x = iota(WY, 1)
    for block in range(BLOCKS + 1):
        low, high = max(block - 1, 0), min(block, BLOCKS - 1)
        z_faces[block] = harmonic(
            kappa[8 + low * WY : 8 + (low + 1) * WY], kappa[8 + high * WY : 8 + (high + 1) * WY]
        )
    for block in range(BLOCKS):
        at = 8 + block * WY
        k = kappa[at : at + WY]
        y_low = jnp.where(y == 0, 0.0, harmonic(k, kappa[at - 1 : at - 1 + WY]))
        y_high = jnp.where(y == 63, 0.0, harmonic(k, kappa[at + 1 : at + 1 + WY]))
        x_low = jnp.where(x == 0, 0.0, harmonic(k, pltpu.roll(k, 1, 1)))
        x_high = jnp.where(x == 127, 0.0, harmonic(k, pltpu.roll(k, 127, 1)))
        sides = 1.0 + y_low + y_high + x_low + x_high
        diagonals = (sides + z_faces[block] + k, sides + k + k, sides + k + z_faces[block + 1])
        for number, value in enumerate((k, y_low, y_high, x_low, x_high)):
            coefs[block, number] = value
        for number, value in enumerate(diagonals):
            coefs[block, 5 + number] = 0.8 / value
            coefs[block, 8 + number] = value


def fine_plane(field, source, coefs, z_faces, z, low=0, size=WY):
    block, p = divmod(z, 4)
    rows = slice(low, low + size)
    at = WY + z * WY + low
    here = field[at : at + size]
    k = coefs[block, 0, rows]
    below = z_faces[block, rows] if p == 0 else k
    above = z_faces[block + 1, rows] if p == 3 else k
    total = (
        source[z * WY + low : z * WY + low + size]
        + below * field[at - WY : at - WY + size]
        + above * field[at + WY : at + WY + size]
        + coefs[block, 1, rows] * field[at - 1 : at - 1 + size]
        + coefs[block, 2, rows] * field[at + 1 : at + 1 + size]
        + coefs[block, 3, rows] * pltpu.roll(here, 1, 1)
        + coefs[block, 4, rows] * pltpu.roll(here, 127, 1)
    )
    kind = (0, 1, 1, 2)[p]
    return here, total, coefs[block, 5 + kind, rows], coefs[block, 8 + kind, rows]


def level_one(y_device):
    return Level(20, 16, 1, 2, 128, 16, y_device * 4 - 4, 32, 160)


def build_one(level, kappa, spread, packed, kappa_one, faces):
    for block in range(BLOCKS):
        spread[block * 32 : block * 32 + WY] = kappa[8 + block * WY : 8 + (block + 1) * WY]
        spread[block * 32 + WY : block * 32 + 32] = jnp.ones((32 - WY, 128), jnp.float32)
    packed[...] = 0.5 * spread[pl.ds(0, BLOCKS * 16, stride=2), :]
    level.close(kappa_one, 1.0)
    for block in range(BLOCKS):
        value = packed[block * 16 : block * 16 + 16]
        kappa_one[16 + block * 32 : 32 + block * 32] = value
        kappa_one[32 + block * 32 : 48 + block * 32] = value
    level.build(kappa_one, faces)


def to_chunk(rows):
    group = iota(8, 1) >> 5
    out = rows[0:8]
    for z in range(1, 4):
        out = jnp.where(group == z, rows[8 * z : 8 * z + 8], out)
    return out


def down_body(first, copies, *refs):
    index, refs = refs[0], refs[1:]
    if first:
        sources, refs = refs[:3], refs[3:]
    else:
        fields, (source, coefs, z_faces, faces), refs = refs[:3], refs[3:7], refs[7:]
    chunk, edge, kept, source_one, kept_one = refs[:5]
    refs = refs[5:]
    if first:
        (source, coefs, z_faces, faces), refs = refs[:4], refs[4:]
    va, vb, rs, oa, tmp = refs[:5]
    _, even = parities(index)
    y_device = index[1]
    level = level_one(y_device)
    if first:
        kappa, spread, packed, kappa_one = refs[5:]
        build_fine(sources, even, y_device, kappa, coefs, z_faces)
        build_one(level, kappa, spread, packed, kappa_one, faces)
    zero = jnp.zeros((WY, 128), jnp.float32)
    for ref in (va, vb):
        ref[0:WY] = zero
        ref[(WZ + 1) * WY : (WZ + 2) * WY] = zero
    if first:
        for z in range(WZ):
            kind = (0, 1, 1, 2)[z % 4]
            inside = 0 <= z + HALO - 12 < 16 + 2 * HALO
            value = window(sources, z + HALO - 12, even) if inside else zero
            source[z * WY : (z + 1) * WY] = value
            va[(z + 1) * WY : (z + 2) * WY] = coefs[z // 4, 5 + kind] * value
    else:
        for z in range(1, WZ - 1):
            vb[(z + 1) * WY : (z + 2) * WY] = window(fields, z - 1, even)
        for z in range(2, WZ - 2):
            here, total, weight, _ = fine_plane(vb, source, coefs, z_faces, z)
            va[(z + 1) * WY : (z + 2) * WY] = 0.2 * here + weight * total
    for z in range(3, WZ - 3):
        here, total, weight, _ = fine_plane(va, source, coefs, z_faces, z)
        value = 0.2 * here + weight * total
        vb[(z + 1) * WY : (z + 2) * WY] = value
        if 10 <= z < 30:
            kept[(z - 10) * WY : (z - 9) * WY] = value
    for plane in range(20):
        if 2 <= plane < 18:
            total_defect = 0.0
            for z in (2 * plane, 2 * plane + 1):
                here, total, _, diagonal = fine_plane(vb, source, coefs, z_faces, z)
                total_defect = total_defect + (total - diagonal * here)
            rs[plane * 32 : plane * 32 + WY] = total_defect
            rs[plane * 32 + WY : plane * 32 + 32] = jnp.zeros((32 - WY, 128), jnp.float32)
        else:
            rs[plane * 32 : plane * 32 + 32] = jnp.zeros((32, 128), jnp.float32)
    source_one[...] = coarsen(rs[pl.ds(0, 320, stride=2), :] + rs[pl.ds(1, 320, stride=2), :], 1)
    for ref in (oa, kept_one):
        level.close(ref, 0.0)
    level.start(oa, source_one, faces)
    level.relax(oa, kept_one, source_one, faces)
    level.defect(kept_one, source_one, faces, tmp, 6 * 16, 8 * 16)
    for z in range(4):
        tmp[z * 16 : z * 16 + 16] = tmp[z * 32 : z * 32 + 16] + tmp[z * 32 + 16 : z * 32 + 32]
    halves = tmp[pl.ds(0, 32, stride=2), :] + tmp[pl.ds(1, 32, stride=2), :]
    mean_two = lane_map(lambda r, c: matrix(((r & 1) == 0) & (r >> 2 == (c & 31)), 0.125))
    values = [to_chunk(dot(halves, mean_two))[2:4]]
    if first:
        pick_two = lane_map(lambda r, c: matrix(r == 4 * (c & 31), 0.5))
        values.append(to_chunk(dot(packed[pl.ds(48, 32, stride=2), :], pick_two))[2:4])
    repeats = 4 // len(values)
    tile = jnp.concatenate(values * repeats, axis=0)
    for at in range(0, copies // repeats):
        chunk[at * 8 : at * 8 + 8] = tile
    for plane in range(20):
        edge[plane * 4 : plane * 4 + 4] = kept_one[16 + plane * 16 + 4 : 16 + plane * 16 + 8]


def coarse_levels():
    return (
        Level(SPAN, 16, 4, 1, 32, 16, 0, 16, 160),
        Level(SPAN, 8, 2, 2, 32, 8, 0, 8, 160),
        Level(SPAN, 4, 1, 4, 32, 8, 0, 4, 128),
    )


def coarse_body(first, z_devices, *refs):
    two, three, four = coarse_levels()
    index, same, mate = refs[:3]
    refs = refs[3:]
    if first:
        near, f2, f3, f4 = refs[:4]
    else:
        f2, f3, f4, near = refs[:4]
    a2, b2, g2, r2, a3, b3, g3, r3, a4, b4, g4, cut_same, cut_mate = refs[4:17]
    z_device = index[0]
    even = index[1] % 2 == 0
    per = 4 if first else 2
    rows = 4 * per
    for number in range(SPAN):
        at = lax.rem(z_device + (number - NEAR + 4 * z_devices), z_devices) * rows
        at = pl.multiple_of(at, 8)
        cut_same[number * rows : (number + 1) * rows] = same[pl.ds(at, rows), :]
        cut_mate[number * rows : (number + 1) * rows] = mate[pl.ds(at, rows), :]

    def interleave(target, start, part):
        for y in range(2):
            take = pl.ds(part + y, 4 * SPAN, stride=per)
            one, two_ = cut_same[take, :], cut_mate[take, :]
            target[pl.ds(start + y, 4 * SPAN, stride=4), :] = jnp.where(even, one, two_)
            target[pl.ds(start + 2 + y, 4 * SPAN, stride=4), :] = jnp.where(even, two_, one)

    interleave(g2, 0, 0)
    if first:
        k2, k3, k4 = refs[17:]
        interleave(k2, two.pad, 2)
        two.close(k2, 1.0)
        two.build(k2, f2)
        r2[...] = k2[two.pad : two.pad + two.rows]
        k3[three.pad : three.pad + three.rows] = 0.5 * coarsen(two.pairs(r2), 1, 4)
        three.close(k3, 1.0)
        three.build(k3, f3)
        r3[...] = k3[three.pad : three.pad + three.rows]
        k4[four.pad : four.pad + four.rows] = 0.5 * coarsen(three.pairs(r3), 2, 2)
        four.close(k4, 1.0)
        four.build(k4, f4)
    for level, fields in ((two, (a2, b2)), (three, (a3, b3)), (four, (a4, b4))):
        for field in fields:
            level.close(field, 0.0)

    two.start(a2, g2, f2)
    two.relax(a2, b2, g2, f2)
    two.defect(b2, g2, f2, r2)
    g3[...] = coarsen(two.pairs(r2), 1, 4)
    three.start(a3, g3, f3)
    three.relax(a3, b3, g3, f3)
    three.defect(b3, g3, f3, r3)
    g4[...] = coarsen(three.pairs(r3), 2, 2)
    four.start(a4, g4, f4)
    for _ in range(2):
        four.relax(a4, b4, g4, f4)
        four.relax(b4, a4, g4, f4)
    four.relax(a4, b4, g4, f4)

    def correct(level, field, start, count, value, tmp):
        tmp[pl.ds(0, count // 2, stride=2), :] = value
        tmp[pl.ds(1, count // 2, stride=2), :] = value
        inner = slice(level.pad + start, level.pad + start + count)
        field[inner] = field[inner] + tmp[0:count]

    low = NEAR - 3
    correct(three, b3, 8 * low, 48, b4[four.pad + 4 * low : four.pad + 4 * low + 24], r3)
    three.relax(b3, a3, g3, f3, 8 * low, 48)
    low = NEAR - 1
    three.relax(a3, b3, g3, f3, 8 * low, 24)
    correct(two, b2, 16 * low, 48, b3[three.pad + 8 * low : three.pad + 8 * low + 24], r2)
    two.relax(b2, a2, g2, f2, 16 * low, 48)
    two.relax(a2, b2, g2, f2, 16 * low, 48)
    near[...] = b2[two.pad + 16 * low : two.pad + 16 * low + 48]


def up_body(last, *refs):
    index, source, coefs, z_faces, faces, near, edge_mate, edge_other, kept, source_one, kept_one, out = refs[:12]
    refs = refs[12:]
    if last:
        out_hbm, (out, sems), refs = out, refs[-2:], refs[:-2]
        halves = (slice(0, 8), slice(8, 16))
        copies = [
            pltpu.make_async_copy(out.at[half], out_hbm.at[half], sems.at[i]) for i, half in enumerate(halves)
        ]
    else:
        (mate, other), refs = refs[:2], refs[2:]
    va, vb, spread, oa, ob = refs
    even_z, even = parities(index)
    y_device = index[1]
    level = level_one(y_device)
    rows = matrix(iota(16, 1, 16) == y_device * 2 - 2 + (iota(16, 0, 16) >> 1), 1.0)
    spread_y = jnp.concatenate([dot(rows, near[16 * part : 16 * part + 16]) for part in range(3)], axis=0)
    by_z = [
        dot(spread_y, lane_map(lambda r, c, z=z: matrix(r == z * 32 + (c >> 2), 1.0))) for z in range(4)
    ]
    for plane in range(20):
        part, z = divmod(plane // 2 + 1, 4)
        at = 16 + plane * 16
        one, two = edge_mate[plane * 4 : plane * 4 + 4], edge_other[plane * 4 : plane * 4 + 4]
        field = jnp.concatenate(
            [jnp.where(even, two, one), kept_one[at + 4 : at + 8], jnp.where(even, one, two),
             jnp.zeros((4, 128), jnp.float32)], axis=0
        )
        oa[at : at + 16] = field + by_z[z][16 * part : 16 * part + 16]
    level.relax(oa, ob, source_one, faces, 4 * 16, 12 * 16)
    level.relax(ob, oa, source_one, faces, 5 * 16, 10 * 16)
    value = oa[16 + 80 : 16 + 240]
    spread[pl.ds(0, 160, stride=2), :] = value
    spread[pl.ds(1, 160, stride=2), :] = value
    for z in range(10, 30):
        at = ((z - 10) // 2) * 32
        va[(z + 1) * WY : (z + 2) * WY] = kept[(z - 10) * WY : (z - 9) * WY] + spread[at : at + WY]
    for z in range(11, 29):
        here, total, weight, _ = fine_plane(va, source, coefs, z_faces, z)
        vb[(z + 1) * WY : (z + 2) * WY] = 0.2 * here + weight * total
    for z in range(12, 28):
        here, total, weight, _ = fine_plane(vb, source, coefs, z_faces, z, 8, 8)
        out[z - 12] = 0.2 * here + weight * total
        if last and z in (19, 27):
            copies[z // 27].start()
    if last:
        for copy in copies:
            copy.wait()
    else:
        top = 16 - FIELD_HALO
        mate[...] = out[pl.ds(jnp.where(even_z, top, 0), FIELD_HALO)]
        other[...] = out[pl.ds(jnp.where(even_z, 0, top), FIELD_HALO)]


def floats(*shape):
    return jax.ShapeDtypeStruct(shape, jnp.float32)


def call(body, outs, scratch, args, inputs=pltpu.VMEM, outputs=pltpu.VMEM):
    return pl.pallas_call(
        body,
        out_shape=outs,
        in_specs=[pl.BlockSpec(memory_space=pltpu.SMEM)] + [pl.BlockSpec(memory_space=inputs)] * (len(args) - 1),
        out_specs=[pl.BlockSpec(memory_space=outputs)] * len(outs),
        scratch_shapes=[pltpu.VMEM(s, jnp.float32) if isinstance(s, tuple) else s for s in scratch],
        compiler_params=pltpu.CompilerParams(vmem_limit_bytes=VMEM_BYTES),
    )(*args)


FIELD = ((WZ + 2) * WY, 128)
SHARED = [(WZ * WY, 128), (BLOCKS, 11, WY, 128), (BLOCKS + 1, WY, 128), (6, 352, 128)]
Z_AXIS = ("gz",)
Y_AXIS = ("gx", "core")


def down(index, arrays, shared):
    first = shared is None
    copies = lax.axis_size("gz") * lax.axis_size("gx")
    outs = [
        floats(copies * (4 if first else 2), 128),
        floats(80, 128),
        floats(20 * WY, 128),
        floats(320, 128),
        floats(352, 128),
    ]
    scratch = [FIELD, FIELD, (640, 128), (352, 128), (128, 128)]
    if first:
        outs += [floats(*shape) for shape in SHARED]
        scratch += [(16 + BLOCKS * WY, 128), (320, 128), (160, 128), (352, 128)]
        args = [index, *arrays]
    else:
        args = [index, *arrays, *shared]
    result = call(lambda *refs: down_body(first, copies, *refs), outs, scratch, args)
    return result[0], result[1], result[2:5], result[5:] if first else shared


def coarse(index, gathered, faces):
    first = faces is None
    z_devices = lax.axis_size("gz")
    levels = coarse_levels()
    outs, scratch = [floats(48, 128)], []
    if first:
        outs += [floats(6, *level.shape()) for level in levels]
    for level in levels:
        scratch += [level.shape(), level.shape(), (level.rows, 128), (level.rows, 128)]
    cut = (SPAN * (16 if first else 8), 128)
    scratch = scratch[:11] + [cut, cut]
    if first:
        scratch += [level.shape() for level in levels]
    args = [index, *gathered] + ([] if first else list(faces))
    near, *new = call(lambda *refs: coarse_body(first, z_devices, *refs), outs, scratch, args)
    return near, new if first else faces


def up(index, shared, near, edges, kept, last):
    outs = [floats(16, 8, 128)] + ([] if last else [floats(FIELD_HALO, 8, 128)] * 2)
    scratch = [FIELD, FIELD, (320, 128), (352, 128), (352, 128)]
    if last:
        scratch += [(16, 8, 128), pltpu.SemaphoreType.DMA((2,))]
    args = [index, *shared, near, *edges, *kept]
    return call(
        lambda *refs: up_body(last, *refs), outs, scratch, args, outputs=pltpu.HBM if last else pltpu.VMEM
    )


def mate_of(i):
    return i + 1 if i % 2 == 0 else i - 1


def other_of(i):
    return i - 1 if i % 2 == 0 else i + 1


def swap(array, axis, partner):
    count = 1
    for name in axis:
        count *= lax.axis_size(name)
    pairs = [(i, partner(i)) for i in range(count)]
    if axis == Y_AXIS:
        pairs = [(i, j if 0 <= j < count else i) for i, j in pairs]
    return lax.ppermute(array, axis, [(i, j % count) for i, j in pairs])


def swaps(mate, other, axis):
    far = swap(other, axis, other_of)
    return swap(mate, axis, mate_of), far


def to_all(copies):
    peers = lax.axis_size("gz") * lax.axis_size("gx")
    copies = copies.reshape(peers, copies.shape[0] // peers, 128)
    out = lax.all_to_all(copies, ("gz", "gx"), 0, 0)
    out = out.reshape(out.shape[0] * out.shape[1], 128)
    return out, swap(out, Y_AXIS, mate_of)


def stack(index, parts, own, halo):
    even = index[0] % 2 == 0
    mate, other = parts
    before, after = jnp.where(even, other, mate), jnp.where(even, mate, other)
    pieces = [before[:halo], own[0], after[:halo]]
    if len(own) > 1:
        pieces += [before[halo:], own[1], after[halo:]]
    return jnp.concatenate(pieces, axis=0)


def cycle(index, arrays, shared, coarse_faces, last):
    copies, edge, kept, shared = down(index, arrays, shared)
    edges = swaps(edge, edge, Y_AXIS)
    gathered = to_all(copies)
    near, coarse_faces = coarse(index, gathered, coarse_faces)
    return up(index, shared, near, edges, kept, last), shared, coarse_faces


def per_device(concentration, phases, grains, grain_class, diffusivity):
    y_device = lax.axis_index("gx") * lax.axis_size("core") + lax.axis_index("core")
    index = jnp.stack([lax.axis_index("gz"), y_device]).astype(jnp.int32)
    plane = (4,) + phases.shape[1:]
    part = floats(HALO + 1, 8, 128)
    kappa, block, *parts = call(
        kappa_body,
        [floats(1, 8, 128), floats(*phases.shape), part, part],
        [
            pltpu.SMEM(grain_class.shape, jnp.int32),
            pltpu.SMEM(diffusivity.shape, jnp.float32),
            pltpu.VMEM(plane, jnp.int32),
            pltpu.VMEM(plane, jnp.int32),
            pltpu.SemaphoreType.DMA((13,)),
        ],
        [index] + [
            pltpu.with_memory_space_constraint(array, pltpu.HBM)
            for array in (grain_class, diffusivity, phases, grains, concentration)
        ],
        pltpu.HBM,
    )
    own = stack(index, swaps(*parts, Z_AXIS), (block, kappa), HALO)
    mate, other = swaps(own, own, Y_AXIS)
    (field, *parts), shared, faces = cycle(index, (mate, own, other), None, None, False)

    own = stack(index, swaps(*parts, Z_AXIS), (field,), FIELD_HALO)
    mate, other = swaps(own, own, Y_AXIS)
    return cycle(index, (mate, own, other), shared, faces, True)[0][0]


def solution(mesh):
    z_devices, y_devices = mesh.shape["gz"], mesh.shape["gy"]
    cores = jax.sharding.Mesh(mesh.devices.reshape(z_devices, y_devices // 2, 2), ("gz", "gx", "core"))
    split = P("gz", ("gx", "core"), None)
    return jax.shard_map(
        per_device, mesh=cores, in_specs=(split, split, split, P(), P()), out_specs=split, check_vma=False
    )
```

```python
import jax
import jax.numpy as jnp
from jax import lax
from jax.experimental import pallas as pl
from jax.experimental.pallas import tpu as pltpu
from jax.sharding import PartitionSpec as P

HALO = 10
FIELD_HALO = 11
WZ = 40
BLOCKS = 10
WY = 24
NEAR = 9
SPAN = 20
VMEM_BYTES = 48 * 1024 * 1024


def harmonic(near_k, far_k):
    return 2.0 * near_k * far_k / (near_k + far_k)


def dot(left, right):
    return jnp.dot(left, right, precision=lax.Precision.HIGHEST, preferred_element_type=jnp.float32)


def iota(rows, dim, lanes=128):
    return lax.broadcasted_iota(jnp.int32, (rows, lanes), dim)


def matrix(condition, value):
    return jnp.where(condition, jnp.float32(value), jnp.float32(0.0))


def lane_map(make):
    return make(iota(128, 0), iota(128, 1))


class Level:
    def __init__(self, planes, ny, zl, step, span, pad, y_start, y_total, chunk):
        self.planes, self.ny, self.zl, self.step, self.span, self.pad = planes, ny, zl, step, span, pad
        self.y_start, self.y_total = y_start, y_total
        self.rows = planes * ny
        self.chunk = min(chunk, self.rows)

    def chunks(self, start=0, count=None):
        count = self.rows if count is None else count
        at = start
        while at < start + count:
            size = min(self.chunk, start + count - at)
            yield at, size
            at += size

    def neighbours(self, ref, at, size):
        base = self.pad + at
        here = ref[base : base + size]
        below = ref[base - self.ny : base - self.ny + size]
        above = ref[base + self.ny : base + self.ny + size]
        if self.zl > 1:
            width = 128 // self.zl
            lane = iota(size, 1)
            below = pltpu.roll(jnp.where(lane >= 128 - width, below, here), width, 1)
            above = pltpu.roll(jnp.where(lane < width, above, here), 128 - width, 1)
        return (
            here,
            (
                below,
                above,
                ref[base - 1 : base - 1 + size],
                ref[base + 1 : base + 1 + size],
                pltpu.roll(here, self.step, 1),
            ),
        )

    def close(self, ref, value):
        edge = jnp.full((self.pad, 128), value, jnp.float32)
        ref[0 : self.pad] = edge
        ref[self.pad + self.rows : 2 * self.pad + self.rows] = edge

    def shape(self):
        return (self.rows + 2 * self.pad, 128)

    def build(self, kappa, faces):
        for number in (0, 2):
            self.close(faces.at[number], 0.0)
        for at, size in self.chunks():
            here, around = self.neighbours(kappa, at, size)
            y = (iota(size, 0) & (self.ny - 1)) + self.y_start
            x = iota(size, 1) & (self.span - 1)
            rows = slice(self.pad + at, self.pad + at + size)
            faces[0, rows] = harmonic(here, around[0])
            faces[2, rows] = jnp.where((y != 0) & (y != self.y_total), harmonic(here, around[2]), 0.0)
            faces[3, rows] = jnp.where(x >= self.step, harmonic(here, around[4]), 0.0)
        for at, size in self.chunks():
            rows = slice(self.pad + at, self.pad + at + size)
            z_low, around = self.neighbours(faces.at[0], at, size)
            z_high = around[1]
            y_high = faces[2, self.pad + at + 1 : self.pad + at + 1 + size]
            x_low = faces[3, rows]
            total = 1.0 + z_low + z_high + faces[2, rows] + y_high + x_low + pltpu.roll(x_low, 128 - self.step, 1)
            faces[1, rows] = z_high
            faces[4, rows] = 0.8 / total
            faces[5, rows] = total

    def coupled(self, field, source, faces, at, size):
        here, around = self.neighbours(field, at, size)
        rows = slice(self.pad + at, self.pad + at + size)
        next_rows = slice(self.pad + at + 1, self.pad + at + 1 + size)
        x_low = faces[3, rows]
        total = (
            source[at : at + size]
            + faces[0, rows] * around[0]
            + faces[1, rows] * around[1]
            + faces[2, rows] * around[2]
            + faces[2, next_rows] * around[3]
            + x_low * around[4]
            + pltpu.roll(x_low * here, 128 - self.step, 1)
        )
        return here, total

    def start(self, field, source, faces):
        for at, size in self.chunks():
            rows = slice(self.pad + at, self.pad + at + size)
            field[rows] = faces[4, rows] * source[at : at + size]

    def relax(self, field, target, source, faces, start=0, count=None):
        for at, size in self.chunks(start, count):
            here, total = self.coupled(field, source, faces, at, size)
            rows = slice(self.pad + at, self.pad + at + size)
            target[rows] = 0.2 * here + faces[4, rows] * total

    def defect(self, field, source, faces, out, start=0, count=None):
        for at, size in self.chunks(start, count):
            here, total = self.coupled(field, source, faces, at, size)
            diagonal = faces[5, self.pad + at : self.pad + at + size]
            out[at - start : at - start + size] = total - diagonal * here

    def pairs(self, ref):
        half = self.rows // 2
        return ref[pl.ds(0, half, stride=2), :] + ref[pl.ds(1, half, stride=2), :]


def coarsen(value, step, zl=1):
    lane = iota(value.shape[0], 1)
    value = value + jnp.where((lane & step) == 0, pltpu.roll(value, 128 - step, 1), pltpu.roll(value, step, 1))
    if zl == 4:
        value = value + jnp.where((lane & 32) == 0, pltpu.roll(value, 96, 1), pltpu.roll(value, 32, 1))
    if zl == 2:
        value = value + pltpu.roll(value, 64, 1)
    return 0.125 * value


def parities(index):
    return index[0] % 2 == 0, index[1] % 2 == 0


def kappa_body(index, class_hbm, diff_hbm, phases_hbm, grains_hbm, conc_hbm, kappa_ref, own_ref, mate_ref, other_ref, classes, diff, phases, grains, sems):
    even, _ = parities(index)
    num_phases, num_classes = diff.shape
    pairs = [(class_hbm, classes), (diff_hbm, diff)]
    for block in range(4):
        pairs += [(phases_hbm.at[4 * block], phases.at[block]), (grains_hbm.at[4 * block], grains.at[block])]
    top = 16 - HALO
    pairs += [
        (conc_hbm.at[pl.ds(jnp.where(even, top, 0), HALO)], mate_ref.at[0:HALO]),
        (conc_hbm.at[pl.ds(jnp.where(even, 0, top), HALO)], other_ref.at[0:HALO]),
        (conc_hbm, own_ref),
    ]
    copies = [pltpu.make_async_copy(source, target, sems.at[i]) for i, (source, target) in enumerate(pairs)]
    for copy in copies:
        copy.start()
    for copy in copies[:-3]:
        copy.wait()
    grain = grains[...]
    phase = phases[...]
    cls = jnp.zeros(grain.shape, jnp.int32)
    for number in range(classes.shape[0]):
        cls = jnp.where(grain == number, classes[number], cls)
    value = jnp.ones(grain.shape, jnp.float32)
    for p in range(num_phases):
        for c in range(num_classes):
            value = jnp.where((phase == p) & (cls == c), diff[p, c], value)
    rows = jnp.concatenate([value[block, 4 * half : 4 * half + 1] for block in range(4) for half in range(2)], axis=0)
    kappa_ref[0] = rows
    mate_ref[HALO] = rows
    other_ref[HALO] = rows
    for copy in copies[-3:]:
        copy.wait()


def window(refs, plane, even):
    mate, own, other = (ref[plane] for ref in refs)
    return jnp.concatenate([jnp.where(even, other, mate), own, jnp.where(even, mate, other)], axis=0)


def build_fine(sources, even, y_device, kappa, coefs, z_faces):
    kappa[0:8] = jnp.ones((8, 128), jnp.float32)
    kappa[8 + BLOCKS * WY : 16 + BLOCKS * WY] = jnp.ones((8, 128), jnp.float32)
    for block in range(BLOCKS):
        plane, number = divmod(block + 1, 4)
        two = slice(2 * number, 2 * number + 2)
        mate, own, other = (ref[16 + 2 * HALO + plane, two] for ref in sources)
        rows = (jnp.where(even, other, mate), own, jnp.where(even, mate, other))
        kappa[8 + block * WY : 8 + (block + 1) * WY] = jnp.concatenate(
            [jnp.broadcast_to(pair[half : half + 1], (4, 128)) for pair in rows for half in range(2)], axis=0
        )
    y = iota(WY, 0) + y_device * 8 - 8
    x = iota(WY, 1)
    for block in range(BLOCKS + 1):
        low, high = max(block - 1, 0), min(block, BLOCKS - 1)
        z_faces[block] = harmonic(
            kappa[8 + low * WY : 8 + (low + 1) * WY], kappa[8 + high * WY : 8 + (high + 1) * WY]
        )
    for block in range(BLOCKS):
        at = 8 + block * WY
        k = kappa[at : at + WY]
        y_low = jnp.where(y == 0, 0.0, harmonic(k, kappa[at - 1 : at - 1 + WY]))
        y_high = jnp.where(y == 63, 0.0, harmonic(k, kappa[at + 1 : at + 1 + WY]))
        x_low = jnp.where(x == 0, 0.0, harmonic(k, pltpu.roll(k, 1, 1)))
        x_high = jnp.where(x == 127, 0.0, harmonic(k, pltpu.roll(k, 127, 1)))
        sides = 1.0 + y_low + y_high + x_low + x_high
        diagonals = (sides + z_faces[block] + k, sides + k + k, sides + k + z_faces[block + 1])
        for number, value in enumerate((k, y_low, y_high, x_low, x_high)):
            coefs[block, number] = value
        for number, value in enumerate(diagonals):
            coefs[block, 5 + number] = 0.8 / value
            coefs[block, 8 + number] = value


def fine_plane(field, source, coefs, z_faces, z, low=0, size=WY):
    block, p = divmod(z, 4)
    rows = slice(low, low + size)
    at = WY + z * WY + low
    here = field[at : at + size]
    k = coefs[block, 0, rows]
    below = z_faces[block, rows] if p == 0 else k
    above = z_faces[block + 1, rows] if p == 3 else k
    total = (
        source[z * WY + low : z * WY + low + size]
        + below * field[at - WY : at - WY + size]
        + above * field[at + WY : at + WY + size]
        + coefs[block, 1, rows] * field[at - 1 : at - 1 + size]
        + coefs[block, 2, rows] * field[at + 1 : at + 1 + size]
        + coefs[block, 3, rows] * pltpu.roll(here, 1, 1)
        + coefs[block, 4, rows] * pltpu.roll(here, 127, 1)
    )
    kind = (0, 1, 1, 2)[p]
    return here, total, coefs[block, 5 + kind, rows], coefs[block, 8 + kind, rows]


def level_one(y_device):
    return Level(20, 16, 1, 2, 128, 16, y_device * 4 - 4, 32, 160)


def build_one(level, kappa, spread, packed, kappa_one, faces):
    for block in range(BLOCKS):
        spread[block * 32 : block * 32 + WY] = kappa[8 + block * WY : 8 + (block + 1) * WY]
        spread[block * 32 + WY : block * 32 + 32] = jnp.ones((32 - WY, 128), jnp.float32)
    packed[...] = 0.5 * spread[pl.ds(0, BLOCKS * 16, stride=2), :]
    level.close(kappa_one, 1.0)
    for block in range(BLOCKS):
        value = packed[block * 16 : block * 16 + 16]
        kappa_one[16 + block * 32 : 32 + block * 32] = value
        kappa_one[32 + block * 32 : 48 + block * 32] = value
    level.build(kappa_one, faces)


def to_chunk(rows):
    group = iota(8, 1) >> 5
    out = rows[0:8]
    for z in range(1, 4):
        out = jnp.where(group == z, rows[8 * z : 8 * z + 8], out)
    return out


def down_body(first, copies, *refs):
    index, refs = refs[0], refs[1:]
    if first:
        sources, refs = refs[:3], refs[3:]
    else:
        fields, (source, coefs, z_faces, faces), refs = refs[:3], refs[3:7], refs[7:]
    chunk, edge, kept, source_one, kept_one = refs[:5]
    refs = refs[5:]
    if first:
        (source, coefs, z_faces, faces), refs = refs[:4], refs[4:]
    va, vb, rs, oa, tmp = refs[:5]
    _, even = parities(index)
    y_device = index[1]
    level = level_one(y_device)
    if first:
        kappa, spread, packed, kappa_one = refs[5:]
        build_fine(sources, even, y_device, kappa, coefs, z_faces)
        build_one(level, kappa, spread, packed, kappa_one, faces)
    zero = jnp.zeros((WY, 128), jnp.float32)
    for ref in (va, vb):
        ref[0:WY] = zero
        ref[(WZ + 1) * WY : (WZ + 2) * WY] = zero
    if first:
        for z in range(WZ):
            kind = (0, 1, 1, 2)[z % 4]
            inside = 0 <= z + HALO - 12 < 16 + 2 * HALO
            value = window(sources, z + HALO - 12, even) if inside else zero
            source[z * WY : (z + 1) * WY] = value
            va[(z + 1) * WY : (z + 2) * WY] = coefs[z // 4, 5 + kind] * value
    else:
        for z in range(1, WZ - 1):
            vb[(z + 1) * WY : (z + 2) * WY] = window(fields, z - 1, even)
        for z in range(2, WZ - 2):
            here, total, weight, _ = fine_plane(vb, source, coefs, z_faces, z)
            va[(z + 1) * WY : (z + 2) * WY] = 0.2 * here + weight * total
    for z in range(3, WZ - 3):
        here, total, weight, _ = fine_plane(va, source, coefs, z_faces, z)
        value = 0.2 * here + weight * total
        vb[(z + 1) * WY : (z + 2) * WY] = value
        if 10 <= z < 30:
            kept[(z - 10) * WY : (z - 9) * WY] = value
    for plane in range(20):
        if 2 <= plane < 18:
            total_defect = 0.0
            for z in (2 * plane, 2 * plane + 1):
                here, total, _, diagonal = fine_plane(vb, source, coefs, z_faces, z)
                total_defect = total_defect + (total - diagonal * here)
            rs[plane * 32 : plane * 32 + WY] = total_defect
            rs[plane * 32 + WY : plane * 32 + 32] = jnp.zeros((32 - WY, 128), jnp.float32)
        else:
            rs[plane * 32 : plane * 32 + 32] = jnp.zeros((32, 128), jnp.float32)
    source_one[...] = coarsen(rs[pl.ds(0, 320, stride=2), :] + rs[pl.ds(1, 320, stride=2), :], 1)
    for ref in (oa, kept_one):
        level.close(ref, 0.0)
    level.start(oa, source_one, faces)
    level.relax(oa, kept_one, source_one, faces)
    level.defect(kept_one, source_one, faces, tmp, 6 * 16, 8 * 16)
    for z in range(4):
        tmp[z * 16 : z * 16 + 16] = tmp[z * 32 : z * 32 + 16] + tmp[z * 32 + 16 : z * 32 + 32]
    halves = tmp[pl.ds(0, 32, stride=2), :] + tmp[pl.ds(1, 32, stride=2), :]
    mean_two = lane_map(lambda r, c: matrix(((r & 1) == 0) & (r >> 2 == (c & 31)), 0.125))
    values = [to_chunk(dot(halves, mean_two))[2:4]]
    if first:
        pick_two = lane_map(lambda r, c: matrix(r == 4 * (c & 31), 0.5))
        values.append(to_chunk(dot(packed[pl.ds(48, 32, stride=2), :], pick_two))[2:4])
    repeats = 4 // len(values)
    tile = jnp.concatenate(values * repeats, axis=0)
    for at in range(0, copies // repeats):
        chunk[at * 8 : at * 8 + 8] = tile
    for plane in range(20):
        edge[plane * 4 : plane * 4 + 4] = kept_one[16 + plane * 16 + 4 : 16 + plane * 16 + 8]


def coarse_levels():
    return (
        Level(SPAN, 16, 4, 1, 32, 16, 0, 16, 160),
        Level(SPAN, 8, 2, 2, 32, 8, 0, 8, 160),
        Level(SPAN, 4, 1, 4, 32, 8, 0, 4, 128),
    )


def coarse_body(first, z_devices, *refs):
    two, three, four = coarse_levels()
    index, same, mate = refs[:3]
    refs = refs[3:]
    if first:
        near, f2, f3, f4 = refs[:4]
    else:
        f2, f3, f4, near = refs[:4]
    a2, b2, g2, r2, a3, b3, g3, r3, a4, b4, g4, cut_same, cut_mate = refs[4:17]
    z_device = index[0]
    even = index[1] % 2 == 0
    per = 4 if first else 2
    rows = 4 * per
    for number in range(SPAN):
        at = lax.rem(z_device + (number - NEAR + 4 * z_devices), z_devices) * rows
        at = pl.multiple_of(at, 8)
        cut_same[number * rows : (number + 1) * rows] = same[pl.ds(at, rows), :]
        cut_mate[number * rows : (number + 1) * rows] = mate[pl.ds(at, rows), :]

    def interleave(target, start, part):
        for y in range(2):
            take = pl.ds(part + y, 4 * SPAN, stride=per)
            one, two_ = cut_same[take, :], cut_mate[take, :]
            target[pl.ds(start + y, 4 * SPAN, stride=4), :] = jnp.where(even, one, two_)
            target[pl.ds(start + 2 + y, 4 * SPAN, stride=4), :] = jnp.where(even, two_, one)

    interleave(g2, 0, 0)
    if first:
        k2, k3, k4 = refs[17:]
        interleave(k2, two.pad, 2)
        two.close(k2, 1.0)
        two.build(k2, f2)
        r2[...] = k2[two.pad : two.pad + two.rows]
        k3[three.pad : three.pad + three.rows] = 0.5 * coarsen(two.pairs(r2), 1, 4)
        three.close(k3, 1.0)
        three.build(k3, f3)
        r3[...] = k3[three.pad : three.pad + three.rows]
        k4[four.pad : four.pad + four.rows] = 0.5 * coarsen(three.pairs(r3), 2, 2)
        four.close(k4, 1.0)
        four.build(k4, f4)
    for level, fields in ((two, (a2, b2)), (three, (a3, b3)), (four, (a4, b4))):
        for field in fields:
            level.close(field, 0.0)

    two.start(a2, g2, f2)
    two.relax(a2, b2, g2, f2)
    two.defect(b2, g2, f2, r2)
    g3[...] = coarsen(two.pairs(r2), 1, 4)
    three.start(a3, g3, f3)
    three.relax(a3, b3, g3, f3)
    three.defect(b3, g3, f3, r3)
    g4[...] = coarsen(three.pairs(r3), 2, 2)
    four.start(a4, g4, f4)
    for _ in range(2):
        four.relax(a4, b4, g4, f4)
        four.relax(b4, a4, g4, f4)
    four.relax(a4, b4, g4, f4)

    def correct(level, field, start, count, value, tmp):
        tmp[pl.ds(0, count // 2, stride=2), :] = value
        tmp[pl.ds(1, count // 2, stride=2), :] = value
        inner = slice(level.pad + start, level.pad + start + count)
        field[inner] = field[inner] + tmp[0:count]

    low = NEAR - 3
    correct(three, b3, 8 * low, 48, b4[four.pad + 4 * low : four.pad + 4 * low + 24], r3)
    three.relax(b3, a3, g3, f3, 8 * low, 48)
    low = NEAR - 1
    three.relax(a3, b3, g3, f3, 8 * low, 24)
    correct(two, b2, 16 * low, 48, b3[three.pad + 8 * low : three.pad + 8 * low + 24], r2)
    two.relax(b2, a2, g2, f2, 16 * low, 48)
    two.relax(a2, b2, g2, f2, 16 * low, 48)
    near[...] = b2[two.pad + 16 * low : two.pad + 16 * low + 48]


def up_body(last, *refs):
    index, source, coefs, z_faces, faces, near, edge_mate, edge_other, kept, source_one, kept_one, out = refs[:12]
    refs = refs[12:]
    if last:
        out_hbm, (out, sems), refs = out, refs[-2:], refs[:-2]
        halves = (slice(0, 8), slice(8, 16))
        copies = [
            pltpu.make_async_copy(out.at[half], out_hbm.at[half], sems.at[i]) for i, half in enumerate(halves)
        ]
    else:
        (mate, other), refs = refs[:2], refs[2:]
    va, vb, spread, oa, ob = refs
    even_z, even = parities(index)
    y_device = index[1]
    level = level_one(y_device)
    rows = matrix(iota(16, 1, 16) == y_device * 2 - 2 + (iota(16, 0, 16) >> 1), 1.0)
    spread_y = jnp.concatenate([dot(rows, near[16 * part : 16 * part + 16]) for part in range(3)], axis=0)
    by_z = [
        dot(spread_y, lane_map(lambda r, c, z=z: matrix(r == z * 32 + (c >> 2), 1.0))) for z in range(4)
    ]
    for plane in range(20):
        part, z = divmod(plane // 2 + 1, 4)
        at = 16 + plane * 16
        one, two = edge_mate[plane * 4 : plane * 4 + 4], edge_other[plane * 4 : plane * 4 + 4]
        field = jnp.concatenate(
            [jnp.where(even, two, one), kept_one[at + 4 : at + 8], jnp.where(even, one, two),
             jnp.zeros((4, 128), jnp.float32)], axis=0
        )
        oa[at : at + 16] = field + by_z[z][16 * part : 16 * part + 16]
    level.relax(oa, ob, source_one, faces, 4 * 16, 12 * 16)
    level.relax(ob, oa, source_one, faces, 5 * 16, 10 * 16)
    value = oa[16 + 80 : 16 + 240]
    spread[pl.ds(0, 160, stride=2), :] = value
    spread[pl.ds(1, 160, stride=2), :] = value
    for z in range(10, 30):
        at = ((z - 10) // 2) * 32
        va[(z + 1) * WY : (z + 2) * WY] = kept[(z - 10) * WY : (z - 9) * WY] + spread[at : at + WY]
    for z in range(11, 29):
        here, total, weight, _ = fine_plane(va, source, coefs, z_faces, z)
        vb[(z + 1) * WY : (z + 2) * WY] = 0.2 * here + weight * total
    for z in range(12, 28):
        here, total, weight, _ = fine_plane(vb, source, coefs, z_faces, z, 8, 8)
        out[z - 12] = 0.2 * here + weight * total
        if last and z in (19, 27):
            copies[z // 27].start()
    if last:
        for copy in copies:
            copy.wait()
    else:
        top = 16 - FIELD_HALO
        mate[...] = out[pl.ds(jnp.where(even_z, top, 0), FIELD_HALO)]
        other[...] = out[pl.ds(jnp.where(even_z, 0, top), FIELD_HALO)]


def floats(*shape):
    return jax.ShapeDtypeStruct(shape, jnp.float32)


def call(body, outs, scratch, args, inputs=pltpu.VMEM, outputs=pltpu.VMEM):
    return pl.pallas_call(
        body,
        out_shape=outs,
        in_specs=[pl.BlockSpec(memory_space=pltpu.SMEM)] + [pl.BlockSpec(memory_space=inputs)] * (len(args) - 1),
        out_specs=[pl.BlockSpec(memory_space=outputs)] * len(outs),
        scratch_shapes=[pltpu.VMEM(s, jnp.float32) if isinstance(s, tuple) else s for s in scratch],
        compiler_params=pltpu.CompilerParams(vmem_limit_bytes=VMEM_BYTES),
    )(*args)


FIELD = ((WZ + 2) * WY, 128)
SHARED = [(WZ * WY, 128), (BLOCKS, 11, WY, 128), (BLOCKS + 1, WY, 128), (6, 352, 128)]
Z_AXIS = ("gz",)
Y_AXIS = ("gx", "core")


def down(index, arrays, shared):
    first = shared is None
    copies = lax.axis_size("gz") * lax.axis_size("gx")
    outs = [
        floats(copies * (4 if first else 2), 128),
        floats(80, 128),
        floats(20 * WY, 128),
        floats(320, 128),
        floats(352, 128),
    ]
    scratch = [FIELD, FIELD, (640, 128), (352, 128), (128, 128)]
    if first:
        outs += [floats(*shape) for shape in SHARED]
        scratch += [(16 + BLOCKS * WY, 128), (320, 128), (160, 128), (352, 128)]
        args = [index, *arrays]
    else:
        args = [index, *arrays, *shared]
    result = call(lambda *refs: down_body(first, copies, *refs), outs, scratch, args)
    return result[0], result[1], result[2:5], result[5:] if first else shared


def coarse(index, gathered, faces):
    first = faces is None
    z_devices = lax.axis_size("gz")
    levels = coarse_levels()
    outs, scratch = [floats(48, 128)], []
    if first:
        outs += [floats(6, *level.shape()) for level in levels]
    for level in levels:
        scratch += [level.shape(), level.shape(), (level.rows, 128), (level.rows, 128)]
    cut = (SPAN * (16 if first else 8), 128)
    scratch = scratch[:11] + [cut, cut]
    if first:
        scratch += [level.shape() for level in levels]
    args = [index, *gathered] + ([] if first else list(faces))
    near, *new = call(lambda *refs: coarse_body(first, z_devices, *refs), outs, scratch, args)
    return near, new if first else faces


def up(index, shared, near, edges, kept, last):
    outs = [floats(16, 8, 128)] + ([] if last else [floats(FIELD_HALO, 8, 128)] * 2)
    scratch = [FIELD, FIELD, (320, 128), (352, 128), (352, 128)]
    if last:
        scratch += [(16, 8, 128), pltpu.SemaphoreType.DMA((2,))]
    args = [index, *shared, near, *edges, *kept]
    return call(
        lambda *refs: up_body(last, *refs), outs, scratch, args, outputs=pltpu.HBM if last else pltpu.VMEM
    )


def mate_of(i):
    return i + 1 if i % 2 == 0 else i - 1


def other_of(i):
    return i - 1 if i % 2 == 0 else i + 1


def swap(array, axis, partner):
    count = 1
    for name in axis:
        count *= lax.axis_size(name)
    return lax.ppermute(array, axis, [(i, partner(i) % count) for i in range(count)])


def swaps(mate, other, axis):
    far = far_in_y(other) if axis == Y_AXIS else swap(other, axis, other_of)
    return swap(mate, axis, mate_of), far


def far_in_y(array):
    y_devices = lax.axis_size("gx") * lax.axis_size("core")
    pairs = []
    for z in range(lax.axis_size("gz")):
        for y in range(y_devices):
            at = other_of(y)
            target = z * y_devices + at if 0 <= at < y_devices else mate_of(z) * y_devices + y
            pairs.append((z * y_devices + y, target))
    return lax.ppermute(array, ("gz", "gx", "core"), pairs)


def to_all(copies):
    peers = lax.axis_size("gz") * lax.axis_size("gx")
    copies = copies.reshape(peers, copies.shape[0] // peers, 128)
    out = lax.all_to_all(copies, ("gz", "gx"), 0, 0)
    out = out.reshape(out.shape[0] * out.shape[1], 128)
    return out, swap(out, Y_AXIS, mate_of)


def stack(index, parts, own, halo):
    even = index[0] % 2 == 0
    mate, other = parts
    before, after = jnp.where(even, other, mate), jnp.where(even, mate, other)
    pieces = [before[:halo], own[0], after[:halo]]
    if len(own) > 1:
        pieces += [before[halo:], own[1], after[halo:]]
    return jnp.concatenate(pieces, axis=0)


def cycle(index, arrays, shared, coarse_faces, last):
    copies, edge, kept, shared = down(index, arrays, shared)
    edges = swaps(edge, edge, Y_AXIS)
    gathered = to_all(copies)
    near, coarse_faces = coarse(index, gathered, coarse_faces)
    return up(index, shared, near, edges, kept, last), shared, coarse_faces


def per_device(concentration, phases, grains, grain_class, diffusivity):
    y_device = lax.axis_index("gx") * lax.axis_size("core") + lax.axis_index("core")
    index = jnp.stack([lax.axis_index("gz"), y_device]).astype(jnp.int32)
    plane = (4,) + phases.shape[1:]
    part = floats(HALO + 1, 8, 128)
    kappa, block, *parts = call(
        kappa_body,
        [floats(1, 8, 128), floats(*phases.shape), part, part],
        [
            pltpu.SMEM(grain_class.shape, jnp.int32),
            pltpu.SMEM(diffusivity.shape, jnp.float32),
            pltpu.VMEM(plane, jnp.int32),
            pltpu.VMEM(plane, jnp.int32),
            pltpu.SemaphoreType.DMA((13,)),
        ],
        [index] + [
            pltpu.with_memory_space_constraint(array, pltpu.HBM)
            for array in (grain_class, diffusivity, phases, grains, concentration)
        ],
        pltpu.HBM,
    )
    own = stack(index, swaps(*parts, Z_AXIS), (block, kappa), HALO)
    mate, other = swaps(own, own, Y_AXIS)
    (field, *parts), shared, faces = cycle(index, (mate, own, other), None, None, False)

    own = stack(index, swaps(*parts, Z_AXIS), (field,), FIELD_HALO)
    mate, other = swaps(own, own, Y_AXIS)
    return cycle(index, (mate, own, other), shared, faces, True)[0][0]


def solution(mesh):
    z_devices, y_devices = mesh.shape["gz"], mesh.shape["gy"]
    cores = jax.sharding.Mesh(mesh.devices.reshape(z_devices, y_devices // 2, 2), ("gz", "gx", "core"))
    split = P("gz", ("gx", "core"), None)
    return jax.shard_map(
        per_device, mesh=cores, in_specs=(split, split, split, P(), P()), out_specs=split, check_vma=False
    )
```

```python
import jax
import jax.numpy as jnp
from jax import lax
from jax.experimental import pallas as pl
from jax.experimental.pallas import tpu as pltpu
from jax.sharding import PartitionSpec as P

HALO = 10
FIELD_HALO = 11
WZ = 40
BLOCKS = 10
WY = 24
NEAR = 9
SPAN = 20
VMEM_BYTES = 48 * 1024 * 1024


def harmonic(near_k, far_k):
    return 2.0 * near_k * far_k / (near_k + far_k)


def dot(left, right):
    return jnp.dot(left, right, precision=lax.Precision.HIGHEST, preferred_element_type=jnp.float32)


def iota(rows, dim, lanes=128):
    return lax.broadcasted_iota(jnp.int32, (rows, lanes), dim)


def matrix(condition, value):
    return jnp.where(condition, jnp.float32(value), jnp.float32(0.0))


def lane_map(make):
    return make(iota(128, 0), iota(128, 1))


class Level:
    def __init__(self, planes, ny, zl, step, span, pad, y_start, y_total, chunk):
        self.planes, self.ny, self.zl, self.step, self.span, self.pad = planes, ny, zl, step, span, pad
        self.y_start, self.y_total = y_start, y_total
        self.rows = planes * ny
        self.chunk = min(chunk, self.rows)

    def chunks(self, start=0, count=None):
        count = self.rows if count is None else count
        at = start
        while at < start + count:
            size = min(self.chunk, start + count - at)
            yield at, size
            at += size

    def neighbours(self, ref, at, size):
        base = self.pad + at
        here = ref[base : base + size]
        below = ref[base - self.ny : base - self.ny + size]
        above = ref[base + self.ny : base + self.ny + size]
        if self.zl > 1:
            width = 128 // self.zl
            lane = iota(size, 1)
            below = pltpu.roll(jnp.where(lane >= 128 - width, below, here), width, 1)
            above = pltpu.roll(jnp.where(lane < width, above, here), 128 - width, 1)
        return (
            here,
            (
                below,
                above,
                ref[base - 1 : base - 1 + size],
                ref[base + 1 : base + 1 + size],
                pltpu.roll(here, self.step, 1),
            ),
        )

    def close(self, ref, value):
        edge = jnp.full((self.pad, 128), value, jnp.float32)
        ref[0 : self.pad] = edge
        ref[self.pad + self.rows : 2 * self.pad + self.rows] = edge

    def shape(self):
        return (self.rows + 2 * self.pad, 128)

    def build(self, kappa, faces):
        for number in (0, 2):
            self.close(faces.at[number], 0.0)
        for at, size in self.chunks():
            here, around = self.neighbours(kappa, at, size)
            y = (iota(size, 0) & (self.ny - 1)) + self.y_start
            x = iota(size, 1) & (self.span - 1)
            rows = slice(self.pad + at, self.pad + at + size)
            faces[0, rows] = harmonic(here, around[0])
            faces[2, rows] = jnp.where((y != 0) & (y != self.y_total), harmonic(here, around[2]), 0.0)
            faces[3, rows] = jnp.where(x >= self.step, harmonic(here, around[4]), 0.0)
        for at, size in self.chunks():
            rows = slice(self.pad + at, self.pad + at + size)
            z_low, around = self.neighbours(faces.at[0], at, size)
            z_high = around[1]
            y_high = faces[2, self.pad + at + 1 : self.pad + at + 1 + size]
            x_low = faces[3, rows]
            total = 1.0 + z_low + z_high + faces[2, rows] + y_high + x_low + pltpu.roll(x_low, 128 - self.step, 1)
            faces[1, rows] = z_high
            faces[4, rows] = 0.8 / total
            faces[5, rows] = total

    def coupled(self, field, source, faces, at, size):
        here, around = self.neighbours(field, at, size)
        rows = slice(self.pad + at, self.pad + at + size)
        next_rows = slice(self.pad + at + 1, self.pad + at + 1 + size)
        x_low = faces[3, rows]
        total = (
            source[at : at + size]
            + faces[0, rows] * around[0]
            + faces[1, rows] * around[1]
            + faces[2, rows] * around[2]
            + faces[2, next_rows] * around[3]
            + x_low * around[4]
            + pltpu.roll(x_low * here, 128 - self.step, 1)
        )
        return here, total

    def start(self, field, source, faces):
        for at, size in self.chunks():
            rows = slice(self.pad + at, self.pad + at + size)
            field[rows] = faces[4, rows] * source[at : at + size]

    def relax(self, field, target, source, faces, start=0, count=None):
        for at, size in self.chunks(start, count):
            here, total = self.coupled(field, source, faces, at, size)
            rows = slice(self.pad + at, self.pad + at + size)
            target[rows] = 0.2 * here + faces[4, rows] * total

    def defect(self, field, source, faces, out, start=0, count=None):
        for at, size in self.chunks(start, count):
            here, total = self.coupled(field, source, faces, at, size)
            diagonal = faces[5, self.pad + at : self.pad + at + size]
            out[at - start : at - start + size] = total - diagonal * here

    def pairs(self, ref):
        half = self.rows // 2
        return ref[pl.ds(0, half, stride=2), :] + ref[pl.ds(1, half, stride=2), :]


def coarsen(value, step, zl=1):
    lane = iota(value.shape[0], 1)
    value = value + jnp.where((lane & step) == 0, pltpu.roll(value, 128 - step, 1), pltpu.roll(value, step, 1))
    if zl == 4:
        value = value + jnp.where((lane & 32) == 0, pltpu.roll(value, 96, 1), pltpu.roll(value, 32, 1))
    if zl == 2:
        value = value + pltpu.roll(value, 64, 1)
    return 0.125 * value


def parities(index):
    return index[0] % 2 == 0, index[1] % 2 == 0


def kappa_body(index, class_hbm, diff_hbm, phases_hbm, grains_hbm, conc_hbm, kappa_ref, own_ref, mate_ref, other_ref, classes, diff, phases, grains, sems):
    even, _ = parities(index)
    num_phases, num_classes = diff.shape
    pairs = [(class_hbm, classes), (diff_hbm, diff)]
    pairs += [(phases_hbm.at[:, 0], phases), (grains_hbm.at[:, 0], grains)]
    top = 16 - HALO
    pairs += [
        (conc_hbm.at[pl.ds(jnp.where(even, top, 0), HALO)], mate_ref.at[0:HALO]),
        (conc_hbm.at[pl.ds(jnp.where(even, 0, top), HALO)], other_ref.at[0:HALO]),
        (conc_hbm, own_ref),
    ]
    copies = [pltpu.make_async_copy(source, target, sems.at[i]) for i, (source, target) in enumerate(pairs)]
    for copy in copies:
        copy.start()
    for copy in copies[:-3]:
        copy.wait()
    grain = grains[...]
    phase = phases[...]
    cls = jnp.zeros(grain.shape, jnp.int32)
    for number in range(classes.shape[0]):
        cls = jnp.where(grain == number, classes[number], cls)
    value = jnp.ones(grain.shape, jnp.float32)
    for p in range(num_phases):
        for c in range(num_classes):
            value = jnp.where((phase == p) & (cls == c), diff[p, c], value)
    rows = jnp.concatenate([value[block, 4 * half : 4 * half + 1] for block in range(4) for half in range(2)], axis=0)
    kappa_ref[0] = rows
    mate_ref[HALO] = rows
    other_ref[HALO] = rows
    for copy in copies[-3:]:
        copy.wait()


def window(refs, plane, even):
    mate, own, other = (ref[plane] for ref in refs)
    return jnp.concatenate([jnp.where(even, other, mate), own, jnp.where(even, mate, other)], axis=0)


def build_fine(sources, even, y_device, kappa, coefs, z_faces):
    kappa[0:8] = jnp.ones((8, 128), jnp.float32)
    kappa[8 + BLOCKS * WY : 16 + BLOCKS * WY] = jnp.ones((8, 128), jnp.float32)
    for block in range(BLOCKS):
        plane, number = divmod(block + 1, 4)
        two = slice(2 * number, 2 * number + 2)
        mate, own, other = (ref[16 + 2 * HALO + plane, two] for ref in sources)
        rows = (jnp.where(even, other, mate), own, jnp.where(even, mate, other))
        kappa[8 + block * WY : 8 + (block + 1) * WY] = jnp.concatenate(
            [jnp.broadcast_to(pair[half : half + 1], (4, 128)) for pair in rows for half in range(2)], axis=0
        )
    y = iota(WY, 0) + y_device * 8 - 8
    x = iota(WY, 1)
    for block in range(BLOCKS + 1):
        low, high = max(block - 1, 0), min(block, BLOCKS - 1)
        z_faces[block] = harmonic(
            kappa[8 + low * WY : 8 + (low + 1) * WY], kappa[8 + high * WY : 8 + (high + 1) * WY]
        )
    for block in range(BLOCKS):
        at = 8 + block * WY
        k = kappa[at : at + WY]
        y_low = jnp.where(y == 0, 0.0, harmonic(k, kappa[at - 1 : at - 1 + WY]))
        y_high = jnp.where(y == 63, 0.0, harmonic(k, kappa[at + 1 : at + 1 + WY]))
        x_low = jnp.where(x == 0, 0.0, harmonic(k, pltpu.roll(k, 1, 1)))
        x_high = jnp.where(x == 127, 0.0, harmonic(k, pltpu.roll(k, 127, 1)))
        sides = 1.0 + y_low + y_high + x_low + x_high
        diagonals = (sides + z_faces[block] + k, sides + k + k, sides + k + z_faces[block + 1])
        for number, value in enumerate((k, y_low, y_high, x_low, x_high)):
            coefs[block, number] = value
        for number, value in enumerate(diagonals):
            coefs[block, 5 + number] = 0.8 / value
            coefs[block, 8 + number] = value


def fine_plane(field, source, coefs, z_faces, z, low=0, size=WY):
    block, p = divmod(z, 4)
    rows = slice(low, low + size)
    at = WY + z * WY + low
    here = field[at : at + size]
    k = coefs[block, 0, rows]
    below = z_faces[block, rows] if p == 0 else k
    above = z_faces[block + 1, rows] if p == 3 else k
    total = (
        source[z * WY + low : z * WY + low + size]
        + below * field[at - WY : at - WY + size]
        + above * field[at + WY : at + WY + size]
        + coefs[block, 1, rows] * field[at - 1 : at - 1 + size]
        + coefs[block, 2, rows] * field[at + 1 : at + 1 + size]
        + coefs[block, 3, rows] * pltpu.roll(here, 1, 1)
        + coefs[block, 4, rows] * pltpu.roll(here, 127, 1)
    )
    kind = (0, 1, 1, 2)[p]
    return here, total, coefs[block, 5 + kind, rows], coefs[block, 8 + kind, rows]


def level_one(y_device):
    return Level(20, 16, 1, 2, 128, 16, y_device * 4 - 4, 32, 160)


def build_one(level, kappa, spread, packed, kappa_one, faces):
    for block in range(BLOCKS):
        spread[block * 32 : block * 32 + WY] = kappa[8 + block * WY : 8 + (block + 1) * WY]
        spread[block * 32 + WY : block * 32 + 32] = jnp.ones((32 - WY, 128), jnp.float32)
    packed[...] = 0.5 * spread[pl.ds(0, BLOCKS * 16, stride=2), :]
    level.close(kappa_one, 1.0)
    for block in range(BLOCKS):
        value = packed[block * 16 : block * 16 + 16]
        kappa_one[16 + block * 32 : 32 + block * 32] = value
        kappa_one[32 + block * 32 : 48 + block * 32] = value
    level.build(kappa_one, faces)


def to_chunk(rows):
    group = iota(8, 1) >> 5
    out = rows[0:8]
    for z in range(1, 4):
        out = jnp.where(group == z, rows[8 * z : 8 * z + 8], out)
    return out


def down_body(first, copies, *refs):
    index, refs = refs[0], refs[1:]
    if first:
        sources, refs = refs[:3], refs[3:]
    else:
        fields, (source, coefs, z_faces, faces), refs = refs[:3], refs[3:7], refs[7:]
    chunk, edge, kept, source_one, kept_one = refs[:5]
    refs = refs[5:]
    if first:
        (source, coefs, z_faces, faces), refs = refs[:4], refs[4:]
    va, vb, rs, oa, tmp = refs[:5]
    _, even = parities(index)
    y_device = index[1]
    level = level_one(y_device)
    if first:
        kappa, spread, packed, kappa_one = refs[5:]
        build_fine(sources, even, y_device, kappa, coefs, z_faces)
        build_one(level, kappa, spread, packed, kappa_one, faces)
    zero = jnp.zeros((WY, 128), jnp.float32)
    for ref in (va, vb):
        ref[0:WY] = zero
        ref[(WZ + 1) * WY : (WZ + 2) * WY] = zero
    if first:
        for z in range(WZ):
            kind = (0, 1, 1, 2)[z % 4]
            inside = 0 <= z + HALO - 12 < 16 + 2 * HALO
            value = window(sources, z + HALO - 12, even) if inside else zero
            source[z * WY : (z + 1) * WY] = value
            va[(z + 1) * WY : (z + 2) * WY] = coefs[z // 4, 5 + kind] * value
    else:
        for z in range(1, WZ - 1):
            vb[(z + 1) * WY : (z + 2) * WY] = window(fields, z - 1, even)
        for z in range(2, WZ - 2):
            here, total, weight, _ = fine_plane(vb, source, coefs, z_faces, z)
            va[(z + 1) * WY : (z + 2) * WY] = 0.2 * here + weight * total
    for z in range(3, WZ - 3):
        here, total, weight, _ = fine_plane(va, source, coefs, z_faces, z)
        value = 0.2 * here + weight * total
        vb[(z + 1) * WY : (z + 2) * WY] = value
        if 10 <= z < 30:
            kept[(z - 10) * WY : (z - 9) * WY] = value
    for plane in range(20):
        if 2 <= plane < 18:
            total_defect = 0.0
            for z in (2 * plane, 2 * plane + 1):
                here, total, _, diagonal = fine_plane(vb, source, coefs, z_faces, z)
                total_defect = total_defect + (total - diagonal * here)
            rs[plane * 32 : plane * 32 + WY] = total_defect
            rs[plane * 32 + WY : plane * 32 + 32] = jnp.zeros((32 - WY, 128), jnp.float32)
        else:
            rs[plane * 32 : plane * 32 + 32] = jnp.zeros((32, 128), jnp.float32)
    source_one[...] = coarsen(rs[pl.ds(0, 320, stride=2), :] + rs[pl.ds(1, 320, stride=2), :], 1)
    for ref in (oa, kept_one):
        level.close(ref, 0.0)
    level.start(oa, source_one, faces)
    level.relax(oa, kept_one, source_one, faces)
    level.defect(kept_one, source_one, faces, tmp, 6 * 16, 8 * 16)
    for z in range(4):
        tmp[z * 16 : z * 16 + 16] = tmp[z * 32 : z * 32 + 16] + tmp[z * 32 + 16 : z * 32 + 32]
    halves = tmp[pl.ds(0, 32, stride=2), :] + tmp[pl.ds(1, 32, stride=2), :]
    mean_two = lane_map(lambda r, c: matrix(((r & 1) == 0) & (r >> 2 == (c & 31)), 0.125))
    values = [to_chunk(dot(halves, mean_two))[2:4]]
    if first:
        pick_two = lane_map(lambda r, c: matrix(r == 4 * (c & 31), 0.5))
        values.append(to_chunk(dot(packed[pl.ds(48, 32, stride=2), :], pick_two))[2:4])
    repeats = 4 // len(values)
    tile = jnp.concatenate(values * repeats, axis=0)
    for at in range(0, copies // repeats):
        chunk[at * 8 : at * 8 + 8] = tile
    for plane in range(20):
        edge[plane * 4 : plane * 4 + 4] = kept_one[16 + plane * 16 + 4 : 16 + plane * 16 + 8]


def coarse_levels():
    return (
        Level(SPAN, 16, 4, 1, 32, 16, 0, 16, 160),
        Level(SPAN, 8, 2, 2, 32, 8, 0, 8, 160),
        Level(SPAN, 4, 1, 4, 32, 8, 0, 4, 128),
    )


def coarse_body(first, z_devices, *refs):
    two, three, four = coarse_levels()
    index, same, mate = refs[:3]
    refs = refs[3:]
    if first:
        near, f2, f3, f4 = refs[:4]
    else:
        f2, f3, f4, near = refs[:4]
    a2, b2, g2, r2, a3, b3, g3, r3, a4, b4, g4, cut_same, cut_mate = refs[4:17]
    z_device = index[0]
    even = index[1] % 2 == 0
    per = 4 if first else 2
    rows = 4 * per
    for number in range(SPAN):
        at = lax.rem(z_device + (number - NEAR + 4 * z_devices), z_devices) * rows
        at = pl.multiple_of(at, 8)
        cut_same[number * rows : (number + 1) * rows] = same[pl.ds(at, rows), :]
        cut_mate[number * rows : (number + 1) * rows] = mate[pl.ds(at, rows), :]

    def interleave(target, start, part):
        for y in range(2):
            take = pl.ds(part + y, 4 * SPAN, stride=per)
            one, two_ = cut_same[take, :], cut_mate[take, :]
            target[pl.ds(start + y, 4 * SPAN, stride=4), :] = jnp.where(even, one, two_)
            target[pl.ds(start + 2 + y, 4 * SPAN, stride=4), :] = jnp.where(even, two_, one)

    interleave(g2, 0, 0)
    if first:
        k2, k3, k4 = refs[17:]
        interleave(k2, two.pad, 2)
        two.close(k2, 1.0)
        two.build(k2, f2)
        r2[...] = k2[two.pad : two.pad + two.rows]
        k3[three.pad : three.pad + three.rows] = 0.5 * coarsen(two.pairs(r2), 1, 4)
        three.close(k3, 1.0)
        three.build(k3, f3)
        r3[...] = k3[three.pad : three.pad + three.rows]
        k4[four.pad : four.pad + four.rows] = 0.5 * coarsen(three.pairs(r3), 2, 2)
        four.close(k4, 1.0)
        four.build(k4, f4)
    for level, fields in ((two, (a2, b2)), (three, (a3, b3)), (four, (a4, b4))):
        for field in fields:
            level.close(field, 0.0)

    two.start(a2, g2, f2)
    two.relax(a2, b2, g2, f2)
    two.defect(b2, g2, f2, r2)
    g3[...] = coarsen(two.pairs(r2), 1, 4)
    three.start(a3, g3, f3)
    three.relax(a3, b3, g3, f3)
    three.defect(b3, g3, f3, r3)
    g4[...] = coarsen(three.pairs(r3), 2, 2)
    four.start(a4, g4, f4)
    for _ in range(2):
        four.relax(a4, b4, g4, f4)
        four.relax(b4, a4, g4, f4)
    four.relax(a4, b4, g4, f4)

    def correct(level, field, start, count, value, tmp):
        tmp[pl.ds(0, count // 2, stride=2), :] = value
        tmp[pl.ds(1, count // 2, stride=2), :] = value
        inner = slice(level.pad + start, level.pad + start + count)
        field[inner] = field[inner] + tmp[0:count]

    low = NEAR - 3
    correct(three, b3, 8 * low, 48, b4[four.pad + 4 * low : four.pad + 4 * low + 24], r3)
    three.relax(b3, a3, g3, f3, 8 * low, 48)
    low = NEAR - 1
    three.relax(a3, b3, g3, f3, 8 * low, 24)
    correct(two, b2, 16 * low, 48, b3[three.pad + 8 * low : three.pad + 8 * low + 24], r2)
    two.relax(b2, a2, g2, f2, 16 * low, 48)
    two.relax(a2, b2, g2, f2, 16 * low, 48)
    near[...] = b2[two.pad + 16 * low : two.pad + 16 * low + 48]


def up_body(last, *refs):
    index, source, coefs, z_faces, faces, near, edge_mate, edge_other, kept, source_one, kept_one, out = refs[:12]
    refs = refs[12:]
    if last:
        out_hbm, (out, sems), refs = out, refs[-2:], refs[:-2]
        halves = (slice(0, 8), slice(8, 16))
        copies = [
            pltpu.make_async_copy(out.at[half], out_hbm.at[half], sems.at[i]) for i, half in enumerate(halves)
        ]
    else:
        (mate, other), refs = refs[:2], refs[2:]
    va, vb, spread, oa, ob = refs
    even_z, even = parities(index)
    y_device = index[1]
    level = level_one(y_device)
    rows = matrix(iota(16, 1, 16) == y_device * 2 - 2 + (iota(16, 0, 16) >> 1), 1.0)
    spread_y = jnp.concatenate([dot(rows, near[16 * part : 16 * part + 16]) for part in range(3)], axis=0)
    by_z = [
        dot(spread_y, lane_map(lambda r, c, z=z: matrix(r == z * 32 + (c >> 2), 1.0))) for z in range(4)
    ]
    for plane in range(20):
        part, z = divmod(plane // 2 + 1, 4)
        at = 16 + plane * 16
        one, two = edge_mate[plane * 4 : plane * 4 + 4], edge_other[plane * 4 : plane * 4 + 4]
        field = jnp.concatenate(
            [jnp.where(even, two, one), kept_one[at + 4 : at + 8], jnp.where(even, one, two),
             jnp.zeros((4, 128), jnp.float32)], axis=0
        )
        oa[at : at + 16] = field + by_z[z][16 * part : 16 * part + 16]
    level.relax(oa, ob, source_one, faces, 4 * 16, 12 * 16)
    level.relax(ob, oa, source_one, faces, 5 * 16, 10 * 16)
    value = oa[16 + 80 : 16 + 240]
    spread[pl.ds(0, 160, stride=2), :] = value
    spread[pl.ds(1, 160, stride=2), :] = value
    for z in range(10, 30):
        at = ((z - 10) // 2) * 32
        va[(z + 1) * WY : (z + 2) * WY] = kept[(z - 10) * WY : (z - 9) * WY] + spread[at : at + WY]
    for z in range(11, 29):
        here, total, weight, _ = fine_plane(va, source, coefs, z_faces, z)
        vb[(z + 1) * WY : (z + 2) * WY] = 0.2 * here + weight * total
    for z in range(12, 28):
        here, total, weight, _ = fine_plane(vb, source, coefs, z_faces, z, 8, 8)
        out[z - 12] = 0.2 * here + weight * total
        if last and z in (19, 27):
            copies[z // 27].start()
    if last:
        for copy in copies:
            copy.wait()
    else:
        top = 16 - FIELD_HALO
        mate[...] = out[pl.ds(jnp.where(even_z, top, 0), FIELD_HALO)]
        other[...] = out[pl.ds(jnp.where(even_z, 0, top), FIELD_HALO)]


def floats(*shape):
    return jax.ShapeDtypeStruct(shape, jnp.float32)


def call(body, outs, scratch, args, inputs=pltpu.VMEM, outputs=pltpu.VMEM):
    return pl.pallas_call(
        body,
        out_shape=outs,
        in_specs=[pl.BlockSpec(memory_space=pltpu.SMEM)] + [pl.BlockSpec(memory_space=inputs)] * (len(args) - 1),
        out_specs=[pl.BlockSpec(memory_space=outputs)] * len(outs),
        scratch_shapes=[pltpu.VMEM(s, jnp.float32) if isinstance(s, tuple) else s for s in scratch],
        compiler_params=pltpu.CompilerParams(vmem_limit_bytes=VMEM_BYTES),
    )(*args)


FIELD = ((WZ + 2) * WY, 128)
SHARED = [(WZ * WY, 128), (BLOCKS, 11, WY, 128), (BLOCKS + 1, WY, 128), (6, 352, 128)]
Z_AXIS = ("gz",)
Y_AXIS = ("gx", "core")


def down(index, arrays, shared):
    first = shared is None
    copies = lax.axis_size("gz") * lax.axis_size("gx")
    outs = [
        floats(copies * (4 if first else 2), 128),
        floats(80, 128),
        floats(20 * WY, 128),
        floats(320, 128),
        floats(352, 128),
    ]
    scratch = [FIELD, FIELD, (640, 128), (352, 128), (128, 128)]
    if first:
        outs += [floats(*shape) for shape in SHARED]
        scratch += [(16 + BLOCKS * WY, 128), (320, 128), (160, 128), (352, 128)]
        args = [index, *arrays]
    else:
        args = [index, *arrays, *shared]
    result = call(lambda *refs: down_body(first, copies, *refs), outs, scratch, args)
    return result[0], result[1], result[2:5], result[5:] if first else shared


def coarse(index, gathered, faces):
    first = faces is None
    z_devices = lax.axis_size("gz")
    levels = coarse_levels()
    outs, scratch = [floats(48, 128)], []
    if first:
        outs += [floats(6, *level.shape()) for level in levels]
    for level in levels:
        scratch += [level.shape(), level.shape(), (level.rows, 128), (level.rows, 128)]
    cut = (SPAN * (16 if first else 8), 128)
    scratch = scratch[:11] + [cut, cut]
    if first:
        scratch += [level.shape() for level in levels]
    args = [index, *gathered] + ([] if first else list(faces))
    near, *new = call(lambda *refs: coarse_body(first, z_devices, *refs), outs, scratch, args)
    return near, new if first else faces


def up(index, shared, near, edges, kept, last):
    outs = [floats(16, 8, 128)] + ([] if last else [floats(FIELD_HALO, 8, 128)] * 2)
    scratch = [FIELD, FIELD, (320, 128), (352, 128), (352, 128)]
    if last:
        scratch += [(16, 8, 128), pltpu.SemaphoreType.DMA((2,))]
    args = [index, *shared, near, *edges, *kept]
    return call(
        lambda *refs: up_body(last, *refs), outs, scratch, args, outputs=pltpu.HBM if last else pltpu.VMEM
    )


def mate_of(i):
    return i + 1 if i % 2 == 0 else i - 1


def other_of(i):
    return i - 1 if i % 2 == 0 else i + 1


def swap(array, axis, partner):
    count = 1
    for name in axis:
        count *= lax.axis_size(name)
    return lax.ppermute(array, axis, [(i, partner(i) % count) for i in range(count)])


def swaps(mate, other, axis):
    far = far_in_y(other) if axis == Y_AXIS else swap(other, axis, other_of)
    return swap(mate, axis, mate_of), far


def far_in_y(array):
    y_devices = lax.axis_size("gx") * lax.axis_size("core")
    pairs = []
    for z in range(lax.axis_size("gz")):
        for y in range(y_devices):
            at = other_of(y)
            target = z * y_devices + at if 0 <= at < y_devices else mate_of(z) * y_devices + y
            pairs.append((z * y_devices + y, target))
    return lax.ppermute(array, ("gz", "gx", "core"), pairs)


def to_all(copies):
    peers = lax.axis_size("gz") * lax.axis_size("gx")
    copies = copies.reshape(peers, copies.shape[0] // peers, 128)
    out = lax.all_to_all(copies, ("gz", "gx"), 0, 0)
    out = out.reshape(out.shape[0] * out.shape[1], 128)
    return out, swap(out, Y_AXIS, mate_of)


def stack(index, parts, own, halo):
    even = index[0] % 2 == 0
    mate, other = parts
    before, after = jnp.where(even, other, mate), jnp.where(even, mate, other)
    pieces = [before[:halo], own[0], after[:halo]]
    if len(own) > 1:
        pieces += [before[halo:], own[1], after[halo:]]
    return jnp.concatenate(pieces, axis=0)


def cycle(index, arrays, shared, coarse_faces, last):
    copies, edge, kept, shared = down(index, arrays, shared)
    edges = swaps(edge, edge, Y_AXIS)
    gathered = to_all(copies)
    near, coarse_faces = coarse(index, gathered, coarse_faces)
    return up(index, shared, near, edges, kept, last), shared, coarse_faces


def per_device(concentration, phases, grains, grain_class, diffusivity):
    y_device = lax.axis_index("gx") * lax.axis_size("core") + lax.axis_index("core")
    index = jnp.stack([lax.axis_index("gz"), y_device]).astype(jnp.int32)
    plane = (4,) + phases.shape[1:]
    blocks = (4, 4) + phases.shape[1:]
    part = floats(HALO + 1, 8, 128)
    kappa, block, *parts = call(
        kappa_body,
        [floats(1, 8, 128), floats(*phases.shape), part, part],
        [
            pltpu.SMEM(grain_class.shape, jnp.int32),
            pltpu.SMEM(diffusivity.shape, jnp.float32),
            pltpu.VMEM(plane, jnp.int32),
            pltpu.VMEM(plane, jnp.int32),
            pltpu.SemaphoreType.DMA((7,)),
        ],
        [index] + [
            pltpu.with_memory_space_constraint(array, pltpu.HBM)
            for array in (grain_class, diffusivity, phases.reshape(blocks), grains.reshape(blocks), concentration)
        ],
        pltpu.HBM,
    )
    own = stack(index, swaps(*parts, Z_AXIS), (block, kappa), HALO)
    mate, other = swaps(own, own, Y_AXIS)
    (field, *parts), shared, faces = cycle(index, (mate, own, other), None, None, False)

    own = stack(index, swaps(*parts, Z_AXIS), (field,), FIELD_HALO)
    mate, other = swaps(own, own, Y_AXIS)
    return cycle(index, (mate, own, other), shared, faces, True)[0][0]


def solution(mesh):
    z_devices, y_devices = mesh.shape["gz"], mesh.shape["gy"]
    cores = jax.sharding.Mesh(mesh.devices.reshape(z_devices, y_devices // 2, 2), ("gz", "gx", "core"))
    split = P("gz", ("gx", "core"), None)
    return jax.shard_map(
        per_device, mesh=cores, in_specs=(split, split, split, P(), P()), out_specs=split, check_vma=False
    )
```

```python
import jax
import jax.numpy as jnp
from jax import lax
from jax.experimental import pallas as pl
from jax.experimental.pallas import tpu as pltpu
from jax.sharding import PartitionSpec as P

HALO = 10
FIELD_HALO = 11
WZ = 40
BLOCKS = 10
WY = 24
NEAR = 9
SPAN = 20
VMEM_BYTES = 48 * 1024 * 1024


def harmonic(near_k, far_k):
    return 2.0 * near_k * far_k / (near_k + far_k)


def dot(left, right):
    return jnp.dot(left, right, precision=lax.Precision.HIGHEST, preferred_element_type=jnp.float32)


def iota(rows, dim, lanes=128):
    return lax.broadcasted_iota(jnp.int32, (rows, lanes), dim)


def matrix(condition, value):
    return jnp.where(condition, jnp.float32(value), jnp.float32(0.0))


def lane_map(make):
    return make(iota(128, 0), iota(128, 1))


class Level:
    def __init__(self, planes, ny, zl, step, span, pad, y_start, y_total, chunk):
        self.planes, self.ny, self.zl, self.step, self.span, self.pad = planes, ny, zl, step, span, pad
        self.y_start, self.y_total = y_start, y_total
        self.rows = planes * ny
        self.chunk = min(chunk, self.rows)

    def chunks(self, start=0, count=None):
        count = self.rows if count is None else count
        at = start
        while at < start + count:
            size = min(self.chunk, start + count - at)
            yield at, size
            at += size

    def neighbours(self, ref, at, size):
        base = self.pad + at
        here = ref[base : base + size]
        below = ref[base - self.ny : base - self.ny + size]
        above = ref[base + self.ny : base + self.ny + size]
        if self.zl > 1:
            width = 128 // self.zl
            lane = iota(size, 1)
            below = pltpu.roll(jnp.where(lane >= 128 - width, below, here), width, 1)
            above = pltpu.roll(jnp.where(lane < width, above, here), 128 - width, 1)
        return (
            here,
            (
                below,
                above,
                ref[base - 1 : base - 1 + size],
                ref[base + 1 : base + 1 + size],
                pltpu.roll(here, self.step, 1),
            ),
        )

    def close(self, ref, value):
        edge = jnp.full((self.pad, 128), value, jnp.float32)
        ref[0 : self.pad] = edge
        ref[self.pad + self.rows : 2 * self.pad + self.rows] = edge

    def shape(self):
        return (self.rows + 2 * self.pad, 128)

    def build(self, kappa, faces):
        for number in (0, 2):
            self.close(faces.at[number], 0.0)
        for at, size in self.chunks():
            here, around = self.neighbours(kappa, at, size)
            y = (iota(size, 0) & (self.ny - 1)) + self.y_start
            x = iota(size, 1) & (self.span - 1)
            rows = slice(self.pad + at, self.pad + at + size)
            faces[0, rows] = harmonic(here, around[0])
            faces[2, rows] = jnp.where((y != 0) & (y != self.y_total), harmonic(here, around[2]), 0.0)
            faces[3, rows] = jnp.where(x >= self.step, harmonic(here, around[4]), 0.0)
        for at, size in self.chunks():
            rows = slice(self.pad + at, self.pad + at + size)
            z_low, around = self.neighbours(faces.at[0], at, size)
            z_high = around[1]
            y_high = faces[2, self.pad + at + 1 : self.pad + at + 1 + size]
            x_low = faces[3, rows]
            total = 1.0 + z_low + z_high + faces[2, rows] + y_high + x_low + pltpu.roll(x_low, 128 - self.step, 1)
            faces[1, rows] = z_high
            faces[4, rows] = 0.8 / total
            faces[5, rows] = total

    def coupled(self, field, source, faces, at, size):
        here, around = self.neighbours(field, at, size)
        rows = slice(self.pad + at, self.pad + at + size)
        next_rows = slice(self.pad + at + 1, self.pad + at + 1 + size)
        x_low = faces[3, rows]
        total = (
            source[at : at + size]
            + faces[0, rows] * around[0]
            + faces[1, rows] * around[1]
            + faces[2, rows] * around[2]
            + faces[2, next_rows] * around[3]
            + x_low * around[4]
            + pltpu.roll(x_low * here, 128 - self.step, 1)
        )
        return here, total

    def start(self, field, source, faces):
        for at, size in self.chunks():
            rows = slice(self.pad + at, self.pad + at + size)
            field[rows] = faces[4, rows] * source[at : at + size]

    def relax(self, field, target, source, faces, start=0, count=None):
        for at, size in self.chunks(start, count):
            here, total = self.coupled(field, source, faces, at, size)
            rows = slice(self.pad + at, self.pad + at + size)
            target[rows] = 0.2 * here + faces[4, rows] * total

    def defect(self, field, source, faces, out, start=0, count=None):
        for at, size in self.chunks(start, count):
            here, total = self.coupled(field, source, faces, at, size)
            diagonal = faces[5, self.pad + at : self.pad + at + size]
            out[at - start : at - start + size] = total - diagonal * here

    def pairs(self, ref):
        half = self.rows // 2
        return ref[pl.ds(0, half, stride=2), :] + ref[pl.ds(1, half, stride=2), :]


def coarsen(value, step, zl=1):
    lane = iota(value.shape[0], 1)
    value = value + jnp.where((lane & step) == 0, pltpu.roll(value, 128 - step, 1), pltpu.roll(value, step, 1))
    if zl == 4:
        value = value + jnp.where((lane & 32) == 0, pltpu.roll(value, 96, 1), pltpu.roll(value, 32, 1))
    if zl == 2:
        value = value + pltpu.roll(value, 64, 1)
    return 0.125 * value


def parities(index):
    return index[0] % 2 == 0, index[1] % 2 == 0


def kappa_body(index, class_hbm, diff_hbm, phases_hbm, grains_hbm, conc_hbm, kappa_ref, own_ref, mate_ref, other_ref, classes, diff, phases, grains, sems):
    even, _ = parities(index)
    num_phases, num_classes = diff.shape
    pairs = [(class_hbm, classes), (diff_hbm, diff)]
    pairs += [(phases_hbm.at[:, 0], phases), (grains_hbm.at[:, 0], grains)]
    top = 16 - HALO
    pairs += [
        (conc_hbm.at[pl.ds(jnp.where(even, top, 0), HALO)], mate_ref.at[0:HALO]),
        (conc_hbm.at[pl.ds(jnp.where(even, 0, top), HALO)], other_ref.at[0:HALO]),
        (conc_hbm, own_ref),
    ]
    copies = [pltpu.make_async_copy(source, target, sems.at[i]) for i, (source, target) in enumerate(pairs)]
    for copy in copies:
        copy.start()
    for copy in copies[:-3]:
        copy.wait()
    halves = [(block, slice(4 * half, 4 * half + 1)) for block in range(4) for half in range(2)]
    grain = jnp.concatenate([grains[at] for at in halves], axis=0)
    phase = jnp.concatenate([phases[at] for at in halves], axis=0)
    cls = jnp.zeros(grain.shape, jnp.int32)
    for number in range(classes.shape[0]):
        cls = jnp.where(grain == number, classes[number], cls)
    value = jnp.ones(grain.shape, jnp.float32)
    for p in range(num_phases):
        for c in range(num_classes):
            value = jnp.where((phase == p) & (cls == c), diff[p, c], value)
    kappa_ref[0] = value
    mate_ref[HALO] = value
    other_ref[HALO] = value
    for copy in copies[-3:]:
        copy.wait()


def window(refs, plane, even):
    mate, own, other = (ref[plane] for ref in refs)
    return jnp.concatenate([jnp.where(even, other, mate), own, jnp.where(even, mate, other)], axis=0)


def build_fine(sources, even, y_device, kappa, coefs, z_faces):
    kappa[0:8] = jnp.ones((8, 128), jnp.float32)
    kappa[8 + BLOCKS * WY : 16 + BLOCKS * WY] = jnp.ones((8, 128), jnp.float32)
    for block in range(BLOCKS):
        plane, number = divmod(block + 1, 4)
        two = slice(2 * number, 2 * number + 2)
        mate, own, other = (ref[16 + 2 * HALO + plane, two] for ref in sources)
        rows = (jnp.where(even, other, mate), own, jnp.where(even, mate, other))
        kappa[8 + block * WY : 8 + (block + 1) * WY] = jnp.concatenate(
            [jnp.broadcast_to(pair[half : half + 1], (4, 128)) for pair in rows for half in range(2)], axis=0
        )
    y = iota(WY, 0) + y_device * 8 - 8
    x = iota(WY, 1)
    for block in range(BLOCKS + 1):
        low, high = max(block - 1, 0), min(block, BLOCKS - 1)
        z_faces[block] = harmonic(
            kappa[8 + low * WY : 8 + (low + 1) * WY], kappa[8 + high * WY : 8 + (high + 1) * WY]
        )
    for block in range(BLOCKS):
        at = 8 + block * WY
        k = kappa[at : at + WY]
        y_low = jnp.where(y == 0, 0.0, harmonic(k, kappa[at - 1 : at - 1 + WY]))
        y_high = jnp.where(y == 63, 0.0, harmonic(k, kappa[at + 1 : at + 1 + WY]))
        x_low = jnp.where(x == 0, 0.0, harmonic(k, pltpu.roll(k, 1, 1)))
        x_high = jnp.where(x == 127, 0.0, harmonic(k, pltpu.roll(k, 127, 1)))
        sides = 1.0 + y_low + y_high + x_low + x_high
        diagonals = (sides + z_faces[block] + k, sides + k + k, sides + k + z_faces[block + 1])
        for number, value in enumerate((k, y_low, y_high, x_low, x_high)):
            coefs[block, number] = value
        for number, value in enumerate(diagonals):
            coefs[block, 5 + number] = 0.8 / value
            coefs[block, 8 + number] = value


def fine_plane(field, source, coefs, z_faces, z, low=0, size=WY):
    block, p = divmod(z, 4)
    rows = slice(low, low + size)
    at = WY + z * WY + low
    here = field[at : at + size]
    k = coefs[block, 0, rows]
    below = z_faces[block, rows] if p == 0 else k
    above = z_faces[block + 1, rows] if p == 3 else k
    total = (
        source[z * WY + low : z * WY + low + size]
        + below * field[at - WY : at - WY + size]
        + above * field[at + WY : at + WY + size]
        + coefs[block, 1, rows] * field[at - 1 : at - 1 + size]
        + coefs[block, 2, rows] * field[at + 1 : at + 1 + size]
        + coefs[block, 3, rows] * pltpu.roll(here, 1, 1)
        + coefs[block, 4, rows] * pltpu.roll(here, 127, 1)
    )
    kind = (0, 1, 1, 2)[p]
    return here, total, coefs[block, 5 + kind, rows], coefs[block, 8 + kind, rows]


def level_one(y_device):
    return Level(20, 16, 1, 2, 128, 16, y_device * 4 - 4, 32, 160)


def build_one(level, kappa, spread, packed, kappa_one, faces):
    for block in range(BLOCKS):
        spread[block * 32 : block * 32 + WY] = kappa[8 + block * WY : 8 + (block + 1) * WY]
        spread[block * 32 + WY : block * 32 + 32] = jnp.ones((32 - WY, 128), jnp.float32)
    packed[...] = 0.5 * spread[pl.ds(0, BLOCKS * 16, stride=2), :]
    level.close(kappa_one, 1.0)
    for block in range(BLOCKS):
        value = packed[block * 16 : block * 16 + 16]
        kappa_one[16 + block * 32 : 32 + block * 32] = value
        kappa_one[32 + block * 32 : 48 + block * 32] = value
    level.build(kappa_one, faces)


def to_chunk(rows):
    group = iota(8, 1) >> 5
    out = rows[0:8]
    for z in range(1, 4):
        out = jnp.where(group == z, rows[8 * z : 8 * z + 8], out)
    return out


def down_body(first, copies, *refs):
    index, refs = refs[0], refs[1:]
    if first:
        sources, refs = refs[:3], refs[3:]
    else:
        fields, (source, coefs, z_faces, faces), refs = refs[:3], refs[3:7], refs[7:]
    chunk, edge, kept, source_one, kept_one = refs[:5]
    refs = refs[5:]
    if first:
        (source, coefs, z_faces, faces), refs = refs[:4], refs[4:]
    va, vb, rs, oa, tmp = refs[:5]
    _, even = parities(index)
    y_device = index[1]
    level = level_one(y_device)
    if first:
        kappa, spread, packed, kappa_one = refs[5:]
        build_fine(sources, even, y_device, kappa, coefs, z_faces)
        build_one(level, kappa, spread, packed, kappa_one, faces)
    zero = jnp.zeros((WY, 128), jnp.float32)
    for ref in (va, vb):
        ref[0:WY] = zero
        ref[(WZ + 1) * WY : (WZ + 2) * WY] = zero
    if first:
        for z in range(WZ):
            kind = (0, 1, 1, 2)[z % 4]
            inside = 0 <= z + HALO - 12 < 16 + 2 * HALO
            value = window(sources, z + HALO - 12, even) if inside else zero
            source[z * WY : (z + 1) * WY] = value
            va[(z + 1) * WY : (z + 2) * WY] = coefs[z // 4, 5 + kind] * value
    else:
        for z in range(1, WZ - 1):
            vb[(z + 1) * WY : (z + 2) * WY] = window(fields, z - 1, even)
        for z in range(2, WZ - 2):
            here, total, weight, _ = fine_plane(vb, source, coefs, z_faces, z)
            va[(z + 1) * WY : (z + 2) * WY] = 0.2 * here + weight * total
    for z in range(3, WZ - 3):
        here, total, weight, _ = fine_plane(va, source, coefs, z_faces, z)
        value = 0.2 * here + weight * total
        vb[(z + 1) * WY : (z + 2) * WY] = value
        if 10 <= z < 30:
            kept[(z - 10) * WY : (z - 9) * WY] = value
    for plane in range(20):
        if 2 <= plane < 18:
            total_defect = 0.0
            for z in (2 * plane, 2 * plane + 1):
                here, total, _, diagonal = fine_plane(vb, source, coefs, z_faces, z)
                total_defect = total_defect + (total - diagonal * here)
            rs[plane * 32 : plane * 32 + WY] = total_defect
            rs[plane * 32 + WY : plane * 32 + 32] = jnp.zeros((32 - WY, 128), jnp.float32)
        else:
            rs[plane * 32 : plane * 32 + 32] = jnp.zeros((32, 128), jnp.float32)
    source_one[...] = coarsen(rs[pl.ds(0, 320, stride=2), :] + rs[pl.ds(1, 320, stride=2), :], 1)
    for ref in (oa, kept_one):
        level.close(ref, 0.0)
    level.start(oa, source_one, faces)
    level.relax(oa, kept_one, source_one, faces)
    level.defect(kept_one, source_one, faces, tmp, 6 * 16, 8 * 16)
    for z in range(4):
        tmp[z * 16 : z * 16 + 16] = tmp[z * 32 : z * 32 + 16] + tmp[z * 32 + 16 : z * 32 + 32]
    halves = tmp[pl.ds(0, 32, stride=2), :] + tmp[pl.ds(1, 32, stride=2), :]
    mean_two = lane_map(lambda r, c: matrix(((r & 1) == 0) & (r >> 2 == (c & 31)), 0.125))
    values = [to_chunk(dot(halves, mean_two))[2:4]]
    if first:
        pick_two = lane_map(lambda r, c: matrix(r == 4 * (c & 31), 0.5))
        values.append(to_chunk(dot(packed[pl.ds(48, 32, stride=2), :], pick_two))[2:4])
    repeats = 4 // len(values)
    tile = jnp.concatenate(values * repeats, axis=0)
    for at in range(0, copies // repeats):
        chunk[at * 8 : at * 8 + 8] = tile
    for plane in range(20):
        edge[plane * 4 : plane * 4 + 4] = kept_one[16 + plane * 16 + 4 : 16 + plane * 16 + 8]


def coarse_levels():
    return (
        Level(SPAN, 16, 4, 1, 32, 16, 0, 16, 160),
        Level(SPAN, 8, 2, 2, 32, 8, 0, 8, 160),
        Level(SPAN, 4, 1, 4, 32, 8, 0, 4, 128),
    )


def coarse_body(first, z_devices, *refs):
    two, three, four = coarse_levels()
    index, same, mate = refs[:3]
    refs = refs[3:]
    if first:
        near, f2, f3, f4 = refs[:4]
    else:
        f2, f3, f4, near = refs[:4]
    a2, b2, g2, r2, a3, b3, g3, r3, a4, b4, g4, cut_same, cut_mate = refs[4:17]
    z_device = index[0]
    even = index[1] % 2 == 0
    per = 4 if first else 2
    rows = 4 * per
    for number in range(SPAN):
        at = lax.rem(z_device + (number - NEAR + 4 * z_devices), z_devices) * rows
        at = pl.multiple_of(at, 8)
        cut_same[number * rows : (number + 1) * rows] = same[pl.ds(at, rows), :]
        cut_mate[number * rows : (number + 1) * rows] = mate[pl.ds(at, rows), :]

    def interleave(target, start, part):
        for y in range(2):
            take = pl.ds(part + y, 4 * SPAN, stride=per)
            one, two_ = cut_same[take, :], cut_mate[take, :]
            target[pl.ds(start + y, 4 * SPAN, stride=4), :] = jnp.where(even, one, two_)
            target[pl.ds(start + 2 + y, 4 * SPAN, stride=4), :] = jnp.where(even, two_, one)

    interleave(g2, 0, 0)
    if first:
        k2, k3, k4 = refs[17:]
        interleave(k2, two.pad, 2)
        two.close(k2, 1.0)
        two.build(k2, f2)
        r2[...] = k2[two.pad : two.pad + two.rows]
        k3[three.pad : three.pad + three.rows] = 0.5 * coarsen(two.pairs(r2), 1, 4)
        three.close(k3, 1.0)
        three.build(k3, f3)
        r3[...] = k3[three.pad : three.pad + three.rows]
        k4[four.pad : four.pad + four.rows] = 0.5 * coarsen(three.pairs(r3), 2, 2)
        four.close(k4, 1.0)
        four.build(k4, f4)
    for level, fields in ((two, (a2, b2)), (three, (a3, b3)), (four, (a4, b4))):
        for field in fields:
            level.close(field, 0.0)

    two.start(a2, g2, f2)
    two.relax(a2, b2, g2, f2)
    two.defect(b2, g2, f2, r2)
    g3[...] = coarsen(two.pairs(r2), 1, 4)
    three.start(a3, g3, f3)
    three.relax(a3, b3, g3, f3)
    three.defect(b3, g3, f3, r3)
    g4[...] = coarsen(three.pairs(r3), 2, 2)
    four.start(a4, g4, f4)
    for _ in range(2):
        four.relax(a4, b4, g4, f4)
        four.relax(b4, a4, g4, f4)
    four.relax(a4, b4, g4, f4)

    def correct(level, field, start, count, value, tmp):
        tmp[pl.ds(0, count // 2, stride=2), :] = value
        tmp[pl.ds(1, count // 2, stride=2), :] = value
        inner = slice(level.pad + start, level.pad + start + count)
        field[inner] = field[inner] + tmp[0:count]

    low = NEAR - 3
    correct(three, b3, 8 * low, 48, b4[four.pad + 4 * low : four.pad + 4 * low + 24], r3)
    three.relax(b3, a3, g3, f3, 8 * low, 48)
    low = NEAR - 1
    three.relax(a3, b3, g3, f3, 8 * low, 24)
    correct(two, b2, 16 * low, 48, b3[three.pad + 8 * low : three.pad + 8 * low + 24], r2)
    two.relax(b2, a2, g2, f2, 16 * low, 48)
    two.relax(a2, b2, g2, f2, 16 * low, 48)
    near[...] = b2[two.pad + 16 * low : two.pad + 16 * low + 48]


def up_body(last, *refs):
    index, source, coefs, z_faces, faces, near, edge_mate, edge_other, kept, source_one, kept_one, out = refs[:12]
    refs = refs[12:]
    if last:
        out_hbm, (out, sems), refs = out, refs[-2:], refs[:-2]
        quarters = [slice(4 * i, 4 * i + 4) for i in range(4)]
        copies = [
            pltpu.make_async_copy(out.at[part], out_hbm.at[part], sems.at[i]) for i, part in enumerate(quarters)
        ]
    else:
        (mate, other), refs = refs[:2], refs[2:]
    va, vb, spread, oa, ob = refs
    even_z, even = parities(index)
    y_device = index[1]
    level = level_one(y_device)
    rows = matrix(iota(16, 1, 16) == y_device * 2 - 2 + (iota(16, 0, 16) >> 1), 1.0)
    spread_y = jnp.concatenate([dot(rows, near[16 * part : 16 * part + 16]) for part in range(3)], axis=0)
    by_z = [
        dot(spread_y, lane_map(lambda r, c, z=z: matrix(r == z * 32 + (c >> 2), 1.0))) for z in range(4)
    ]
    for plane in range(20):
        part, z = divmod(plane // 2 + 1, 4)
        at = 16 + plane * 16
        one, two = edge_mate[plane * 4 : plane * 4 + 4], edge_other[plane * 4 : plane * 4 + 4]
        field = jnp.concatenate(
            [jnp.where(even, two, one), kept_one[at + 4 : at + 8], jnp.where(even, one, two),
             jnp.zeros((4, 128), jnp.float32)], axis=0
        )
        oa[at : at + 16] = field + by_z[z][16 * part : 16 * part + 16]
    level.relax(oa, ob, source_one, faces, 4 * 16, 12 * 16)
    level.relax(ob, oa, source_one, faces, 5 * 16, 10 * 16)
    value = oa[16 + 80 : 16 + 240]
    spread[pl.ds(0, 160, stride=2), :] = value
    spread[pl.ds(1, 160, stride=2), :] = value
    for z in range(10, 30):
        at = ((z - 10) // 2) * 32
        va[(z + 1) * WY : (z + 2) * WY] = kept[(z - 10) * WY : (z - 9) * WY] + spread[at : at + WY]
    for z in range(11, 29):
        here, total, weight, _ = fine_plane(va, source, coefs, z_faces, z)
        vb[(z + 1) * WY : (z + 2) * WY] = 0.2 * here + weight * total
    for z in range(12, 28):
        here, total, weight, _ = fine_plane(vb, source, coefs, z_faces, z, 8, 8)
        out[z - 12] = 0.2 * here + weight * total
        if last and z % 4 == 3:
            copies[(z - 12) // 4].start()
    if last:
        for copy in copies:
            copy.wait()
    else:
        top = 16 - FIELD_HALO
        mate[...] = out[pl.ds(jnp.where(even_z, top, 0), FIELD_HALO)]
        other[...] = out[pl.ds(jnp.where(even_z, 0, top), FIELD_HALO)]


def floats(*shape):
    return jax.ShapeDtypeStruct(shape, jnp.float32)


def call(body, outs, scratch, args, inputs=pltpu.VMEM, outputs=pltpu.VMEM):
    return pl.pallas_call(
        body,
        out_shape=outs,
        in_specs=[pl.BlockSpec(memory_space=pltpu.SMEM)] + [pl.BlockSpec(memory_space=inputs)] * (len(args) - 1),
        out_specs=[pl.BlockSpec(memory_space=outputs)] * len(outs),
        scratch_shapes=[pltpu.VMEM(s, jnp.float32) if isinstance(s, tuple) else s for s in scratch],
        compiler_params=pltpu.CompilerParams(vmem_limit_bytes=VMEM_BYTES),
    )(*args)


FIELD = ((WZ + 2) * WY, 128)
SHARED = [(WZ * WY, 128), (BLOCKS, 11, WY, 128), (BLOCKS + 1, WY, 128), (6, 352, 128)]
Z_AXIS = ("gz",)
Y_AXIS = ("gx", "core")


def down(index, arrays, shared):
    first = shared is None
    copies = lax.axis_size("gz") * lax.axis_size("gx")
    outs = [
        floats(copies * (4 if first else 2), 128),
        floats(80, 128),
        floats(20 * WY, 128),
        floats(320, 128),
        floats(352, 128),
    ]
    scratch = [FIELD, FIELD, (640, 128), (352, 128), (128, 128)]
    if first:
        outs += [floats(*shape) for shape in SHARED]
        scratch += [(16 + BLOCKS * WY, 128), (320, 128), (160, 128), (352, 128)]
        args = [index, *arrays]
    else:
        args = [index, *arrays, *shared]
    result = call(lambda *refs: down_body(first, copies, *refs), outs, scratch, args)
    return result[0], result[1], result[2:5], result[5:] if first else shared


def coarse(index, gathered, faces):
    first = faces is None
    z_devices = lax.axis_size("gz")
    levels = coarse_levels()
    outs, scratch = [floats(48, 128)], []
    if first:
        outs += [floats(6, *level.shape()) for level in levels]
    for level in levels:
        scratch += [level.shape(), level.shape(), (level.rows, 128), (level.rows, 128)]
    cut = (SPAN * (16 if first else 8), 128)
    scratch = scratch[:11] + [cut, cut]
    if first:
        scratch += [level.shape() for level in levels]
    args = [index, *gathered] + ([] if first else list(faces))
    near, *new = call(lambda *refs: coarse_body(first, z_devices, *refs), outs, scratch, args)
    return near, new if first else faces


def up(index, shared, near, edges, kept, last):
    outs = [floats(16, 8, 128)] + ([] if last else [floats(FIELD_HALO, 8, 128)] * 2)
    scratch = [FIELD, FIELD, (320, 128), (352, 128), (352, 128)]
    if last:
        scratch += [(16, 8, 128), pltpu.SemaphoreType.DMA((4,))]
    args = [index, *shared, near, *edges, *kept]
    return call(
        lambda *refs: up_body(last, *refs), outs, scratch, args, outputs=pltpu.HBM if last else pltpu.VMEM
    )


def mate_of(i):
    return i + 1 if i % 2 == 0 else i - 1


def other_of(i):
    return i - 1 if i % 2 == 0 else i + 1


def swap(array, axis, partner):
    count = 1
    for name in axis:
        count *= lax.axis_size(name)
    return lax.ppermute(array, axis, [(i, partner(i) % count) for i in range(count)])


def swaps(mate, other, axis):
    far = far_in_y(other) if axis == Y_AXIS else swap(other, axis, other_of)
    return swap(mate, axis, mate_of), far


def far_in_y(array):
    y_devices = lax.axis_size("gx") * lax.axis_size("core")
    pairs = []
    for z in range(lax.axis_size("gz")):
        for y in range(y_devices):
            at = other_of(y)
            target = z * y_devices + at if 0 <= at < y_devices else mate_of(z) * y_devices + y
            pairs.append((z * y_devices + y, target))
    return lax.ppermute(array, ("gz", "gx", "core"), pairs)


def to_all(copies):
    peers = lax.axis_size("gz") * lax.axis_size("gx")
    copies = copies.reshape(peers, copies.shape[0] // peers, 128)
    out = lax.all_to_all(copies, ("gz", "gx"), 0, 0)
    out = out.reshape(out.shape[0] * out.shape[1], 128)
    return out, swap(out, Y_AXIS, mate_of)


def stack(index, parts, own, halo):
    even = index[0] % 2 == 0
    mate, other = parts
    before, after = jnp.where(even, other, mate), jnp.where(even, mate, other)
    pieces = [before[:halo], own[0], after[:halo]]
    if len(own) > 1:
        pieces += [before[halo:], own[1], after[halo:]]
    return jnp.concatenate(pieces, axis=0)


def cycle(index, arrays, shared, coarse_faces, last):
    copies, edge, kept, shared = down(index, arrays, shared)
    edges = swaps(edge, edge, Y_AXIS)
    gathered = to_all(copies)
    near, coarse_faces = coarse(index, gathered, coarse_faces)
    return up(index, shared, near, edges, kept, last), shared, coarse_faces


def per_device(concentration, phases, grains, grain_class, diffusivity):
    y_device = lax.axis_index("gx") * lax.axis_size("core") + lax.axis_index("core")
    index = jnp.stack([lax.axis_index("gz"), y_device]).astype(jnp.int32)
    plane = (4,) + phases.shape[1:]
    blocks = (4, 4) + phases.shape[1:]
    part = floats(HALO + 1, 8, 128)
    kappa, block, *parts = call(
        kappa_body,
        [floats(1, 8, 128), floats(*phases.shape), part, part],
        [
            pltpu.SMEM(grain_class.shape, jnp.int32),
            pltpu.SMEM(diffusivity.shape, jnp.float32),
            pltpu.VMEM(plane, jnp.int32),
            pltpu.VMEM(plane, jnp.int32),
            pltpu.SemaphoreType.DMA((7,)),
        ],
        [index] + [
            pltpu.with_memory_space_constraint(array, pltpu.HBM)
            for array in (grain_class, diffusivity, phases.reshape(blocks), grains.reshape(blocks), concentration)
        ],
        pltpu.HBM,
    )
    own = stack(index, swaps(*parts, Z_AXIS), (block, kappa), HALO)
    mate, other = swaps(own, own, Y_AXIS)
    (field, *parts), shared, faces = cycle(index, (mate, own, other), None, None, False)

    own = stack(index, swaps(*parts, Z_AXIS), (field,), FIELD_HALO)
    mate, other = swaps(own, own, Y_AXIS)
    return cycle(index, (mate, own, other), shared, faces, True)[0][0]


def solution(mesh):
    z_devices, y_devices = mesh.shape["gz"], mesh.shape["gy"]
    cores = jax.sharding.Mesh(mesh.devices.reshape(z_devices, y_devices // 2, 2), ("gz", "gx", "core"))
    split = P("gz", ("gx", "core"), None)
    return jax.shard_map(
        per_device, mesh=cores, in_specs=(split, split, split, P(), P()), out_specs=split, check_vma=False
    )
```

```python
import jax
import jax.numpy as jnp
from jax import lax
from jax.experimental import pallas as pl
from jax.experimental.pallas import tpu as pltpu
from jax.sharding import PartitionSpec as P

HALO = 10
FIELD_HALO = 11
WZ = 40
BLOCKS = 10
WY = 24
NEAR = 9
SPAN = 20
VMEM_BYTES = 48 * 1024 * 1024


def harmonic(near_k, far_k):
    return 2.0 * near_k * far_k / (near_k + far_k)


def dot(left, right):
    return jnp.dot(left, right, precision=lax.Precision.HIGHEST, preferred_element_type=jnp.float32)


def iota(rows, dim, lanes=128):
    return lax.broadcasted_iota(jnp.int32, (rows, lanes), dim)


def matrix(condition, value):
    return jnp.where(condition, jnp.float32(value), jnp.float32(0.0))


def lane_map(make):
    return make(iota(128, 0), iota(128, 1))


class Level:
    def __init__(self, planes, ny, zl, step, span, pad, y_start, y_total, chunk):
        self.planes, self.ny, self.zl, self.step, self.span, self.pad = planes, ny, zl, step, span, pad
        self.y_start, self.y_total = y_start, y_total
        self.rows = planes * ny
        self.chunk = min(chunk, self.rows)

    def chunks(self, start=0, count=None):
        count = self.rows if count is None else count
        at = start
        while at < start + count:
            size = min(self.chunk, start + count - at)
            yield at, size
            at += size

    def neighbours(self, ref, at, size):
        base = self.pad + at
        here = ref[base : base + size]
        below = ref[base - self.ny : base - self.ny + size]
        above = ref[base + self.ny : base + self.ny + size]
        if self.zl > 1:
            width = 128 // self.zl
            lane = iota(size, 1)
            below = pltpu.roll(jnp.where(lane >= 128 - width, below, here), width, 1)
            above = pltpu.roll(jnp.where(lane < width, above, here), 128 - width, 1)
        return (
            here,
            (
                below,
                above,
                ref[base - 1 : base - 1 + size],
                ref[base + 1 : base + 1 + size],
                pltpu.roll(here, self.step, 1),
            ),
        )

    def close(self, ref, value):
        edge = jnp.full((self.pad, 128), value, jnp.float32)
        ref[0 : self.pad] = edge
        ref[self.pad + self.rows : 2 * self.pad + self.rows] = edge

    def shape(self):
        return (self.rows + 2 * self.pad, 128)

    def build(self, kappa, faces):
        for number in (0, 2):
            self.close(faces.at[number], 0.0)
        for at, size in self.chunks():
            here, around = self.neighbours(kappa, at, size)
            y = (iota(size, 0) & (self.ny - 1)) + self.y_start
            x = iota(size, 1) & (self.span - 1)
            rows = slice(self.pad + at, self.pad + at + size)
            faces[0, rows] = harmonic(here, around[0])
            faces[2, rows] = jnp.where((y != 0) & (y != self.y_total), harmonic(here, around[2]), 0.0)
            faces[3, rows] = jnp.where(x >= self.step, harmonic(here, around[4]), 0.0)
        for at, size in self.chunks():
            rows = slice(self.pad + at, self.pad + at + size)
            z_low, around = self.neighbours(faces.at[0], at, size)
            z_high = around[1]
            y_high = faces[2, self.pad + at + 1 : self.pad + at + 1 + size]
            x_low = faces[3, rows]
            total = 1.0 + z_low + z_high + faces[2, rows] + y_high + x_low + pltpu.roll(x_low, 128 - self.step, 1)
            faces[1, rows] = z_high
            faces[4, rows] = 0.8 / total
            faces[5, rows] = total

    def coupled(self, field, source, faces, at, size):
        here, around = self.neighbours(field, at, size)
        rows = slice(self.pad + at, self.pad + at + size)
        next_rows = slice(self.pad + at + 1, self.pad + at + 1 + size)
        x_low = faces[3, rows]
        total = (
            source[at : at + size]
            + faces[0, rows] * around[0]
            + faces[1, rows] * around[1]
            + faces[2, rows] * around[2]
            + faces[2, next_rows] * around[3]
            + x_low * around[4]
            + pltpu.roll(x_low * here, 128 - self.step, 1)
        )
        return here, total

    def start(self, field, source, faces):
        for at, size in self.chunks():
            rows = slice(self.pad + at, self.pad + at + size)
            field[rows] = faces[4, rows] * source[at : at + size]

    def relax(self, field, target, source, faces, start=0, count=None):
        for at, size in self.chunks(start, count):
            here, total = self.coupled(field, source, faces, at, size)
            rows = slice(self.pad + at, self.pad + at + size)
            target[rows] = 0.2 * here + faces[4, rows] * total

    def defect(self, field, source, faces, out, start=0, count=None):
        for at, size in self.chunks(start, count):
            here, total = self.coupled(field, source, faces, at, size)
            diagonal = faces[5, self.pad + at : self.pad + at + size]
            out[at - start : at - start + size] = total - diagonal * here

    def pairs(self, ref):
        half = self.rows // 2
        return ref[pl.ds(0, half, stride=2), :] + ref[pl.ds(1, half, stride=2), :]


def coarsen(value, step, zl=1):
    lane = iota(value.shape[0], 1)
    value = value + jnp.where((lane & step) == 0, pltpu.roll(value, 128 - step, 1), pltpu.roll(value, step, 1))
    if zl == 4:
        value = value + jnp.where((lane & 32) == 0, pltpu.roll(value, 96, 1), pltpu.roll(value, 32, 1))
    if zl == 2:
        value = value + pltpu.roll(value, 64, 1)
    return 0.125 * value


def parities(index):
    return index[0] % 2 == 0, index[1] % 2 == 0


def kappa_body(index, class_hbm, diff_hbm, phases_hbm, grains_hbm, conc_hbm, kappa_ref, own_ref, mate_ref, other_ref, classes, diff, phases, grains, sems):
    even, _ = parities(index)
    num_phases, num_classes = diff.shape
    pairs = [(class_hbm, classes), (diff_hbm, diff)]
    pairs += [(phases_hbm.at[:, 0], phases), (grains_hbm.at[:, 0], grains)]
    top = 16 - HALO
    pairs += [
        (conc_hbm.at[pl.ds(jnp.where(even, top, 0), HALO)], mate_ref.at[0:HALO]),
        (conc_hbm.at[pl.ds(jnp.where(even, 0, top), HALO)], other_ref.at[0:HALO]),
        (conc_hbm, own_ref),
    ]
    copies = [pltpu.make_async_copy(source, target, sems.at[i]) for i, (source, target) in enumerate(pairs)]
    for copy in copies:
        copy.start()
    for copy in copies[:-3]:
        copy.wait()
    grain = grains[...]
    phase = phases[...]
    cls = jnp.zeros(grain.shape, jnp.int32)
    for number in range(classes.shape[0]):
        cls = jnp.where(grain == number, classes[number], cls)
    value = jnp.ones(grain.shape, jnp.float32)
    for p in range(num_phases):
        for c in range(num_classes):
            value = jnp.where((phase == p) & (cls == c), diff[p, c], value)
    rows = jnp.concatenate([value[block, 4 * half : 4 * half + 1] for block in range(4) for half in range(2)], axis=0)
    kappa_ref[0] = rows
    mate_ref[HALO] = rows
    other_ref[HALO] = rows
    for copy in copies[-3:]:
        copy.wait()


def window(refs, plane, even):
    mate, own, other = (ref[plane] for ref in refs)
    return jnp.concatenate([jnp.where(even, other, mate), own, jnp.where(even, mate, other)], axis=0)


def build_fine(sources, even, y_device, kappa, coefs, z_faces):
    kappa[0:8] = jnp.ones((8, 128), jnp.float32)
    kappa[8 + BLOCKS * WY : 16 + BLOCKS * WY] = jnp.ones((8, 128), jnp.float32)
    for block in range(BLOCKS):
        plane, number = divmod(block + 1, 4)
        two = slice(2 * number, 2 * number + 2)
        mate, own, other = (ref[16 + 2 * HALO + plane, two] for ref in sources)
        rows = (jnp.where(even, other, mate), own, jnp.where(even, mate, other))
        kappa[8 + block * WY : 8 + (block + 1) * WY] = jnp.concatenate(
            [jnp.broadcast_to(pair[half : half + 1], (4, 128)) for pair in rows for half in range(2)], axis=0
        )
    y = iota(WY, 0) + y_device * 8 - 8
    x = iota(WY, 1)
    for block in range(BLOCKS + 1):
        low, high = max(block - 1, 0), min(block, BLOCKS - 1)
        z_faces[block] = harmonic(
            kappa[8 + low * WY : 8 + (low + 1) * WY], kappa[8 + high * WY : 8 + (high + 1) * WY]
        )
    for block in range(BLOCKS):
        at = 8 + block * WY
        k = kappa[at : at + WY]
        y_low = jnp.where(y == 0, 0.0, harmonic(k, kappa[at - 1 : at - 1 + WY]))
        y_high = jnp.where(y == 63, 0.0, harmonic(k, kappa[at + 1 : at + 1 + WY]))
        x_low = jnp.where(x == 0, 0.0, harmonic(k, pltpu.roll(k, 1, 1)))
        x_high = jnp.where(x == 127, 0.0, harmonic(k, pltpu.roll(k, 127, 1)))
        sides = 1.0 + y_low + y_high + x_low + x_high
        diagonals = (sides + z_faces[block] + k, sides + k + k, sides + k + z_faces[block + 1])
        for number, value in enumerate((k, y_low, y_high, x_low, x_high)):
            coefs[block, number] = value
        for number, value in enumerate(diagonals):
            coefs[block, 5 + number] = 0.8 / value
            coefs[block, 8 + number] = value


def fine_plane(field, source, coefs, z_faces, z, low=0, size=WY):
    block, p = divmod(z, 4)
    rows = slice(low, low + size)
    at = WY + z * WY + low
    here = field[at : at + size]
    k = coefs[block, 0, rows]
    below = z_faces[block, rows] if p == 0 else k
    above = z_faces[block + 1, rows] if p == 3 else k
    total = (
        source[z * WY + low : z * WY + low + size]
        + below * field[at - WY : at - WY + size]
        + above * field[at + WY : at + WY + size]
        + coefs[block, 1, rows] * field[at - 1 : at - 1 + size]
        + coefs[block, 2, rows] * field[at + 1 : at + 1 + size]
        + coefs[block, 3, rows] * pltpu.roll(here, 1, 1)
        + coefs[block, 4, rows] * pltpu.roll(here, 127, 1)
    )
    kind = (0, 1, 1, 2)[p]
    return here, total, coefs[block, 5 + kind, rows], coefs[block, 8 + kind, rows]


def level_one(y_device):
    return Level(20, 16, 1, 2, 128, 16, y_device * 4 - 4, 32, 160)


def build_one(level, kappa, spread, packed, kappa_one, faces):
    for block in range(BLOCKS):
        spread[block * 32 : block * 32 + WY] = kappa[8 + block * WY : 8 + (block + 1) * WY]
        spread[block * 32 + WY : block * 32 + 32] = jnp.ones((32 - WY, 128), jnp.float32)
    packed[...] = 0.5 * spread[pl.ds(0, BLOCKS * 16, stride=2), :]
    level.close(kappa_one, 1.0)
    for block in range(BLOCKS):
        value = packed[block * 16 : block * 16 + 16]
        kappa_one[16 + block * 32 : 32 + block * 32] = value
        kappa_one[32 + block * 32 : 48 + block * 32] = value
    level.build(kappa_one, faces)


def to_chunk(rows):
    group = iota(8, 1) >> 5
    out = rows[0:8]
    for z in range(1, 4):
        out = jnp.where(group == z, rows[8 * z : 8 * z + 8], out)
    return out


def down_body(first, copies, *refs):
    index, refs = refs[0], refs[1:]
    if first:
        sources, refs = refs[:3], refs[3:]
    else:
        fields, (source, coefs, z_faces, faces), refs = refs[:3], refs[3:7], refs[7:]
    chunk, edge, kept, source_one, kept_one = refs[:5]
    refs = refs[5:]
    if first:
        (source, coefs, z_faces, faces), refs = refs[:4], refs[4:]
    va, vb, rs, oa, tmp = refs[:5]
    _, even = parities(index)
    y_device = index[1]
    level = level_one(y_device)
    if first:
        kappa, spread, packed, kappa_one = refs[5:]
        build_fine(sources, even, y_device, kappa, coefs, z_faces)
        build_one(level, kappa, spread, packed, kappa_one, faces)
    zero = jnp.zeros((WY, 128), jnp.float32)
    for ref in (va, vb):
        ref[0:WY] = zero
        ref[(WZ + 1) * WY : (WZ + 2) * WY] = zero
    if first:
        for z in range(WZ):
            kind = (0, 1, 1, 2)[z % 4]
            inside = 0 <= z + HALO - 12 < 16 + 2 * HALO
            value = window(sources, z + HALO - 12, even) if inside else zero
            source[z * WY : (z + 1) * WY] = value
            va[(z + 1) * WY : (z + 2) * WY] = coefs[z // 4, 5 + kind] * value
    else:
        for z in range(1, WZ - 1):
            vb[(z + 1) * WY : (z + 2) * WY] = window(fields, z - 1, even)
        for z in range(2, WZ - 2):
            here, total, weight, _ = fine_plane(vb, source, coefs, z_faces, z)
            va[(z + 1) * WY : (z + 2) * WY] = 0.2 * here + weight * total
    for z in range(3, WZ - 3):
        here, total, weight, _ = fine_plane(va, source, coefs, z_faces, z)
        value = 0.2 * here + weight * total
        vb[(z + 1) * WY : (z + 2) * WY] = value
        if 10 <= z < 30:
            kept[(z - 10) * WY : (z - 9) * WY] = value
    for plane in range(20):
        if 2 <= plane < 18:
            total_defect = 0.0
            for z in (2 * plane, 2 * plane + 1):
                here, total, _, diagonal = fine_plane(vb, source, coefs, z_faces, z)
                total_defect = total_defect + (total - diagonal * here)
            rs[plane * 32 : plane * 32 + WY] = total_defect
            rs[plane * 32 + WY : plane * 32 + 32] = jnp.zeros((32 - WY, 128), jnp.float32)
        else:
            rs[plane * 32 : plane * 32 + 32] = jnp.zeros((32, 128), jnp.float32)
    source_one[...] = coarsen(rs[pl.ds(0, 320, stride=2), :] + rs[pl.ds(1, 320, stride=2), :], 1)
    for ref in (oa, kept_one):
        level.close(ref, 0.0)
    level.start(oa, source_one, faces)
    level.relax(oa, kept_one, source_one, faces)
    level.defect(kept_one, source_one, faces, tmp, 6 * 16, 8 * 16)
    for z in range(4):
        tmp[z * 16 : z * 16 + 16] = tmp[z * 32 : z * 32 + 16] + tmp[z * 32 + 16 : z * 32 + 32]
    halves = tmp[pl.ds(0, 32, stride=2), :] + tmp[pl.ds(1, 32, stride=2), :]
    mean_two = lane_map(lambda r, c: matrix(((r & 1) == 0) & (r >> 2 == (c & 31)), 0.125))
    values = [to_chunk(dot(halves, mean_two))[2:4]]
    if first:
        pick_two = lane_map(lambda r, c: matrix(r == 4 * (c & 31), 0.5))
        values.append(to_chunk(dot(packed[pl.ds(48, 32, stride=2), :], pick_two))[2:4])
    repeats = 4 // len(values)
    tile = jnp.concatenate(values * repeats, axis=0)
    for at in range(0, copies // repeats):
        chunk[at * 8 : at * 8 + 8] = tile
    for plane in range(3, 17):
        edge[plane * 4 - 12 : plane * 4 - 8] = kept_one[16 + plane * 16 + 4 : 16 + plane * 16 + 8]


def coarse_levels():
    return (
        Level(SPAN, 16, 4, 1, 32, 16, 0, 16, 160),
        Level(SPAN, 8, 2, 2, 32, 8, 0, 8, 160),
        Level(SPAN, 4, 1, 4, 32, 8, 0, 4, 128),
    )


def coarse_body(first, z_devices, *refs):
    two, three, four = coarse_levels()
    index, same, mate = refs[:3]
    refs = refs[3:]
    if first:
        near, f2, f3, f4 = refs[:4]
    else:
        f2, f3, f4, near = refs[:4]
    a2, b2, g2, r2, a3, b3, g3, r3, a4, b4, g4, cut_same, cut_mate = refs[4:17]
    z_device = index[0]
    even = index[1] % 2 == 0
    per = 4 if first else 2
    rows = 4 * per
    for number in range(SPAN):
        at = lax.rem(z_device + (number - NEAR + 4 * z_devices), z_devices) * rows
        at = pl.multiple_of(at, 8)
        cut_same[number * rows : (number + 1) * rows] = same[pl.ds(at, rows), :]
        cut_mate[number * rows : (number + 1) * rows] = mate[pl.ds(at, rows), :]

    def interleave(target, start, part):
        for y in range(2):
            take = pl.ds(part + y, 4 * SPAN, stride=per)
            one, two_ = cut_same[take, :], cut_mate[take, :]
            target[pl.ds(start + y, 4 * SPAN, stride=4), :] = jnp.where(even, one, two_)
            target[pl.ds(start + 2 + y, 4 * SPAN, stride=4), :] = jnp.where(even, two_, one)

    interleave(g2, 0, 0)
    if first:
        k2, k3, k4 = refs[17:]
        interleave(k2, two.pad, 2)
        two.close(k2, 1.0)
        two.build(k2, f2)
        r2[...] = k2[two.pad : two.pad + two.rows]
        k3[three.pad : three.pad + three.rows] = 0.5 * coarsen(two.pairs(r2), 1, 4)
        three.close(k3, 1.0)
        three.build(k3, f3)
        r3[...] = k3[three.pad : three.pad + three.rows]
        k4[four.pad : four.pad + four.rows] = 0.5 * coarsen(three.pairs(r3), 2, 2)
        four.close(k4, 1.0)
        four.build(k4, f4)
    for level, fields in ((two, (a2, b2)), (three, (a3, b3)), (four, (a4, b4))):
        for field in fields:
            level.close(field, 0.0)

    two.start(a2, g2, f2)
    two.relax(a2, b2, g2, f2)
    two.defect(b2, g2, f2, r2)
    g3[...] = coarsen(two.pairs(r2), 1, 4)
    three.start(a3, g3, f3)
    three.relax(a3, b3, g3, f3)
    three.defect(b3, g3, f3, r3)
    g4[...] = coarsen(three.pairs(r3), 2, 2)
    four.start(a4, g4, f4)
    for _ in range(2):
        four.relax(a4, b4, g4, f4)
        four.relax(b4, a4, g4, f4)
    four.relax(a4, b4, g4, f4)

    def correct(level, field, start, count, value, tmp):
        tmp[pl.ds(0, count // 2, stride=2), :] = value
        tmp[pl.ds(1, count // 2, stride=2), :] = value
        inner = slice(level.pad + start, level.pad + start + count)
        field[inner] = field[inner] + tmp[0:count]

    low = NEAR - 3
    correct(three, b3, 8 * low, 48, b4[four.pad + 4 * low : four.pad + 4 * low + 24], r3)
    three.relax(b3, a3, g3, f3, 8 * low, 48)
    low = NEAR - 1
    three.relax(a3, b3, g3, f3, 8 * low, 24)
    correct(two, b2, 16 * low, 48, b3[three.pad + 8 * low : three.pad + 8 * low + 24], r2)
    two.relax(b2, a2, g2, f2, 16 * low, 48)
    two.relax(a2, b2, g2, f2, 16 * low, 48)
    near[...] = b2[two.pad + 16 * low : two.pad + 16 * low + 48]


def up_body(last, *refs):
    index, source, coefs, z_faces, faces, near, edge_mate, edge_other, kept, source_one, kept_one, out = refs[:12]
    refs = refs[12:]
    if last:
        out_hbm, (out, sems), refs = out, refs[-2:], refs[:-2]
        halves = (slice(0, 8), slice(8, 16))
        copies = [
            pltpu.make_async_copy(out.at[half], out_hbm.at[half], sems.at[i]) for i, half in enumerate(halves)
        ]
    else:
        (mate, other), refs = refs[:2], refs[2:]
    va, vb, spread, oa, ob = refs
    even_z, even = parities(index)
    y_device = index[1]
    level = level_one(y_device)
    rows = matrix(iota(16, 1, 16) == y_device * 2 - 2 + (iota(16, 0, 16) >> 1), 1.0)
    spread_y = jnp.concatenate([dot(rows, near[16 * part : 16 * part + 16]) for part in range(3)], axis=0)
    by_z = [
        dot(spread_y, lane_map(lambda r, c, z=z: matrix(r == z * 32 + (c >> 2), 1.0))) for z in range(4)
    ]
    for plane in range(3, 17):
        part, z = divmod(plane // 2 + 1, 4)
        at = 16 + plane * 16
        one, two = edge_mate[plane * 4 - 12 : plane * 4 - 8], edge_other[plane * 4 - 12 : plane * 4 - 8]
        field = jnp.concatenate(
            [jnp.where(even, two, one), kept_one[at + 4 : at + 8], jnp.where(even, one, two),
             jnp.zeros((4, 128), jnp.float32)], axis=0
        )
        oa[at : at + 16] = field + by_z[z][16 * part : 16 * part + 16]
    level.relax(oa, ob, source_one, faces, 4 * 16, 12 * 16)
    level.relax(ob, oa, source_one, faces, 5 * 16, 10 * 16)
    value = oa[16 + 80 : 16 + 240]
    spread[pl.ds(0, 160, stride=2), :] = value
    spread[pl.ds(1, 160, stride=2), :] = value
    for z in range(10, 30):
        at = ((z - 10) // 2) * 32
        va[(z + 1) * WY : (z + 2) * WY] = kept[(z - 10) * WY : (z - 9) * WY] + spread[at : at + WY]
    for z in range(11, 29):
        here, total, weight, _ = fine_plane(va, source, coefs, z_faces, z)
        vb[(z + 1) * WY : (z + 2) * WY] = 0.2 * here + weight * total
    for z in range(12, 28):
        here, total, weight, _ = fine_plane(vb, source, coefs, z_faces, z, 8, 8)
        out[z - 12] = 0.2 * here + weight * total
        if last and z in (19, 27):
            copies[z // 27].start()
    if last:
        for copy in copies:
            copy.wait()
    else:
        top = 16 - FIELD_HALO
        mate[...] = out[pl.ds(jnp.where(even_z, top, 0), FIELD_HALO)]
        other[...] = out[pl.ds(jnp.where(even_z, 0, top), FIELD_HALO)]


def floats(*shape):
    return jax.ShapeDtypeStruct(shape, jnp.float32)


def call(body, outs, scratch, args, inputs=pltpu.VMEM, outputs=pltpu.VMEM):
    return pl.pallas_call(
        body,
        out_shape=outs,
        in_specs=[pl.BlockSpec(memory_space=pltpu.SMEM)] + [pl.BlockSpec(memory_space=inputs)] * (len(args) - 1),
        out_specs=[pl.BlockSpec(memory_space=outputs)] * len(outs),
        scratch_shapes=[pltpu.VMEM(s, jnp.float32) if isinstance(s, tuple) else s for s in scratch],
        compiler_params=pltpu.CompilerParams(vmem_limit_bytes=VMEM_BYTES),
    )(*args)


FIELD = ((WZ + 2) * WY, 128)
SHARED = [(WZ * WY, 128), (BLOCKS, 11, WY, 128), (BLOCKS + 1, WY, 128), (6, 352, 128)]
Z_AXIS = ("gz",)
Y_AXIS = ("gx", "core")


def down(index, arrays, shared):
    first = shared is None
    copies = lax.axis_size("gz") * lax.axis_size("gx")
    outs = [
        floats(copies * (4 if first else 2), 128),
        floats(56, 128),
        floats(20 * WY, 128),
        floats(320, 128),
        floats(352, 128),
    ]
    scratch = [FIELD, FIELD, (640, 128), (352, 128), (128, 128)]
    if first:
        outs += [floats(*shape) for shape in SHARED]
        scratch += [(16 + BLOCKS * WY, 128), (320, 128), (160, 128), (352, 128)]
        args = [index, *arrays]
    else:
        args = [index, *arrays, *shared]
    result = call(lambda *refs: down_body(first, copies, *refs), outs, scratch, args)
    return result[0], result[1], result[2:5], result[5:] if first else shared


def coarse(index, gathered, faces):
    first = faces is None
    z_devices = lax.axis_size("gz")
    levels = coarse_levels()
    outs, scratch = [floats(48, 128)], []
    if first:
        outs += [floats(6, *level.shape()) for level in levels]
    for level in levels:
        scratch += [level.shape(), level.shape(), (level.rows, 128), (level.rows, 128)]
    cut = (SPAN * (16 if first else 8), 128)
    scratch = scratch[:11] + [cut, cut]
    if first:
        scratch += [level.shape() for level in levels]
    args = [index, *gathered] + ([] if first else list(faces))
    near, *new = call(lambda *refs: coarse_body(first, z_devices, *refs), outs, scratch, args)
    return near, new if first else faces


def up(index, shared, near, edges, kept, last):
    outs = [floats(16, 8, 128)] + ([] if last else [floats(FIELD_HALO, 8, 128)] * 2)
    scratch = [FIELD, FIELD, (320, 128), (352, 128), (352, 128)]
    if last:
        scratch += [(16, 8, 128), pltpu.SemaphoreType.DMA((2,))]
    args = [index, *shared, near, *edges, *kept]
    return call(
        lambda *refs: up_body(last, *refs), outs, scratch, args, outputs=pltpu.HBM if last else pltpu.VMEM
    )


def mate_of(i):
    return i + 1 if i % 2 == 0 else i - 1


def other_of(i):
    return i - 1 if i % 2 == 0 else i + 1


def swap(array, axis, partner):
    count = 1
    for name in axis:
        count *= lax.axis_size(name)
    return lax.ppermute(array, axis, [(i, partner(i) % count) for i in range(count)])


def swaps(mate, other, axis):
    far = far_in_y(other) if axis == Y_AXIS else swap(other, axis, other_of)
    return swap(mate, axis, mate_of), far


def far_in_y(array):
    y_devices = lax.axis_size("gx") * lax.axis_size("core")
    pairs = []
    for z in range(lax.axis_size("gz")):
        for y in range(y_devices):
            at = other_of(y)
            target = z * y_devices + at if 0 <= at < y_devices else mate_of(z) * y_devices + y
            pairs.append((z * y_devices + y, target))
    return lax.ppermute(array, ("gz", "gx", "core"), pairs)


def to_all(copies):
    peers = lax.axis_size("gz") * lax.axis_size("gx")
    copies = copies.reshape(peers, copies.shape[0] // peers, 128)
    out = lax.all_to_all(copies, ("gz", "gx"), 0, 0)
    out = out.reshape(out.shape[0] * out.shape[1], 128)
    return out, swap(out, Y_AXIS, mate_of)


def stack(index, parts, own, halo):
    even = index[0] % 2 == 0
    mate, other = parts
    before, after = jnp.where(even, other, mate), jnp.where(even, mate, other)
    pieces = [before[:halo], own[0], after[:halo]]
    if len(own) > 1:
        pieces += [before[halo:], own[1], after[halo:]]
    return jnp.concatenate(pieces, axis=0)


def cycle(index, arrays, shared, coarse_faces, last):
    copies, edge, kept, shared = down(index, arrays, shared)
    edges = swaps(edge, edge, Y_AXIS)
    gathered = to_all(copies)
    near, coarse_faces = coarse(index, gathered, coarse_faces)
    return up(index, shared, near, edges, kept, last), shared, coarse_faces


def per_device(concentration, phases, grains, grain_class, diffusivity):
    y_device = lax.axis_index("gx") * lax.axis_size("core") + lax.axis_index("core")
    index = jnp.stack([lax.axis_index("gz"), y_device]).astype(jnp.int32)
    plane = (4,) + phases.shape[1:]
    blocks = (4, 4) + phases.shape[1:]
    part = floats(HALO + 1, 8, 128)
    kappa, block, *parts = call(
        kappa_body,
        [floats(1, 8, 128), floats(*phases.shape), part, part],
        [
            pltpu.SMEM(grain_class.shape, jnp.int32),
            pltpu.SMEM(diffusivity.shape, jnp.float32),
            pltpu.VMEM(plane, jnp.int32),
            pltpu.VMEM(plane, jnp.int32),
            pltpu.SemaphoreType.DMA((7,)),
        ],
        [index] + [
            pltpu.with_memory_space_constraint(array, pltpu.HBM)
            for array in (grain_class, diffusivity, phases.reshape(blocks), grains.reshape(blocks), concentration)
        ],
        pltpu.HBM,
    )
    own = stack(index, swaps(*parts, Z_AXIS), (block, kappa), HALO)
    mate, other = swaps(own, own, Y_AXIS)
    (field, *parts), shared, faces = cycle(index, (mate, own, other), None, None, False)

    own = stack(index, swaps(*parts, Z_AXIS), (field,), FIELD_HALO)
    mate, other = swaps(own, own, Y_AXIS)
    return cycle(index, (mate, own, other), shared, faces, True)[0][0]


def solution(mesh):
    z_devices, y_devices = mesh.shape["gz"], mesh.shape["gy"]
    cores = jax.sharding.Mesh(mesh.devices.reshape(z_devices, y_devices // 2, 2), ("gz", "gx", "core"))
    split = P("gz", ("gx", "core"), None)
    return jax.shard_map(
        per_device, mesh=cores, in_specs=(split, split, split, P(), P()), out_specs=split, check_vma=False
    )
```
